256 devices in a mesh: src: 4 (over z_hi, core), tile: 64 (over x, z_lo, y).
Axes of the slice: x: 4, y: 4, z: 8 (z_hi: 2, z_lo: 4; z = z_hi * 4 + z_lo), core: 2. Of those that a mesh axis runs over, the one named last changes fastest.
Arguments:
- mask_logits: float32 [32768, 512], P('tile'), may hold values from -10 to 10
- target: int32 [32768, 512], P('tile'), may hold values 0 or 1
- weights: float32 [64], P('src'), may hold values from 0.0078125 to 0.03125
- shifts: int32 [64, 2], P('src'), may hold values from -11 to 11
Outputs:
- mask_grad: float32 [32768, 512], P('tile')
- weight_grad: float32 [64], P('src')
- loss: float32 [], replicated
The draws below stay inside these ranges and needn't reach their ends.
All inputs are finite; a program needn't handle non-finite values. No bound on the sum of `target` on one device may be relied on, other than what follows from the above.
Results may differ from the reference program's by a relative error of at most 0.0008.
The reference program's roundings to bfloat16 on the way count: a program that leaves them out, or rounds other values in their place, can miss the bound.
Values may be sent and summed in bfloat16 or wider, within the bound.
No kernel may reach another device: no remote copies, remote signals or barrier semaphores. Data moves between devices by JAX's collectives and lax.ppermute only.
A program may use at most 64 MiB of HBM per device.

```python
import math
import jax
import jax.numpy as jnp
from jax import lax

COLS = 512
FREQS = 64
RADIUS = 20
MARGIN = 64
TILE_ROWS = 512
SOURCES = 64
TILES = 64
FRAME = 640
SHIFT = 11
PIXELS = 16777216
N_TILE = 64


def draw_mask_logits(key, part):
    band_rows = TILES * TILE_ROWS
    position = jnp.arange(band_rows, dtype=jnp.float32)[:, None] / band_rows
    noise = jnp.clip(2.0 * jax.random.normal(key, (band_rows, COLS), jnp.float32), -8.0, 8.0)
    trend = -1.5 + 3.0 * position
    return noise + trend


def plant(entries, rng, least, high):
    extent = entries.shape
    index_at = [jax.random.randint(jax.random.fold_in(rng, axis), (), 0, extent[axis]) for axis in range(len(extent))]
    entries = entries.at[tuple(index_at)].set(least)
    longest = extent.index(max(extent))
    index_at[longest] = (index_at[longest] + 1) % extent[longest]
    return entries.at[tuple(index_at)].set(high)


def levels(own_key, dims, cuts, low, largest):
    def one(axis_at, shards_of):
        heights = jax.random.uniform(jax.random.fold_in(jax.random.fold_in(own_key, 6), axis_at), (shards_of,), jnp.float32, low / len(cuts), largest / len(cuts))
        return jnp.repeat(jnp.exp(heights), dims[axis_at] // shards_of).reshape((-1,) + (1,) * (len(dims) - axis_at - 1))

    loudness = one(*cuts[0])
    for cut in cuts[1:]:
        loudness = loudness * one(*cut)
    return loudness


def setup_inputs(seed: int = 0) -> dict:
    key_of = jax.random.split(jax.random.key(seed), 5)
    return {
        "mask_logits": draw_mask_logits(jax.random.fold_in(key_of[4], 71), 0),
        "target": plant((jax.random.randint(key_of[1], (TILES * TILE_ROWS, COLS), 0, 2) < 1).astype(jnp.int32), jax.random.fold_in(key_of[1], 1), 0, 1),
        "weights": jnp.clip(jnp.exp(math.log(0.03125) - 1.3862944 * jax.random.uniform(key_of[2], (SOURCES,), jnp.float32) ** levels(key_of[2], (SOURCES,), ((0, 4),), -0.2, 0.2)), 0.0078125, 0.03125),
        "shifts": plant(jax.random.randint(key_of[3], (SOURCES, 2), 0 - SHIFT, SHIFT + 1), jax.random.fold_in(key_of[3], 1), 0 - SHIFT, SHIFT).astype(jnp.int32),
    }


STEEPNESS = 12.0
THRESHOLD = 0.2
HIGHEST = lax.Precision.HIGHEST


def angles(length_used, offset, period):
    position = jnp.arange(length_used, dtype=jnp.int32)[:, None] + offset
    frequency = jnp.arange(FREQS, dtype=jnp.int32)[None, :] - FREQS // 2
    cycles = jnp.mod(position * frequency, period).astype(jnp.float32)
    angle_value = cycles * jnp.float32(2.0 * 3.141592653589793 / period)
    return jnp.cos(angle_value), jnp.sin(angle_value)


def make_tables(tile_rows, frame_rows, col_count):
    column_cosine, column_sine = angles(col_count, 0, col_count)
    column_forward = jnp.concatenate([column_cosine, -column_sine], 1).astype(jnp.bfloat16)
    frame_cosine, frame_sine = angles(frame_rows, 0, frame_rows)
    row_forward = jnp.concatenate([frame_cosine.T, -frame_sine.T], 0).astype(jnp.bfloat16)
    owned_cosine, owned_sine = angles(tile_rows, MARGIN, frame_rows)
    row_inverse = (jnp.concatenate([owned_cosine, owned_sine], 1) / frame_rows).astype(jnp.bfloat16)
    cosine_scaled = column_cosine.T / col_count
    sine_scaled = column_sine.T / col_count
    upper_block = jnp.concatenate([cosine_scaled, sine_scaled], 1)
    lower_block = jnp.concatenate([-sine_scaled, cosine_scaled], 1)
    column_inverse = jnp.concatenate([upper_block, lower_block], 0).astype(jnp.bfloat16)
    return column_forward, row_forward, row_inverse, column_inverse


def pupil_masks(shifts):
    frequency = jnp.arange(FREQS, dtype=jnp.int32) - FREQS // 2
    offset_across = frequency[None, :, None] - shifts[:, 0][:, None, None]
    offset_along = frequency[None, None, :] - shifts[:, 1][:, None, None]
    inside = offset_across * offset_across + offset_along * offset_along <= RADIUS * RADIUS
    return inside.astype(jnp.float32)


def spectrum(framed, column_forward, row_forward):
    column_part = jnp.dot(framed, column_forward, preferred_element_type=jnp.float32).astype(jnp.bfloat16)
    product = jnp.dot(row_forward, column_part, preferred_element_type=jnp.float32)
    spectrum_real = (product[:FREQS, :FREQS] - product[FREQS:, FREQS:]).astype(jnp.bfloat16)
    spectrum_imag = (product[:FREQS, FREQS:] + product[FREQS:, :FREQS]).astype(jnp.bfloat16)
    return spectrum_real, spectrum_imag


def pupil_blocks(pupils, spectrum_real, spectrum_imag):
    pass_real = pupils * spectrum_real.astype(jnp.float32)
    pass_imag = pupils * spectrum_imag.astype(jnp.float32)
    upper_block = jnp.concatenate([pass_real, pass_imag], 2)
    lower_block = jnp.concatenate([-pass_imag, pass_real], 2)
    return jnp.concatenate([upper_block, lower_block], 1).astype(jnp.bfloat16)


def apply_resist(intensity, target_rows):
    printed = jax.nn.sigmoid(STEEPNESS * (intensity - THRESHOLD))
    error_value = printed - target_rows.astype(jnp.float32)
    cotangent = 2.0 * STEEPNESS * error_value * printed * (1.0 - printed)
    return cotangent, jnp.sum(error_value * error_value)


def frame_gradient(grad_real, grad_imag, column_forward, row_forward):
    upper_block = jnp.concatenate([grad_real, grad_imag], 1)
    lower_block = jnp.concatenate([grad_imag, -grad_real], 1)
    product_grad = jnp.concatenate([upper_block, lower_block], 0)
    column_grad = jnp.dot(row_forward.astype(jnp.float32).T, product_grad, precision=HIGHEST)
    return jnp.dot(column_grad, column_forward.astype(jnp.float32).T, precision=HIGHEST)


def tile_pass(framed, target_rows, weights, pupils, tables):
    column_forward, row_forward, row_inverse, column_inverse = tables
    spectrum_real, spectrum_imag = spectrum(framed, column_forward, row_forward)
    blocks = pupil_blocks(pupils, spectrum_real, spectrum_imag)
    row_field = jnp.einsum('pk,skj->spj', row_inverse.astype(jnp.float32), blocks.astype(jnp.float32), precision=HIGHEST).astype(jnp.bfloat16)
    source_count, tile_rows, doubled_freqs = row_field.shape
    fields = jnp.dot(row_field.reshape(source_count * tile_rows, doubled_freqs), column_inverse, preferred_element_type=jnp.float32)
    fields = fields.reshape(source_count, tile_rows, -1)
    col_count = fields.shape[2] // 2
    powers = fields[:, :, :col_count] * fields[:, :, :col_count] + fields[:, :, col_count:] * fields[:, :, col_count:]
    intensity = jnp.sum(weights[:, None, None] * powers, 0)
    cotangent, error_sum = apply_resist(intensity, target_rows)
    source_terms = jnp.sum(cotangent[None] * powers, axis=(1, 2))
    doubled = jnp.concatenate([cotangent, cotangent], 1)
    scaling = (2.0 * weights)[:, None, None] * doubled[None]
    field_grad = (scaling * fields).astype(jnp.bfloat16)
    row_grad = jnp.dot(field_grad.reshape(source_count * tile_rows, -1), column_inverse.T, preferred_element_type=jnp.float32)
    row_grad = row_grad.astype(jnp.bfloat16).reshape(source_count, tile_rows, -1)
    block_grad = jnp.einsum('pk,spj->skj', row_inverse.astype(jnp.float32), row_grad.astype(jnp.float32), precision=HIGHEST)
    grad_real = jnp.sum(pupils * (block_grad[:, :FREQS, :FREQS] + block_grad[:, FREQS:, FREQS:]), 0)
    grad_imag = jnp.sum(pupils * (block_grad[:, :FREQS, FREQS:] - block_grad[:, FREQS:, :FREQS]), 0)
    return frame_gradient(grad_real, grad_imag, column_forward, row_forward), source_terms, error_sum


def reference(mask_logits, target, weights, shifts):
    opening = jax.nn.sigmoid(mask_logits)
    padded = jnp.pad(opening.astype(jnp.bfloat16), ((MARGIN, MARGIN), (0, 0)))
    tables = make_tables(TILE_ROWS, FRAME, COLS)
    pupils = pupil_masks(shifts)

    def one_tile(tile_index):
        row_start = (tile_index * TILE_ROWS).astype(jnp.int32)
        framed = lax.dynamic_slice_in_dim(padded, row_start, FRAME, 0)
        target_rows = lax.dynamic_slice_in_dim(target, row_start, TILE_ROWS, 0)
        return tile_pass(framed, target_rows, weights, pupils, tables)

    frame_grads, source_terms, error_sums = lax.map(one_tile, jnp.arange(N_TILE, dtype=jnp.int32))
    owned_grads = frame_grads[:, MARGIN:MARGIN + TILE_ROWS]
    owned_grads = owned_grads.at[:-1, TILE_ROWS - MARGIN:].add(frame_grads[1:, :MARGIN])
    owned_grads = owned_grads.at[1:, :MARGIN].add(frame_grads[:-1, MARGIN + TILE_ROWS:])
    mask_grad = owned_grads.reshape(-1, COLS) * opening * (1.0 - opening)
    weight_grad = jnp.sum(source_terms, 0) / PIXELS
    loss = jnp.sum(error_sums) / PIXELS
    return mask_grad, weight_grad, loss
```

```python
import numpy as np
import jax
import jax.numpy as jnp
from jax import lax
from jax.experimental import pallas as pl
from jax.experimental.pallas import tpu as pltpu
from jax.sharding import PartitionSpec as P

FREQS = 64
RADIUS = 20
MARGIN = 64
COLS = 512
TILE_ROWS = 512
FRAME = 640
SOURCES = 64
GROUPS = 4
PER_GROUP = SOURCES // GROUPS
ROWS = TILE_ROWS // GROUPS
STEEPNESS = 12.0
THRESHOLD = 0.2
STEP = 4
F32 = jnp.float32
BF16 = jnp.bfloat16


def angles(length_used, offset, period):
    position = np.arange(length_used, dtype=np.int32)[:, None] + offset
    frequency = np.arange(FREQS, dtype=np.int32)[None, :] - FREQS // 2
    cycles = np.mod(position * frequency, period).astype(np.float32)
    angle_value = (cycles * np.float32(2.0 * 3.141592653589793 / period)).astype(np.float64)
    return np.cos(angle_value).astype(np.float32), np.sin(angle_value).astype(np.float32)


def make_tables():
    column_cosine, column_sine = angles(COLS, 0, COLS)
    column_forward = np.concatenate([column_cosine, -column_sine], 1)
    frame_cosine, frame_sine = angles(FRAME, 0, FRAME)
    row_forward = np.concatenate([frame_cosine.T, -frame_sine.T], 0)
    owned_cosine, owned_sine = angles(TILE_ROWS, MARGIN, FRAME)
    row_inverse = np.concatenate([owned_cosine, owned_sine], 1) / np.float32(FRAME)
    cosine_scaled = column_cosine.T / np.float32(COLS)
    sine_scaled = column_sine.T / np.float32(COLS)
    upper_block = np.concatenate([cosine_scaled, sine_scaled], 1)
    lower_block = np.concatenate([-sine_scaled, cosine_scaled], 1)
    column_inverse = np.concatenate([upper_block, lower_block], 0)
    chunked = column_inverse.reshape(2 * FREQS, 2, COLS // 128, 128).transpose(0, 2, 1, 3)
    chunked = chunked.reshape(2 * FREQS, 2 * COLS)
    rounded = lambda a: np.ascontiguousarray(a).astype(BF16)
    return [rounded(a) for a in (column_forward, row_forward, row_inverse, chunked)]


COLUMN_FORWARD, ROW_FORWARD, ROW_INVERSE, COLUMN_INVERSE = make_tables()


def dot(a, b):
    return jnp.dot(a, b, preferred_element_type=F32)


def halves_sign(rows, left, right):
    lane = lax.broadcasted_iota(jnp.int32, (rows, 128), 1)
    return jnp.where(lane < FREQS, F32(left), F32(right))


def column_kernel(logits_ref, table_ref, out_ref, first_ref, last_ref):
    opening = jax.nn.sigmoid(logits_ref[...]).astype(BF16)
    out = dot(opening, table_ref[...]).astype(BF16)
    out_ref[...] = out
    first_ref[...] = out[:MARGIN]
    last_ref[...] = out[TILE_ROWS - MARGIN:]


def column_spectrum(mask_logits):
    shapes = [(TILE_ROWS, 128), (MARGIN, 128), (MARGIN, 128)]
    return pl.pallas_call(
        column_kernel,
        out_shape=[jax.ShapeDtypeStruct(s, BF16) for s in shapes],
        name="column_spectrum",
    )(mask_logits, jnp.asarray(COLUMN_FORWARD))


def pupil(scalars_ref, s):
    group, i = s // PER_GROUP, s % PER_GROUP
    across = scalars_ref[group, PER_GROUP + i]
    along = scalars_ref[group, 2 * PER_GROUP + i]
    row = lax.broadcasted_iota(jnp.int32, (FREQS, 128), 0) - FREQS // 2
    lane = jnp.bitwise_and(lax.broadcasted_iota(jnp.int32, (FREQS, 128), 1), FREQS - 1) - FREQS // 2
    row, lane = row.astype(F32) - across, lane.astype(F32) - along
    return row * row + lane * lane <= F32(RADIUS * RADIUS)


def image_kernel(group_ref, scalars_ref, own_ref, before_ref, after_ref, target_ref, row_forward_ref,
                 row_inverse_ref, row_inverse_t_ref, inverse_ref, inverse_t_ref, out_ref,
                 fields_ref, row_field_ref, intensity_ref, cotangent_ref, spectra_ref, terms_ref, grad_ref):
    frame = jnp.concatenate([before_ref[...], own_ref[...], after_ref[...]], 0)
    product = dot(row_forward_ref[...], frame)
    swapped = pltpu.roll(product[FREQS:], FREQS, 1)
    spectrum = (product[:FREQS] + halves_sign(FREQS, -1.0, 1.0) * swapped).astype(BF16).astype(F32)
    spectra_ref[:FREQS] = spectrum
    spectra_ref[FREQS:] = pltpu.roll(spectrum, FREQS, 1) * halves_sign(FREQS, -1.0, 1.0)
    intensity_ref[...] = jnp.zeros_like(intensity_ref)
    spectra = spectra_ref[...]

    @pl.loop(0, SOURCES // STEP)
    def _(step):
        blocks = []
        for j in range(STEP):
            inside = pupil(scalars_ref, step * STEP + j)
            inside = jnp.concatenate([inside, inside], 0)
            blocks.append(jnp.where(inside, spectra, F32(0)).astype(BF16))
        row_field = dot(row_inverse_ref[...], jnp.concatenate(blocks, 1)).astype(BF16)
        for j in range(STEP):
            start = pl.multiple_of((step * STEP + j) * ROWS, ROWS)
            row_field_ref[pl.ds(start, ROWS), :] = row_field[:, 128 * j:128 * (j + 1)]

    def weight(s):
        return scalars_ref[s // PER_GROUP, s % PER_GROUP]

    @pl.loop(0, SOURCES // STEP)
    def _(step):
        start = pl.multiple_of(step * (STEP * ROWS), STEP * ROWS)
        row_field = row_field_ref[pl.ds(start, STEP * ROWS), :]
        for n in range(4):
            fields = dot(row_field, inverse_ref[:, 256 * n:256 * (n + 1)])
            fields_ref[pl.ds(start, STEP * ROWS), 256 * n:256 * (n + 1)] = fields
            power = fields[:, :128] * fields[:, :128] + fields[:, 128:] * fields[:, 128:]
            total = weight(step * STEP) * power[:ROWS]
            for j in range(1, STEP):
                total = total + weight(step * STEP + j) * power[j * ROWS:(j + 1) * ROWS]
            intensity_ref[:, 128 * n:128 * (n + 1)] += total

    printed = jax.nn.sigmoid(F32(STEEPNESS) * (intensity_ref[...] - F32(THRESHOLD)))
    error_value = printed - target_ref[...].astype(F32)
    cotangent_ref[...] = F32(2.0 * STEEPNESS) * error_value * printed * (F32(1.0) - printed)
    error_rows = jnp.sum(error_value * error_value, 0, keepdims=True)
    error_lanes = (error_rows[:, :128] + error_rows[:, 128:256]) + (error_rows[:, 256:384] + error_rows[:, 384:])
    error_sum = jnp.sum(error_lanes, 1, keepdims=True)
    grad_ref[...] = jnp.zeros_like(grad_ref)

    @pl.loop(0, SOURCES // STEP)
    def _(step):
        start = pl.multiple_of(step * (STEP * ROWS), STEP * ROWS)
        row_grad = None
        for n in range(4):
            cot = cotangent_ref[:, 128 * n:128 * (n + 1)]
            parts = []
            for j in range(STEP):
                scaling = (F32(2.0) * weight(step * STEP + j)) * cot
                at = pl.multiple_of(start + j * ROWS, ROWS)
                fields = fields_ref[pl.ds(at, ROWS), 256 * n:256 * (n + 1)]
                parts.append((jnp.concatenate([scaling, scaling], 1) * fields).astype(BF16))
            part = dot(jnp.concatenate(parts, 0), inverse_t_ref[256 * n:256 * (n + 1), :])
            row_grad = part if row_grad is None else row_grad + part
        row_field = row_field_ref[pl.ds(start, STEP * ROWS), :].astype(F32)
        terms = row_grad * row_field
        rounded = row_grad.astype(BF16)
        for j in range(STEP):
            terms_ref[pl.ds(step * STEP + j, 1), :] = jnp.sum(terms[j * ROWS:(j + 1) * ROWS], 0, keepdims=True)
        block_grad = dot(row_inverse_t_ref[...],
                         jnp.concatenate([rounded[j * ROWS:(j + 1) * ROWS] for j in range(STEP)], 1))
        total = jnp.zeros((2 * FREQS, 128), F32)
        for j in range(STEP):
            inside = pupil(scalars_ref, step * STEP + j)
            inside = jnp.concatenate([inside, inside], 0)
            total = total + jnp.where(inside, block_grad[:, 128 * j:128 * (j + 1)], F32(0))
        grad_ref[...] += total

    grads = grad_ref[...]
    out_ref[:FREQS] = grads[:FREQS] + halves_sign(FREQS, 1.0, -1.0) * pltpu.roll(grads[FREQS:], FREQS, 1)
    term = jnp.sum(terms_ref[...], 1, keepdims=True)
    row = lax.broadcasted_iota(jnp.int32, (SOURCES, 128), 0)
    lane = lax.broadcasted_iota(jnp.int32, (SOURCES, 128), 1)
    term_row = jnp.sum(jnp.where(row == lane, term, F32(0)), 0, keepdims=True)
    lane_row = lax.broadcasted_iota(jnp.int32, (1, 128), 1)
    out_ref[FREQS:] = jnp.broadcast_to(jnp.where(lane_row == SOURCES, error_sum, term_row), (8, 128))


def image(group, scalars, own, before, after, target):
    fixed = lambda i, g: (0, 0)
    whole = lambda shape: pl.BlockSpec(shape, fixed)
    return pl.pallas_call(
        image_kernel,
        grid_spec=pltpu.PrefetchScalarGridSpec(
            num_scalar_prefetch=1,
            grid=(1,),
            in_specs=[
                pl.BlockSpec(memory_space=pltpu.SMEM),
                whole((TILE_ROWS, 128)), whole((MARGIN, 128)), whole((MARGIN, 128)),
                pl.BlockSpec((ROWS, COLS), lambda i, g: (g[0], 0)),
                whole((128, FRAME)),
                pl.BlockSpec((ROWS, 128), lambda i, g: (g[0], 0)),
                pl.BlockSpec((128, ROWS), lambda i, g: (0, g[0])),
                whole((128, 2 * COLS)), whole((2 * COLS, 128)),
            ],
            out_specs=whole((FREQS + 8, 128)),
            scratch_shapes=[
                pltpu.VMEM((SOURCES * ROWS, 2 * COLS), F32),
                pltpu.VMEM((SOURCES * ROWS, 128), BF16),
                pltpu.VMEM((ROWS, COLS), F32),
                pltpu.VMEM((ROWS, COLS), F32),
                pltpu.VMEM((128, 128), F32),
                pltpu.VMEM((SOURCES, 128), F32),
                pltpu.VMEM((128, 128), F32),
            ],
        ),
        out_shape=jax.ShapeDtypeStruct((FREQS + 8, 128), F32),
        compiler_params=pltpu.CompilerParams(vmem_limit_bytes=58 * 1024 * 1024),
        name="image",
    )(group, scalars, own, before, after, target, jnp.asarray(ROW_FORWARD), jnp.asarray(ROW_INVERSE),
      jnp.asarray(np.ascontiguousarray(ROW_INVERSE.T)), jnp.asarray(COLUMN_INVERSE),
      jnp.asarray(np.ascontiguousarray(COLUMN_INVERSE.T)))


def split_dot(table, x):
    high = x.astype(BF16)
    low = (x - high.astype(F32)).astype(BF16)
    return dot(jnp.concatenate([table, table], 1), jnp.concatenate([high, low], 0))


def dot_split(x, table):
    high = x.astype(BF16)
    low = (x - high.astype(F32)).astype(BF16)
    return dot(jnp.concatenate([high, low], 1), jnp.concatenate([table, table], 0))


def product_gradient(spectrum_grad):
    lower = pltpu.roll(spectrum_grad, FREQS, 1) * halves_sign(FREQS, 1.0, -1.0)
    return jnp.concatenate([spectrum_grad, lower], 0)


def owned_kernel(grad_ref, logits_ref, row_ref, column_ref, out_ref):
    column_grad = split_dot(row_ref[...], product_gradient(grad_ref[...]))
    opening = jax.nn.sigmoid(logits_ref[...])
    out_ref[...] = dot_split(column_grad, column_ref[...]) * opening * (F32(1.0) - opening)


def owned_gradient(spectrum_grad, mask_logits):
    return pl.pallas_call(
        owned_kernel,
        out_shape=jax.ShapeDtypeStruct((TILE_ROWS, COLS), F32),
        name="owned_gradient",
    )(spectrum_grad, mask_logits,
      jnp.asarray(np.ascontiguousarray(ROW_FORWARD.T[MARGIN:MARGIN + TILE_ROWS])),
      jnp.asarray(np.ascontiguousarray(COLUMN_FORWARD.T)))


def margin_kernel(before_ref, after_ref, logits_ref, row_ref, column_ref, grad_ref, out_ref):
    first = pl.program_id(0) == 0
    spectrum_grad = jnp.where(first, before_ref[...], after_ref[...])
    column_grad = split_dot(row_ref[...], product_gradient(spectrum_grad))
    opening = jax.nn.sigmoid(logits_ref[...])
    added = dot_split(column_grad, column_ref[...]) * opening * (F32(1.0) - opening)
    out_ref[...] = grad_ref[...] + added


def margin_gradient(before, after, mask_logits, grad):
    edge = lambda i: (i * (TILE_ROWS // MARGIN - 1), 0)
    fixed = lambda i: (0, 0)
    rows = np.concatenate([ROW_FORWARD.T[MARGIN + TILE_ROWS:], ROW_FORWARD.T[:MARGIN]], 0)
    return pl.pallas_call(
        margin_kernel,
        grid=(2,),
        in_specs=[
            pl.BlockSpec((FREQS, 128), fixed), pl.BlockSpec((FREQS, 128), fixed),
            pl.BlockSpec((MARGIN, COLS), edge),
            pl.BlockSpec((MARGIN, 128), lambda i: (i, 0)),
            pl.BlockSpec((128, COLS), fixed),
            pl.BlockSpec((MARGIN, COLS), edge),
        ],
        out_specs=pl.BlockSpec((MARGIN, COLS), edge),
        out_shape=jax.ShapeDtypeStruct((TILE_ROWS, COLS), F32),
        input_output_aliases={5: 0},
        name="margin_gradient",
    )(before, after, mask_logits, jnp.asarray(np.ascontiguousarray(rows)),
      jnp.asarray(np.ascontiguousarray(COLUMN_FORWARD.T)), grad)


def from_tiles_beside(last, first):
    peers = lax.axis_size("tile")
    up = [(i, i + 1) for i in range(peers - 1)]
    down = [(j, i) for i, j in up]
    return lax.ppermute(last, "tile", up), lax.ppermute(first, "tile", down)


def from_groups(x):
    return [x] + [lax.ppermute(x, "src", [(i, i ^ d) for i in range(GROUPS)]) for d in range(1, GROUPS)]


def on_device(mask_logits, target, weights, shifts):
    group = lax.axis_index("src").astype(jnp.int32).reshape(1)
    own_scalars = jnp.concatenate([weights, shifts[:, 0].astype(F32), shifts[:, 1].astype(F32)])
    scalars = jnp.stack(from_groups(own_scalars))
    own, first, last = column_spectrum(mask_logits)
    before, after = from_tiles_beside(last, first)
    partial = image(group, scalars, own, before, after, target)
    parts = from_groups(partial)
    spectrum_grad = (parts[0][:FREQS] + parts[1][:FREQS]) + (parts[2][:FREQS] + parts[3][:FREQS])
    grad_before, grad_after = from_tiles_beside(spectrum_grad, spectrum_grad)
    grad = owned_gradient(spectrum_grad, mask_logits)
    mask_grad = margin_gradient(grad_before, grad_after, mask_logits, grad)
    rows = [p[FREQS] for p in parts]
    own_terms = sum(rows[d][d * PER_GROUP:(d + 1) * PER_GROUP] for d in range(GROUPS))
    error = (rows[0][SOURCES] + rows[1][SOURCES]) + (rows[2][SOURCES] + rows[3][SOURCES])
    sums = jnp.concatenate([own_terms, error[None]])
    peers = lax.axis_size("tile")
    everyone = lax.all_to_all(jnp.broadcast_to(sums[None], (peers, PER_GROUP + 1)), "tile", 0, 0, tiled=True)
    total = everyone.sum(axis=0)
    pixels = TILE_ROWS * COLS * peers
    return mask_grad, total[:PER_GROUP] / (2.0 * weights) / pixels, total[PER_GROUP] / pixels


def solution(mesh):
    placed = (P("tile", None), P("tile", None), P("src"), P("src", None))
    return jax.shard_map(
        on_device,
        mesh=mesh,
        in_specs=placed,
        out_specs=(P("tile", None), P("src"), P()),
        check_vma=False,
    )
```

```python
import functools

import numpy as np
import jax
import jax.numpy as jnp
from jax import lax
from jax.experimental import pallas as pl
from jax.experimental.pallas import tpu as pltpu
from jax.sharding import PartitionSpec as P

FREQS = 64
RADIUS = 20
MARGIN = 64
COLS = 512
TILE_ROWS = 512
FRAME = 640
SOURCES = 64
GROUPS = 4
PER_GROUP = SOURCES // GROUPS
ROWS = TILE_ROWS // GROUPS
MIB = 1024 * 1024
STEEPNESS = 12.0
THRESHOLD = 0.2
STEP = 16
F32 = jnp.float32
BF16 = jnp.bfloat16


def angles(length_used, offset, period):
    position = np.arange(length_used, dtype=np.int32)[:, None] + offset
    frequency = np.arange(FREQS, dtype=np.int32)[None, :] - FREQS // 2
    cycles = np.mod(position * frequency, period).astype(np.float32)
    angle_value = (cycles * np.float32(2.0 * 3.141592653589793 / period)).astype(np.float64)
    return np.cos(angle_value).astype(np.float32), np.sin(angle_value).astype(np.float32)


def make_tables():
    column_cosine, column_sine = angles(COLS, 0, COLS)
    column_forward = np.concatenate([column_cosine, -column_sine], 1)
    frame_cosine, frame_sine = angles(FRAME, 0, FRAME)
    row_forward = np.concatenate([frame_cosine.T, -frame_sine.T], 0)
    owned_cosine, owned_sine = angles(TILE_ROWS, MARGIN, FRAME)
    row_inverse = np.concatenate([owned_cosine, owned_sine], 1) / np.float32(FRAME)
    cosine_scaled = column_cosine.T / np.float32(COLS)
    sine_scaled = column_sine.T / np.float32(COLS)
    upper_block = np.concatenate([cosine_scaled, sine_scaled], 1)
    lower_block = np.concatenate([-sine_scaled, cosine_scaled], 1)
    column_inverse = np.concatenate([upper_block, lower_block], 0)
    chunked = column_inverse.reshape(2 * FREQS, 2, COLS // 128, 128).transpose(0, 2, 1, 3)
    chunked = chunked.reshape(2 * FREQS, 2 * COLS)
    rounded = lambda a: np.ascontiguousarray(a).astype(BF16)
    return [rounded(a) for a in (column_forward, row_forward, row_inverse, chunked)]


COLUMN_FORWARD, ROW_FORWARD, ROW_INVERSE, COLUMN_INVERSE = make_tables()


def dot(a, b):
    return jnp.dot(a, b, preferred_element_type=F32)


def halves_sign(rows, left, right):
    lane = lax.broadcasted_iota(jnp.int32, (rows, 128), 1)
    return jnp.where(lane < FREQS, F32(left), F32(right))


def edge_kernel(first_ref, last_ref, table_ref, weights_ref, shifts_ref, first_out, last_out, packed_ref):
    first_out[...] = dot(jax.nn.sigmoid(first_ref[...]).astype(BF16), table_ref[...]).astype(BF16)
    last_out[...] = dot(jax.nn.sigmoid(last_ref[...]).astype(BF16), table_ref[...]).astype(BF16)
    packed_ref[0:1] = weights_ref[...]
    packed_ref[1:3] = shifts_ref[...].astype(F32)


def edge_spectrum(mask_logits, weights, shifts):
    fixed = lambda i: (0, 0)
    return pl.pallas_call(
        edge_kernel,
        grid=(1,),
        in_specs=[
            pl.BlockSpec((MARGIN, COLS), fixed),
            pl.BlockSpec((MARGIN, COLS), lambda i: (TILE_ROWS // MARGIN - 1, 0)),
            pl.BlockSpec((COLS, 128), fixed),
            pl.BlockSpec((1, PER_GROUP), fixed),
            pl.BlockSpec((2, PER_GROUP), fixed),
        ],
        out_specs=[pl.BlockSpec((MARGIN, 128), fixed), pl.BlockSpec((MARGIN, 128), fixed),
                   pl.BlockSpec((3, PER_GROUP), fixed)],
        out_shape=[jax.ShapeDtypeStruct((MARGIN, 128), BF16), jax.ShapeDtypeStruct((MARGIN, 128), BF16),
                   jax.ShapeDtypeStruct((3, PER_GROUP), F32)],
        compiler_params=pltpu.CompilerParams(vmem_limit_bytes=4 * MIB),
        name="edge_spectrum",
    )(mask_logits, mask_logits, jnp.asarray(COLUMN_FORWARD), weights.reshape(1, PER_GROUP), shifts.T)


def column_kernel(logits_ref, table_ref, out_ref):
    out_ref[...] = dot(jax.nn.sigmoid(logits_ref[...]).astype(BF16), table_ref[...]).astype(BF16)


def column_spectrum(mask_logits):
    return pl.pallas_call(
        column_kernel,
        out_shape=jax.ShapeDtypeStruct((TILE_ROWS, 128), BF16),
        compiler_params=pltpu.CompilerParams(vmem_limit_bytes=6 * MIB),
        name="column_spectrum",
    )(mask_logits, jnp.asarray(COLUMN_FORWARD))


def pupil(scalars, step, j):
    ref, i = scalars[j % GROUPS], step * (STEP // GROUPS) + j // GROUPS
    across, along = ref[1, i], ref[2, i]
    row = lax.broadcasted_iota(jnp.int32, (FREQS, 128), 0) - FREQS // 2
    lane = jnp.bitwise_and(lax.broadcasted_iota(jnp.int32, (FREQS, 128), 1), FREQS - 1) - FREQS // 2
    row, lane = row.astype(F32) - across, lane.astype(F32) - along
    return row * row + lane * lane <= F32(RADIUS * RADIUS)


def image_kernel(group_ref, own_scalars, scalars_1, scalars_2, scalars_3, own_ref, before_ref, after_ref, target_ref, row_forward_ref,
                 row_inverse_ref, row_inverse_t_ref, inverse_ref, inverse_t_ref, out_ref, sums_ref,
                 fields_ref, row_field_ref, intensity_ref, cotangent_ref, spectra_ref, terms_ref, grad_ref, rounded_ref):
    scalars = [own_scalars, scalars_1, scalars_2, scalars_3]
    frame = jnp.concatenate([before_ref[...], own_ref[...], after_ref[...]], 0)
    product = dot(row_forward_ref[...], frame)
    swapped = pltpu.roll(product[FREQS:], FREQS, 1)
    spectrum = (product[:FREQS] + halves_sign(FREQS, -1.0, 1.0) * swapped).astype(BF16).astype(F32)
    spectra_ref[:FREQS] = spectrum
    spectra_ref[FREQS:] = pltpu.roll(spectrum, FREQS, 1) * halves_sign(FREQS, -1.0, 1.0)
    intensity_ref[...] = jnp.zeros_like(intensity_ref)

    steps = SOURCES // STEP

    def image_rows(step):
        blocks = []
        for j in range(STEP):
            inside = pupil(scalars, step, j)
            inside = jnp.concatenate([inside, inside], 0)
            blocks.append(jnp.where(inside, spectra_ref[...], F32(0)).astype(BF16))
        row_field = dot(row_inverse_ref[...], jnp.concatenate(blocks, 1)).astype(BF16)
        for j in range(STEP):
            start = pl.multiple_of((step * STEP + j) * ROWS, ROWS)
            row_field_ref[pl.ds(start, ROWS), :] = row_field[:, 128 * j:128 * (j + 1)]

    def weight(step, j):
        return scalars[j % GROUPS][0, step * (STEP // GROUPS) + j // GROUPS]

    image_rows(0)

    @pl.loop(0, steps)
    def _(step):
        start = pl.multiple_of(step * (STEP * ROWS), STEP * ROWS)
        row_field = row_field_ref[pl.ds(start, STEP * ROWS), :]
        for n in range(4):
            fields = dot(row_field, inverse_ref[:, 256 * n:256 * (n + 1)])
            fields_ref[pl.ds(start, STEP * ROWS), 256 * n:256 * (n + 1)] = fields
            power = fields[:, :128] * fields[:, :128] + fields[:, 128:] * fields[:, 128:]
            total = weight(step, 0) * power[:ROWS]
            for j in range(1, STEP):
                total = total + weight(step, j) * power[j * ROWS:(j + 1) * ROWS]
            intensity_ref[:, 128 * n:128 * (n + 1)] += total
        image_rows(jnp.minimum(step + 1, steps - 1))

    printed = jax.nn.sigmoid(F32(STEEPNESS) * (intensity_ref[...] - F32(THRESHOLD)))
    error_value = printed - target_ref[...].astype(F32)
    cotangent_ref[...] = F32(2.0 * STEEPNESS) * error_value * printed * (F32(1.0) - printed)
    error_rows = jnp.sum(error_value * error_value, 0, keepdims=True)
    error_lanes = (error_rows[:, :128] + error_rows[:, 128:256]) + (error_rows[:, 256:384] + error_rows[:, 384:])
    error_sum = jnp.sum(error_lanes, 1, keepdims=True)
    grad_ref[...] = jnp.zeros_like(grad_ref)

    rounded_ref[...] = jnp.zeros_like(rounded_ref)

    def add_block_grad(step):
        block_grad = dot(row_inverse_t_ref[...], rounded_ref[...])
        total = jnp.zeros((2 * FREQS, 128), F32)
        for j in range(STEP):
            inside = pupil(scalars, step, j)
            inside = jnp.concatenate([inside, inside], 0)
            total = total + jnp.where(inside, block_grad[:, 128 * j:128 * (j + 1)], F32(0))
        grad_ref[...] += total

    @pl.loop(0, steps)
    def _(step):
        start = pl.multiple_of(step * (STEP * ROWS), STEP * ROWS)
        add_block_grad(jnp.maximum(step - 1, 0))
        row_grad = None
        for n in range(4):
            cot = cotangent_ref[:, 128 * n:128 * (n + 1)]
            parts = []
            for j in range(STEP):
                scaling = (F32(2.0) * weight(step, j)) * cot
                at = pl.multiple_of(start + j * ROWS, ROWS)
                fields = fields_ref[pl.ds(at, ROWS), 256 * n:256 * (n + 1)]
                parts.append((jnp.concatenate([scaling, scaling], 1) * fields).astype(BF16))
            part = dot(jnp.concatenate(parts, 0), inverse_t_ref[256 * n:256 * (n + 1), :])
            row_grad = part if row_grad is None else row_grad + part
        row_field = row_field_ref[pl.ds(start, STEP * ROWS), :].astype(F32)
        terms = row_grad * row_field
        rounded = row_grad.astype(BF16)
        for j in range(STEP):
            terms_ref[pl.ds(step * STEP + j, 1), :] = jnp.sum(terms[j * ROWS:(j + 1) * ROWS], 0, keepdims=True)
            rounded_ref[:, 128 * j:128 * (j + 1)] = rounded[j * ROWS:(j + 1) * ROWS]

    add_block_grad(steps - 1)
    grads = grad_ref[...]
    out_ref[...] = grads[:FREQS] + halves_sign(FREQS, 1.0, -1.0) * pltpu.roll(grads[FREQS:], FREQS, 1)
    term = jnp.sum(terms_ref[...], 1, keepdims=True)
    row = lax.broadcasted_iota(jnp.int32, (SOURCES, 128), 0)
    lane = lax.broadcasted_iota(jnp.int32, (SOURCES, 128), 1)
    wanted = (row % GROUPS) * PER_GROUP + row // GROUPS
    term_row = jnp.sum(jnp.where(wanted == lane, term, F32(0)), 0, keepdims=True)
    lane = lax.broadcasted_iota(jnp.int32, (1, 128), 1)
    own = group_ref[0]
    for bit, width in ((1, PER_GROUP), (2, 2 * PER_GROUP)):
        swapped = jnp.where((lane // width) % 2 == 0, pltpu.roll(term_row, 128 - width, 1),
                            pltpu.roll(term_row, width, 1))
        term_row = jnp.where(jnp.bitwise_and(own, bit) != 0, swapped, term_row)
    term_row = jnp.where(lane < SOURCES, term_row, F32(0))
    sums_ref[...] = jnp.broadcast_to(jnp.where(lane == SOURCES, error_sum, term_row)[None], sums_ref.shape)


def image(group, scalars, own, before, after, target, peers):
    fixed = lambda i, g: (0, 0)
    whole = lambda shape: pl.BlockSpec(shape, fixed)
    return pl.pallas_call(
        image_kernel,
        grid_spec=pltpu.PrefetchScalarGridSpec(
            num_scalar_prefetch=1,
            grid=(1,),
            in_specs=[
                *[pl.BlockSpec(memory_space=pltpu.SMEM)] * GROUPS,
                whole((TILE_ROWS, 128)), whole((MARGIN, 128)), whole((MARGIN, 128)),
                pl.BlockSpec((ROWS, COLS), lambda i, g: (g[0], 0)),
                whole((128, FRAME)),
                pl.BlockSpec((ROWS, 128), lambda i, g: (g[0], 0)),
                pl.BlockSpec((128, ROWS), lambda i, g: (0, g[0])),
                whole((128, 2 * COLS)), whole((2 * COLS, 128)),
            ],
            out_specs=[whole((FREQS, 128)), pl.BlockSpec((peers, 1, 128), lambda i, g: (0, 0, 0))],
            scratch_shapes=[
                pltpu.VMEM((SOURCES * ROWS, 2 * COLS), F32),
                pltpu.VMEM((SOURCES * ROWS, 128), BF16),
                pltpu.VMEM((ROWS, COLS), F32),
                pltpu.VMEM((ROWS, COLS), F32),
                pltpu.VMEM((128, 128), F32),
                pltpu.VMEM((SOURCES, 128), F32),
                pltpu.VMEM((128, 128), F32),
                pltpu.VMEM((ROWS, STEP * 128), BF16),
            ],
        ),
        out_shape=[jax.ShapeDtypeStruct((FREQS, 128), F32), jax.ShapeDtypeStruct((peers, 1, 128), F32)],
        compiler_params=pltpu.CompilerParams(vmem_limit_bytes=44 * MIB),
        name="image",
    )(group, *scalars, own, before, after, target, jnp.asarray(ROW_FORWARD), jnp.asarray(ROW_INVERSE),
      jnp.asarray(np.ascontiguousarray(ROW_INVERSE.T)), jnp.asarray(COLUMN_INVERSE),
      jnp.asarray(np.ascontiguousarray(COLUMN_INVERSE.T)))


def split_dot(table, x):
    high = x.astype(BF16)
    low = (x - high.astype(F32)).astype(BF16)
    return dot(jnp.concatenate([table, table], 1), jnp.concatenate([high, low], 0))


def dot_split(x, table):
    high = x.astype(BF16)
    low = (x - high.astype(F32)).astype(BF16)
    return dot(jnp.concatenate([high, low], 1), jnp.concatenate([table, table], 0))


def product_gradient(spectrum_grad):
    lower = pltpu.roll(spectrum_grad, FREQS, 1) * halves_sign(FREQS, 1.0, -1.0)
    return jnp.concatenate([spectrum_grad, lower], 0)


def owned_kernel(grad_ref, logits_ref, row_ref, column_ref, out_ref):
    column_grad = split_dot(row_ref[...], product_gradient(grad_ref[...]))
    opening = jax.nn.sigmoid(logits_ref[...])
    out_ref[...] = dot_split(column_grad, column_ref[...]) * opening * (F32(1.0) - opening)


def owned_gradient(spectrum_grad, mask_logits):
    return pl.pallas_call(
        owned_kernel,
        out_shape=jax.ShapeDtypeStruct((TILE_ROWS, COLS), F32),
        compiler_params=pltpu.CompilerParams(vmem_limit_bytes=8 * MIB),
        name="owned_gradient",
    )(spectrum_grad, mask_logits,
      jnp.asarray(np.ascontiguousarray(ROW_FORWARD.T[MARGIN:MARGIN + TILE_ROWS])),
      jnp.asarray(np.ascontiguousarray(COLUMN_FORWARD.T)))


def last_kernel(group_ref, before_ref, after_ref, logits_ref, row_ref, column_ref, grad_ref, own_ref, beside_ref,
                far_ref, across_ref, weights_ref, out_ref, weight_grad_ref, loss_ref, *, pixels):
    first = pl.program_id(0) == 0
    spectrum_grad = jnp.where(first, before_ref[...], after_ref[...])
    column_grad = split_dot(row_ref[...], product_gradient(spectrum_grad))
    opening = jax.nn.sigmoid(logits_ref[...])
    added = dot_split(column_grad, column_ref[...]) * opening * (F32(1.0) - opening)
    out_ref[...] = grad_ref[...] + added

    @pl.when(first)
    def _():
        total = (own_ref[...] + beside_ref[...]) + (far_ref[...] + across_ref[...])
        row = total
        for bit, width in ((1, PER_GROUP), (2, 2 * PER_GROUP)):
            row = jnp.where(jnp.bitwise_and(group_ref[0], bit) != 0, pltpu.roll(row, 128 - width, 1), row)
        weight_grad_ref[...] = row[:, :PER_GROUP] / (F32(2.0) * weights_ref[...]) / F32(pixels)
        loss_ref[...] = total[:, SOURCES:SOURCES + 1] / F32(pixels)


def last_steps(group, before, after, mask_logits, grad, sums, weights, pixels):
    edge = lambda i: (i * (TILE_ROWS // MARGIN - 1), 0)
    fixed = lambda i: (0, 0)
    rows = np.concatenate([ROW_FORWARD.T[MARGIN + TILE_ROWS:], ROW_FORWARD.T[:MARGIN]], 0)
    return pl.pallas_call(
        functools.partial(last_kernel, pixels=pixels),
        grid=(2,),
        in_specs=[
            pl.BlockSpec(memory_space=pltpu.SMEM),
            pl.BlockSpec((FREQS, 128), fixed), pl.BlockSpec((FREQS, 128), fixed),
            pl.BlockSpec((MARGIN, COLS), edge),
            pl.BlockSpec((MARGIN, 128), lambda i: (i, 0)),
            pl.BlockSpec((128, COLS), fixed),
            pl.BlockSpec((MARGIN, COLS), edge),
            *[pl.BlockSpec((1, 128), fixed)] * GROUPS,
            pl.BlockSpec((1, PER_GROUP), fixed),
        ],
        out_specs=[pl.BlockSpec((MARGIN, COLS), edge), pl.BlockSpec((1, PER_GROUP), fixed),
                   pl.BlockSpec((1, 1), fixed)],
        out_shape=[jax.ShapeDtypeStruct((TILE_ROWS, COLS), F32), jax.ShapeDtypeStruct((1, PER_GROUP), F32),
                   jax.ShapeDtypeStruct((1, 1), F32)],
        input_output_aliases={6: 0},
        compiler_params=pltpu.CompilerParams(vmem_limit_bytes=4 * MIB),
        name="last_steps",
    )(group, before, after, mask_logits, jnp.asarray(np.ascontiguousarray(rows)),
      jnp.asarray(np.ascontiguousarray(COLUMN_FORWARD.T)), grad, *sums, weights.reshape(1, PER_GROUP))


def from_tiles_beside(last, first):
    peers = lax.axis_size("tile")
    up = [(i, i + 1) for i in range(peers - 1)]
    down = [(j, i) for i, j in up]
    return lax.ppermute(last, "tile", up), lax.ppermute(first, "tile", down)


def from_groups(x):
    return [x] + [lax.ppermute(x, "src", [(i, i ^ d) for i in range(GROUPS)]) for d in range(1, GROUPS)]


def on_device(mask_logits, target, weights, shifts):
    peers = lax.axis_size("tile")
    group = lax.axis_index("src").astype(jnp.int32).reshape(1)
    first, last, packed = edge_spectrum(mask_logits, weights, shifts)
    before, after = from_tiles_beside(last, first)
    scalars = from_groups(packed)
    own = column_spectrum(mask_logits)
    partial, sums = image(group, scalars, own, before, after, target, peers)
    chip = partial + lax.ppermute(partial, "src", [(i, i ^ 1) for i in range(GROUPS)])
    far = lax.ppermute(chip, "src", [(i, i ^ 2) for i in range(GROUPS)])
    sums = lax.all_to_all(sums, "tile", 0, 0, tiled=True)
    spectrum_grad = chip + far
    grad_before, grad_after = from_tiles_beside(spectrum_grad, spectrum_grad)
    sums = from_groups(jnp.sum(sums, 0))
    grad = owned_gradient(spectrum_grad, mask_logits)
    mask_grad, weight_grad, loss = last_steps(
        group, grad_before, grad_after, mask_logits, grad, sums, weights, TILE_ROWS * COLS * peers)
    return mask_grad, weight_grad.reshape(PER_GROUP), loss.reshape(())


def solution(mesh):
    placed = (P("tile", None), P("tile", None), P("src"), P("src", None))
    return jax.shard_map(
        on_device,
        mesh=mesh,
        in_specs=placed,
        out_specs=(P("tile", None), P("src"), P()),
        check_vma=False,
    )
```

```python
import functools

import numpy as np
import jax
import jax.numpy as jnp
from jax import lax
from jax.experimental import pallas as pl
from jax.experimental.pallas import tpu as pltpu
from jax.sharding import PartitionSpec as P

FREQS = 64
RADIUS = 20
MARGIN = 64
COLS = 512
TILE_ROWS = 512
FRAME = 640
SOURCES = 64
GROUPS = 4
PER_GROUP = SOURCES // GROUPS
ROWS = TILE_ROWS // GROUPS
MIB = 1024 * 1024
STEEPNESS = 12.0
THRESHOLD = 0.2
STEP = 16
F32 = jnp.float32
BF16 = jnp.bfloat16


def angles(length_used, offset, period):
    position = np.arange(length_used, dtype=np.int32)[:, None] + offset
    frequency = np.arange(FREQS, dtype=np.int32)[None, :] - FREQS // 2
    cycles = np.mod(position * frequency, period).astype(np.float32)
    angle_value = (cycles * np.float32(2.0 * 3.141592653589793 / period)).astype(np.float64)
    return np.cos(angle_value).astype(np.float32), np.sin(angle_value).astype(np.float32)


def make_tables():
    column_cosine, column_sine = angles(COLS, 0, COLS)
    column_forward = np.concatenate([column_cosine, -column_sine], 1)
    frame_cosine, frame_sine = angles(FRAME, 0, FRAME)
    row_forward = np.concatenate([frame_cosine.T, -frame_sine.T], 0)
    owned_cosine, owned_sine = angles(TILE_ROWS, MARGIN, FRAME)
    row_inverse = np.concatenate([owned_cosine, owned_sine], 1) / np.float32(FRAME)
    cosine_scaled = column_cosine.T / np.float32(COLS)
    sine_scaled = column_sine.T / np.float32(COLS)
    upper_block = np.concatenate([cosine_scaled, sine_scaled], 1)
    lower_block = np.concatenate([-sine_scaled, cosine_scaled], 1)
    column_inverse = np.concatenate([upper_block, lower_block], 0)
    chunked = column_inverse.reshape(2 * FREQS, 2, COLS // 128, 128).transpose(0, 2, 1, 3)
    chunked = chunked.reshape(2 * FREQS, 2 * COLS)
    rounded = lambda a: np.ascontiguousarray(a).astype(BF16)
    return [rounded(a) for a in (column_forward, row_forward, row_inverse, chunked)]


COLUMN_FORWARD, ROW_FORWARD, ROW_INVERSE, COLUMN_INVERSE = make_tables()


def stacked(table):
    return np.concatenate([table[:, c:c + 128] for c in range(0, table.shape[1], 128)], 0)


PARTS = [ROW_INVERSE, stacked(ROW_INVERSE.T), COLUMN_INVERSE.T, stacked(COLUMN_INVERSE), stacked(ROW_FORWARD)]
IMAGE_TABLE = np.ascontiguousarray(np.concatenate(PARTS, 0))
INVERSE_T_AT = 2 * TILE_ROWS
INVERSE_AT = INVERSE_T_AT + 2 * COLS
FORWARD_AT = INVERSE_AT + 8 * 128


def dot(a, b):
    return jnp.dot(a, b, preferred_element_type=F32)


def halves_sign(rows, left, right):
    lane = lax.broadcasted_iota(jnp.int32, (rows, 128), 1)
    return jnp.where(lane < FREQS, F32(left), F32(right))


def edge_kernel(group_ref, logits_ref, table_ref, weights_ref, shifts_ref, edge_out, packed_out,
                rows, table, weights, shifts, semaphores):
    start = jnp.where(group_ref[0] % 2 == 0, TILE_ROWS - MARGIN, 0)
    rows_from = logits_ref.at[pl.ds(pl.multiple_of(start, MARGIN), MARGIN), :]
    pairs = ((rows_from, rows), (table_ref, table), (weights_ref, weights), (shifts_ref, shifts))
    copies = [pltpu.make_async_copy(a, b, semaphores.at[i]) for i, (a, b) in enumerate(pairs)]
    for copy in copies:
        copy.start()
    for copy in copies:
        copy.wait()
    edge_out[...] = dot(jax.nn.sigmoid(rows[...]).astype(BF16), table[...]).astype(BF16)
    packed_out[0:1] = weights[...]
    packed_out[1:3] = shifts[...].astype(F32)


def edge_spectrum(group, mask_logits, weights, shifts):
    return pl.pallas_call(
        edge_kernel,
        in_specs=[pl.BlockSpec(memory_space=pltpu.SMEM)] + [pl.BlockSpec(memory_space=pltpu.HBM)] * 4,
        out_shape=[jax.ShapeDtypeStruct((MARGIN, 128), BF16), jax.ShapeDtypeStruct((3, PER_GROUP), F32)],
        scratch_shapes=[
            pltpu.VMEM((MARGIN, COLS), F32), pltpu.VMEM((COLS, 128), BF16),
            pltpu.VMEM((1, PER_GROUP), F32), pltpu.VMEM((2, PER_GROUP), jnp.int32),
            pltpu.SemaphoreType.DMA((4,)),
        ],
        compiler_params=pltpu.CompilerParams(vmem_limit_bytes=60 * MIB),
        name="edge_spectrum",
    )(group, mask_logits, jnp.asarray(COLUMN_FORWARD), weights.reshape(1, PER_GROUP), shifts.T)


def column_kernel(logits_ref, table_ref, image_table_ref, out_ref, image_table_out, semaphore):
    copy = pltpu.make_async_copy(image_table_ref, image_table_out, semaphore)
    copy.start()
    out_ref[...] = dot(jax.nn.sigmoid(logits_ref[...]).astype(BF16), table_ref[...]).astype(BF16)
    copy.wait()


def column_spectrum(mask_logits):
    return pl.pallas_call(
        column_kernel,
        in_specs=[pl.BlockSpec(), pl.BlockSpec(), pl.BlockSpec(memory_space=pltpu.HBM)],
        out_shape=[jax.ShapeDtypeStruct((TILE_ROWS, 128), BF16), jax.ShapeDtypeStruct(IMAGE_TABLE.shape, BF16)],
        scratch_shapes=[pltpu.SemaphoreType.DMA],
        compiler_params=pltpu.CompilerParams(vmem_limit_bytes=8 * MIB),
        name="column_spectrum",
    )(mask_logits, jnp.asarray(COLUMN_FORWARD), jnp.asarray(IMAGE_TABLE))


def pupil(scalars, step, j):
    ref, i = scalars[j % GROUPS], step * (STEP // GROUPS) + j // GROUPS
    across, along = ref[1, i], ref[2, i]
    row = lax.broadcasted_iota(jnp.int32, (FREQS, 128), 0) - FREQS // 2
    lane = jnp.bitwise_and(lax.broadcasted_iota(jnp.int32, (FREQS, 128), 1), FREQS - 1) - FREQS // 2
    row, lane = row.astype(F32) - across, lane.astype(F32) - along
    return row * row + lane * lane <= F32(RADIUS * RADIUS)


def image_kernel(group_ref, own_scalars, scalars_1, scalars_2, scalars_3, own_ref, near_ref, other_ref, target_ref, table_ref, out_ref, sums_ref,
                 fields_ref, row_field_ref, intensity_ref, cotangent_ref, spectra_ref, terms_ref, grad_ref, rounded_ref, frame_ref):
    scalars = [own_scalars, scalars_1, scalars_2, scalars_3]
    def beside(start, count):
        return jnp.concatenate([table_ref[start + 128 * i:start + 128 * (i + 1), :] for i in range(count)], 1)

    row_inverse = table_ref.at[pl.ds(pl.multiple_of(group_ref[0] * ROWS, ROWS), ROWS), :]
    row_inverse_t = table_ref.at[pl.ds(pl.multiple_of(TILE_ROWS + group_ref[0] * 128, 128), 128), :]
    even = group_ref[0] % 2 == 0
    frame_ref[MARGIN:MARGIN + TILE_ROWS] = own_ref[...]

    @pl.when(even)
    def _():
        frame_ref[:MARGIN] = near_ref[...]
        frame_ref[MARGIN + TILE_ROWS:] = other_ref[...]

    @pl.when(jnp.logical_not(even))
    def _():
        frame_ref[:MARGIN] = other_ref[...]
        frame_ref[MARGIN + TILE_ROWS:] = near_ref[...]

    product = dot(beside(FORWARD_AT, FRAME // 128), frame_ref[...])
    swapped = pltpu.roll(product[FREQS:], FREQS, 1)
    spectrum = (product[:FREQS] + halves_sign(FREQS, -1.0, 1.0) * swapped).astype(BF16).astype(F32)
    spectra_ref[:FREQS] = spectrum
    spectra_ref[FREQS:] = pltpu.roll(spectrum, FREQS, 1) * halves_sign(FREQS, -1.0, 1.0)
    intensity_ref[...] = jnp.zeros_like(intensity_ref)

    steps = SOURCES // STEP

    def image_rows(step):
        blocks = []
        for j in range(STEP):
            inside = pupil(scalars, step, j)
            inside = jnp.concatenate([inside, inside], 0)
            blocks.append(jnp.where(inside, spectra_ref[...], F32(0)).astype(BF16))
        row_field = dot(row_inverse[...], jnp.concatenate(blocks, 1)).astype(BF16)
        for j in range(STEP):
            start = pl.multiple_of((step * STEP + j) * ROWS, ROWS)
            row_field_ref[pl.ds(start, ROWS), :] = row_field[:, 128 * j:128 * (j + 1)]

    def weight(step, j):
        return scalars[j % GROUPS][0, step * (STEP // GROUPS) + j // GROUPS]

    image_rows(0)

    @pl.loop(0, steps)
    def _(step):
        start = pl.multiple_of(step * (STEP * ROWS), STEP * ROWS)
        row_field = row_field_ref[pl.ds(start, STEP * ROWS), :]
        for n in range(4):
            fields = dot(row_field, beside(INVERSE_AT + 256 * n, 2))
            fields_ref[pl.ds(start, STEP * ROWS), 256 * n:256 * (n + 1)] = fields
            power = fields[:, :128] * fields[:, :128] + fields[:, 128:] * fields[:, 128:]
            total = weight(step, 0) * power[:ROWS]
            for j in range(1, STEP):
                total = total + weight(step, j) * power[j * ROWS:(j + 1) * ROWS]
            intensity_ref[:, 128 * n:128 * (n + 1)] += total
        image_rows(jnp.minimum(step + 1, steps - 1))

    printed = jax.nn.sigmoid(F32(STEEPNESS) * (intensity_ref[...] - F32(THRESHOLD)))
    error_value = printed - target_ref[...].astype(F32)
    cotangent_ref[...] = F32(2.0 * STEEPNESS) * error_value * printed * (F32(1.0) - printed)
    error_rows = jnp.sum(error_value * error_value, 0, keepdims=True)
    error_lanes = (error_rows[:, :128] + error_rows[:, 128:256]) + (error_rows[:, 256:384] + error_rows[:, 384:])
    error_sum = jnp.sum(error_lanes, 1, keepdims=True)
    grad_ref[...] = jnp.zeros_like(grad_ref)

    rounded_ref[...] = jnp.zeros_like(rounded_ref)

    def add_block_grad(step):
        block_grad = dot(row_inverse_t[...], rounded_ref[...])
        total = jnp.zeros((2 * FREQS, 128), F32)
        for j in range(STEP):
            inside = pupil(scalars, step, j)
            inside = jnp.concatenate([inside, inside], 0)
            total = total + jnp.where(inside, block_grad[:, 128 * j:128 * (j + 1)], F32(0))
        grad_ref[...] += total

    @pl.loop(0, steps)
    def _(step):
        start = pl.multiple_of(step * (STEP * ROWS), STEP * ROWS)
        add_block_grad(jnp.maximum(step - 1, 0))
        row_grad = None
        for n in range(4):
            cot = cotangent_ref[:, 128 * n:128 * (n + 1)]
            parts = []
            for j in range(STEP):
                scaling = (F32(2.0) * weight(step, j)) * cot
                at = pl.multiple_of(start + j * ROWS, ROWS)
                fields = fields_ref[pl.ds(at, ROWS), 256 * n:256 * (n + 1)]
                parts.append((jnp.concatenate([scaling, scaling], 1) * fields).astype(BF16))
            part = dot(jnp.concatenate(parts, 0), table_ref[INVERSE_T_AT + 256 * n:INVERSE_T_AT + 256 * (n + 1), :])
            row_grad = part if row_grad is None else row_grad + part
        row_field = row_field_ref[pl.ds(start, STEP * ROWS), :].astype(F32)
        terms = row_grad * row_field
        rounded = row_grad.astype(BF16)
        for j in range(STEP):
            terms_ref[pl.ds(step * STEP + j, 1), :] = jnp.sum(terms[j * ROWS:(j + 1) * ROWS], 0, keepdims=True)
            rounded_ref[:, 128 * j:128 * (j + 1)] = rounded[j * ROWS:(j + 1) * ROWS]

    add_block_grad(steps - 1)
    grads = grad_ref[...]
    out_ref[...] = grads[:FREQS] + halves_sign(FREQS, 1.0, -1.0) * pltpu.roll(grads[FREQS:], FREQS, 1)
    term = jnp.sum(terms_ref[...], 1, keepdims=True)
    row = lax.broadcasted_iota(jnp.int32, (SOURCES, 128), 0)
    lane = lax.broadcasted_iota(jnp.int32, (SOURCES, 128), 1)
    wanted = (row % GROUPS) * PER_GROUP + row // GROUPS
    term_row = jnp.sum(jnp.where(wanted == lane, term, F32(0)), 0, keepdims=True)
    lane = lax.broadcasted_iota(jnp.int32, (1, 128), 1)
    own = group_ref[0]
    for bit, width in ((1, PER_GROUP), (2, 2 * PER_GROUP)):
        swapped = jnp.where((lane // width) % 2 == 0, pltpu.roll(term_row, 128 - width, 1),
                            pltpu.roll(term_row, width, 1))
        term_row = jnp.where(jnp.bitwise_and(own, bit) != 0, swapped, term_row)
    term_row = jnp.where(lane < SOURCES, term_row, F32(0))
    sums_ref[...] = jnp.broadcast_to(jnp.where(lane == SOURCES, error_sum, term_row)[None], sums_ref.shape)


def image(group, scalars, own, near, other, target, table, peers):
    fixed = lambda i, g: (0, 0)
    whole = lambda shape: pl.BlockSpec(shape, fixed)
    return pl.pallas_call(
        image_kernel,
        grid_spec=pltpu.PrefetchScalarGridSpec(
            num_scalar_prefetch=1,
            grid=(1,),
            in_specs=[
                *[pl.BlockSpec(memory_space=pltpu.SMEM)] * GROUPS,
                whole((TILE_ROWS, 128)), whole((MARGIN, 128)), whole((MARGIN, 128)),
                pl.BlockSpec((ROWS, COLS), lambda i, g: (g[0], 0)),
                whole(IMAGE_TABLE.shape),
            ],
            out_specs=[whole((FREQS, 128)), pl.BlockSpec((peers, 1, 128), lambda i, g: (0, 0, 0))],
            scratch_shapes=[
                pltpu.VMEM((SOURCES * ROWS, 2 * COLS), F32),
                pltpu.VMEM((SOURCES * ROWS, 128), BF16),
                pltpu.VMEM((ROWS, COLS), F32),
                pltpu.VMEM((ROWS, COLS), F32),
                pltpu.VMEM((128, 128), F32),
                pltpu.VMEM((SOURCES, 128), F32),
                pltpu.VMEM((128, 128), F32),
                pltpu.VMEM((ROWS, STEP * 128), BF16),
                pltpu.VMEM((FRAME, 128), BF16),
            ],
        ),
        out_shape=[jax.ShapeDtypeStruct((FREQS, 128), F32), jax.ShapeDtypeStruct((peers, 1, 128), F32)],
        compiler_params=pltpu.CompilerParams(vmem_limit_bytes=44 * MIB),
        name="image",
    )(group, *scalars, own, near, other, target, table)


def split_dot(table, x):
    high = x.astype(BF16)
    low = (x - high.astype(F32)).astype(BF16)
    return dot(jnp.concatenate([table, table], 1), jnp.concatenate([high, low], 0))


def dot_split(x, table):
    high = x.astype(BF16)
    low = (x - high.astype(F32)).astype(BF16)
    return dot(jnp.concatenate([high, low], 1), jnp.concatenate([table, table], 0))


def product_gradient(spectrum_grad):
    lower = pltpu.roll(spectrum_grad, FREQS, 1) * halves_sign(FREQS, 1.0, -1.0)
    return jnp.concatenate([spectrum_grad, lower], 0)


def owned_kernel(grad_ref, logits_ref, row_ref, column_ref, out_ref, edges_ref, slope_ref):
    column_grad = split_dot(row_ref[...], product_gradient(grad_ref[...]))
    opening = jax.nn.sigmoid(logits_ref[...])
    slope = opening * (F32(1.0) - opening)
    out = dot_split(column_grad, column_ref[...]) * slope
    out_ref[...] = out
    edges_ref[:MARGIN] = out[:MARGIN]
    edges_ref[MARGIN:] = out[TILE_ROWS - MARGIN:]
    slope_ref[:MARGIN] = slope[:MARGIN]
    slope_ref[MARGIN:] = slope[TILE_ROWS - MARGIN:]


def owned_gradient(spectrum_grad, mask_logits):
    return pl.pallas_call(
        owned_kernel,
        out_shape=[jax.ShapeDtypeStruct((n, COLS), F32) for n in (TILE_ROWS, 2 * MARGIN, 2 * MARGIN)],
        compiler_params=pltpu.CompilerParams(vmem_limit_bytes=10 * MIB),
        name="owned_gradient",
    )(spectrum_grad, mask_logits,
      jnp.asarray(np.ascontiguousarray(ROW_FORWARD.T[MARGIN:MARGIN + TILE_ROWS])),
      jnp.asarray(np.ascontiguousarray(COLUMN_FORWARD.T)))


def last_kernel(group_ref, near_ref, other_ref, edges_ref, slope_ref, row_ref, column_ref, own_ref, beside_ref,
                far_ref, across_ref, weights_ref, grad_ref, out_ref, weight_grad_ref, loss_ref,
                rows_ref, semaphores, *, pixels):
    del grad_ref
    even = group_ref[0] % 2 == 0
    before = jnp.where(even, near_ref[...], other_ref[...])
    after = jnp.where(even, other_ref[...], near_ref[...])
    column_grad = jnp.concatenate([split_dot(row_ref[:MARGIN], product_gradient(before)),
                                   split_dot(row_ref[MARGIN:], product_gradient(after))], 0)
    rows_ref[...] = edges_ref[...] + dot_split(column_grad, column_ref[...]) * slope_ref[...]
    copies = [
        pltpu.make_async_copy(rows_ref.at[pl.ds(0, MARGIN), :], out_ref.at[pl.ds(0, MARGIN), :], semaphores.at[0]),
        pltpu.make_async_copy(rows_ref.at[pl.ds(MARGIN, MARGIN), :],
                              out_ref.at[pl.ds(TILE_ROWS - MARGIN, MARGIN), :], semaphores.at[1]),
    ]
    for copy in copies:
        copy.start()
    total = (own_ref[...] + beside_ref[...]) + (far_ref[...] + across_ref[...])
    row = total
    for bit, width in ((1, PER_GROUP), (2, 2 * PER_GROUP)):
        row = jnp.where(jnp.bitwise_and(group_ref[0], bit) != 0, pltpu.roll(row, 128 - width, 1), row)
    weight_grad_ref[...] = row[:, :PER_GROUP] / (F32(2.0) * weights_ref[...]) / F32(pixels)
    loss_ref[...] = total[:, SOURCES:SOURCES + 1] / F32(pixels)
    for copy in copies:
        copy.wait()


def last_steps(group, near, other, edges, slope, grad, sums, weights, pixels):
    rows = np.concatenate([ROW_FORWARD.T[MARGIN + TILE_ROWS:], ROW_FORWARD.T[:MARGIN]], 0)
    block = pl.BlockSpec()
    hbm = pl.BlockSpec(memory_space=pltpu.HBM)
    return pl.pallas_call(
        functools.partial(last_kernel, pixels=pixels),
        in_specs=[pl.BlockSpec(memory_space=pltpu.SMEM)] + [block] * 11 + [hbm],
        out_specs=[hbm, block, block],
        out_shape=[jax.ShapeDtypeStruct((TILE_ROWS, COLS), F32), jax.ShapeDtypeStruct((1, PER_GROUP), F32),
                   jax.ShapeDtypeStruct((1, 1), F32)],
        scratch_shapes=[pltpu.VMEM((2 * MARGIN, COLS), F32), pltpu.SemaphoreType.DMA((2,))],
        input_output_aliases={12: 0},
        compiler_params=pltpu.CompilerParams(vmem_limit_bytes=4 * MIB),
        name="last_steps",
    )(group, near, other, edges, slope, jnp.asarray(np.ascontiguousarray(rows)),
      jnp.asarray(np.ascontiguousarray(COLUMN_FORWARD.T)), *sums, weights.reshape(1, PER_GROUP), grad)


def from_tile_beside(x):
    peers = lax.axis_size("tile")
    pairs = [(s * peers + i, s * peers + j) for s in range(GROUPS) for i in range(peers)
             for j in [i + 1 - 2 * (s % 2)] if 0 <= j < peers]
    return lax.ppermute(x, ("src", "tile"), pairs)


def from_group(x, d):
    return lax.ppermute(x, "src", [(i, i ^ d) for i in range(GROUPS)])


def from_core(x):
    return from_group(x, 1)


def from_chip(x):
    return from_group(x, 2)


def on_device(mask_logits, target, weights, shifts):
    peers = lax.axis_size("tile")
    group = lax.axis_index("src").astype(jnp.int32).reshape(1)
    edge, packed = edge_spectrum(group, mask_logits, weights, shifts)
    near = from_tile_beside(edge)
    packed_far = from_chip(packed)
    packed_core = from_core(packed)
    own, table = column_spectrum(mask_logits)
    near, packed_far, own = lax.optimization_barrier((near, packed_far, own))
    scalars = [packed, packed_core, packed_far, from_core(packed_far)]
    partial, sums = image(group, scalars, own, near, from_core(near), target, table, peers)
    chip = partial + from_core(partial)
    far = from_chip(chip)
    sums = lax.all_to_all(sums, "tile", 0, 0, tiled=True)
    spectrum_grad = chip + far
    near_grad = from_tile_beside(spectrum_grad)
    sums = jnp.sum(sums, 0)
    sums_far = from_chip(sums)
    grad, edges, slope = owned_gradient(spectrum_grad, mask_logits)
    near_grad, sums_far, edges = lax.optimization_barrier((near_grad, sums_far, edges))
    sums = [sums, from_core(sums), sums_far, from_core(sums_far)]
    mask_grad, weight_grad, loss = last_steps(
        group, near_grad, from_core(near_grad), edges, slope, grad, sums, weights, TILE_ROWS * COLS * peers)
    return mask_grad, weight_grad.reshape(PER_GROUP), loss.reshape(())


def solution(mesh):
    placed = (P("tile", None), P("tile", None), P("src"), P("src", None))
    return jax.shard_map(
        on_device,
        mesh=mesh,
        in_specs=placed,
        out_specs=(P("tile", None), P("src"), P()),
        check_vma=False,
    )
```

```python
import functools

import numpy as np
import jax
import jax.numpy as jnp
from jax import lax
from jax.experimental import pallas as pl
from jax.experimental.pallas import tpu as pltpu
from jax.sharding import PartitionSpec as P

FREQS = 64
RADIUS = 20
MARGIN = 64
COLS = 512
TILE_ROWS = 512
FRAME = 640
SOURCES = 64
GROUPS = 4
PER_GROUP = SOURCES // GROUPS
ROWS = TILE_ROWS // GROUPS
MIB = 1024 * 1024
STEEPNESS = 12.0
THRESHOLD = 0.2
STEP = 16
F32 = jnp.float32
BF16 = jnp.bfloat16


def angles(length_used, offset, period):
    position = np.arange(length_used, dtype=np.int32)[:, None] + offset
    frequency = np.arange(FREQS, dtype=np.int32)[None, :] - FREQS // 2
    cycles = np.mod(position * frequency, period).astype(np.float32)
    angle_value = (cycles * np.float32(2.0 * 3.141592653589793 / period)).astype(np.float64)
    return np.cos(angle_value).astype(np.float32), np.sin(angle_value).astype(np.float32)


def make_tables():
    column_cosine, column_sine = angles(COLS, 0, COLS)
    column_forward = np.concatenate([column_cosine, -column_sine], 1)
    frame_cosine, frame_sine = angles(FRAME, 0, FRAME)
    row_forward = np.concatenate([frame_cosine.T, -frame_sine.T], 0)
    owned_cosine, owned_sine = angles(TILE_ROWS, MARGIN, FRAME)
    row_inverse = np.concatenate([owned_cosine, owned_sine], 1) / np.float32(FRAME)
    cosine_scaled = column_cosine.T / np.float32(COLS)
    sine_scaled = column_sine.T / np.float32(COLS)
    upper_block = np.concatenate([cosine_scaled, sine_scaled], 1)
    lower_block = np.concatenate([-sine_scaled, cosine_scaled], 1)
    column_inverse = np.concatenate([upper_block, lower_block], 0)
    chunked = column_inverse.reshape(2 * FREQS, 2, COLS // 128, 128).transpose(0, 2, 1, 3)
    chunked = chunked.reshape(2 * FREQS, 2 * COLS)
    rounded = lambda a: np.ascontiguousarray(a).astype(BF16)
    return [rounded(a) for a in (column_forward, row_forward, row_inverse, chunked)]


COLUMN_FORWARD, ROW_FORWARD, ROW_INVERSE, COLUMN_INVERSE = make_tables()


def stacked(table):
    return np.concatenate([table[:, c:c + 128] for c in range(0, table.shape[1], 128)], 0)


PARTS = [ROW_INVERSE, stacked(ROW_INVERSE.T), COLUMN_INVERSE.T, stacked(COLUMN_INVERSE), stacked(ROW_FORWARD)]
IMAGE_TABLE = np.ascontiguousarray(np.concatenate(PARTS, 0))
INVERSE_T_AT = 2 * TILE_ROWS
INVERSE_AT = INVERSE_T_AT + 2 * COLS
FORWARD_AT = INVERSE_AT + 8 * 128


def dot(a, b):
    return jnp.dot(a, b, preferred_element_type=F32)


def halves_sign(rows, left, right):
    lane = lax.broadcasted_iota(jnp.int32, (rows, 128), 1)
    return jnp.where(lane < FREQS, F32(left), F32(right))


def edge_kernel(group_ref, logits_ref, table_ref, weights_ref, shifts_ref, edge_out, packed_out,
                rows, table, weights, shifts, semaphores):
    start = jnp.where(group_ref[0] % 2 == 0, TILE_ROWS - MARGIN, 0)
    rows_from = logits_ref.at[pl.ds(pl.multiple_of(start, MARGIN), MARGIN), :]
    pairs = ((rows_from, rows), (table_ref, table), (weights_ref, weights), (shifts_ref, shifts))
    copies = [pltpu.make_async_copy(a, b, semaphores.at[i]) for i, (a, b) in enumerate(pairs)]
    for copy in copies:
        copy.start()
    for copy in copies:
        copy.wait()
    edge_out[...] = dot(jax.nn.sigmoid(rows[...]).astype(BF16), table[...]).astype(BF16)
    packed_out[0:1] = weights[...]
    packed_out[1:3] = shifts[...].astype(F32)


def edge_spectrum(group, mask_logits, weights, shifts):
    return pl.pallas_call(
        edge_kernel,
        in_specs=[pl.BlockSpec(memory_space=pltpu.SMEM)] + [pl.BlockSpec(memory_space=pltpu.HBM)] * 4,
        out_shape=[jax.ShapeDtypeStruct((MARGIN, 128), BF16), jax.ShapeDtypeStruct((3, PER_GROUP), F32)],
        scratch_shapes=[
            pltpu.VMEM((MARGIN, COLS), F32), pltpu.VMEM((COLS, 128), BF16),
            pltpu.VMEM((1, PER_GROUP), F32), pltpu.VMEM((2, PER_GROUP), jnp.int32),
            pltpu.SemaphoreType.DMA((4,)),
        ],
        compiler_params=pltpu.CompilerParams(vmem_limit_bytes=60 * MIB),
        name="edge_spectrum",
    )(group, mask_logits, jnp.asarray(COLUMN_FORWARD), weights.reshape(1, PER_GROUP), shifts.T)


def column_kernel(logits_ref, table_ref, image_table_ref, out_ref, image_table_out, semaphore):
    copy = pltpu.make_async_copy(image_table_ref, image_table_out, semaphore)
    copy.start()
    out_ref[...] = dot(jax.nn.sigmoid(logits_ref[...]).astype(BF16), table_ref[...]).astype(BF16)
    copy.wait()


def column_spectrum(mask_logits):
    return pl.pallas_call(
        column_kernel,
        in_specs=[pl.BlockSpec(), pl.BlockSpec(), pl.BlockSpec(memory_space=pltpu.HBM)],
        out_shape=[jax.ShapeDtypeStruct((TILE_ROWS, 128), BF16), jax.ShapeDtypeStruct(IMAGE_TABLE.shape, BF16)],
        scratch_shapes=[pltpu.SemaphoreType.DMA],
        compiler_params=pltpu.CompilerParams(vmem_limit_bytes=8 * MIB),
        name="column_spectrum",
    )(mask_logits, jnp.asarray(COLUMN_FORWARD), jnp.asarray(IMAGE_TABLE))


def pupil(scalars, step, j):
    ref, i = scalars[j % GROUPS], step * (STEP // GROUPS) + j // GROUPS
    across, along = ref[1, i], ref[2, i]
    row = lax.broadcasted_iota(jnp.int32, (FREQS, 128), 0) - FREQS // 2
    lane = jnp.bitwise_and(lax.broadcasted_iota(jnp.int32, (FREQS, 128), 1), FREQS - 1) - FREQS // 2
    row, lane = row.astype(F32) - across, lane.astype(F32) - along
    return row * row + lane * lane <= F32(RADIUS * RADIUS)


def image_kernel(group_ref, own_scalars, scalars_1, scalars_2, scalars_3, own_ref, near_ref, other_ref, target_ref, table_ref, out_ref,
                 fields_ref, row_field_ref, intensity_ref, cotangent_ref, spectra_ref, terms_ref, grad_ref, rounded_ref, frame_ref):
    scalars = [own_scalars, scalars_1, scalars_2, scalars_3]
    def beside(start, count):
        return jnp.concatenate([table_ref[start + 128 * i:start + 128 * (i + 1), :] for i in range(count)], 1)

    row_inverse = table_ref.at[pl.ds(pl.multiple_of(group_ref[0] * ROWS, ROWS), ROWS), :]
    row_inverse_t = table_ref.at[pl.ds(pl.multiple_of(TILE_ROWS + group_ref[0] * 128, 128), 128), :]
    even = group_ref[0] % 2 == 0
    frame_ref[MARGIN:MARGIN + TILE_ROWS] = own_ref[...]

    @pl.when(even)
    def _():
        frame_ref[:MARGIN] = near_ref[...]
        frame_ref[MARGIN + TILE_ROWS:] = other_ref[...]

    @pl.when(jnp.logical_not(even))
    def _():
        frame_ref[:MARGIN] = other_ref[...]
        frame_ref[MARGIN + TILE_ROWS:] = near_ref[...]

    product = dot(beside(FORWARD_AT, FRAME // 128), frame_ref[...])
    swapped = pltpu.roll(product[FREQS:], FREQS, 1)
    spectrum = (product[:FREQS] + halves_sign(FREQS, -1.0, 1.0) * swapped).astype(BF16).astype(F32)
    spectra_ref[:FREQS] = spectrum
    spectra_ref[FREQS:] = pltpu.roll(spectrum, FREQS, 1) * halves_sign(FREQS, -1.0, 1.0)
    intensity_ref[...] = jnp.zeros_like(intensity_ref)

    steps = SOURCES // STEP

    def image_rows(step):
        blocks = []
        for j in range(STEP):
            inside = pupil(scalars, step, j)
            inside = jnp.concatenate([inside, inside], 0)
            blocks.append(jnp.where(inside, spectra_ref[...], F32(0)).astype(BF16))
        row_field = dot(row_inverse[...], jnp.concatenate(blocks, 1)).astype(BF16)
        for j in range(STEP):
            start = pl.multiple_of((step * STEP + j) * ROWS, ROWS)
            row_field_ref[pl.ds(start, ROWS), :] = row_field[:, 128 * j:128 * (j + 1)]

    def weight(step, j):
        return scalars[j % GROUPS][0, step * (STEP // GROUPS) + j // GROUPS]

    image_rows(0)

    @pl.loop(0, steps)
    def _(step):
        start = pl.multiple_of(step * (STEP * ROWS), STEP * ROWS)
        row_field = row_field_ref[pl.ds(start, STEP * ROWS), :]
        for n in range(4):
            fields = dot(row_field, beside(INVERSE_AT + 256 * n, 2))
            fields_ref[pl.ds(start, STEP * ROWS), 256 * n:256 * (n + 1)] = fields
            power = fields[:, :128] * fields[:, :128] + fields[:, 128:] * fields[:, 128:]
            total = weight(step, 0) * power[:ROWS]
            for j in range(1, STEP):
                total = total + weight(step, j) * power[j * ROWS:(j + 1) * ROWS]
            intensity_ref[:, 128 * n:128 * (n + 1)] += total
        image_rows(jnp.minimum(step + 1, steps - 1))

    printed = jax.nn.sigmoid(F32(STEEPNESS) * (intensity_ref[...] - F32(THRESHOLD)))
    error_value = printed - target_ref[...].astype(F32)
    cotangent_ref[...] = F32(2.0 * STEEPNESS) * error_value * printed * (F32(1.0) - printed)
    error_rows = jnp.sum(error_value * error_value, 0, keepdims=True)
    error_lanes = (error_rows[:, :128] + error_rows[:, 128:256]) + (error_rows[:, 256:384] + error_rows[:, 384:])
    error_sum = jnp.sum(error_lanes, 1, keepdims=True)
    grad_ref[...] = jnp.zeros_like(grad_ref)

    rounded_ref[...] = jnp.zeros_like(rounded_ref)

    def add_block_grad(step):
        block_grad = dot(row_inverse_t[...], rounded_ref[...])
        total = jnp.zeros((2 * FREQS, 128), F32)
        for j in range(STEP):
            inside = pupil(scalars, step, j)
            inside = jnp.concatenate([inside, inside], 0)
            total = total + jnp.where(inside, block_grad[:, 128 * j:128 * (j + 1)], F32(0))
        grad_ref[...] += total

    @pl.loop(0, steps)
    def _(step):
        start = pl.multiple_of(step * (STEP * ROWS), STEP * ROWS)
        add_block_grad(jnp.maximum(step - 1, 0))
        row_grad = None
        for n in range(4):
            cot = cotangent_ref[:, 128 * n:128 * (n + 1)]
            parts = []
            for j in range(STEP):
                scaling = (F32(2.0) * weight(step, j)) * cot
                at = pl.multiple_of(start + j * ROWS, ROWS)
                fields = fields_ref[pl.ds(at, ROWS), 256 * n:256 * (n + 1)]
                parts.append((jnp.concatenate([scaling, scaling], 1) * fields).astype(BF16))
            part = dot(jnp.concatenate(parts, 0), table_ref[INVERSE_T_AT + 256 * n:INVERSE_T_AT + 256 * (n + 1), :])
            row_grad = part if row_grad is None else row_grad + part
        row_field = row_field_ref[pl.ds(start, STEP * ROWS), :].astype(F32)
        terms = row_grad * row_field
        rounded = row_grad.astype(BF16)
        for j in range(STEP):
            terms_ref[pl.ds(step * STEP + j, 1), :] = jnp.sum(terms[j * ROWS:(j + 1) * ROWS], 0, keepdims=True)
            rounded_ref[:, 128 * j:128 * (j + 1)] = rounded[j * ROWS:(j + 1) * ROWS]

    add_block_grad(steps - 1)
    grads = grad_ref[...]
    out_ref[:FREQS] = grads[:FREQS] + halves_sign(FREQS, 1.0, -1.0) * pltpu.roll(grads[FREQS:], FREQS, 1)
    term = jnp.sum(terms_ref[...], 1, keepdims=True)
    row = lax.broadcasted_iota(jnp.int32, (SOURCES, 128), 0)
    lane = lax.broadcasted_iota(jnp.int32, (SOURCES, 128), 1)
    wanted = (row % GROUPS) * PER_GROUP + row // GROUPS
    term_row = jnp.sum(jnp.where(wanted == lane, term, F32(0)), 0, keepdims=True)
    lane = lax.broadcasted_iota(jnp.int32, (1, 128), 1)
    own = group_ref[0]
    for bit, width in ((1, PER_GROUP), (2, 2 * PER_GROUP)):
        swapped = jnp.where((lane // width) % 2 == 0, pltpu.roll(term_row, 128 - width, 1),
                            pltpu.roll(term_row, width, 1))
        term_row = jnp.where(jnp.bitwise_and(own, bit) != 0, swapped, term_row)
    term_row = jnp.where(lane < SOURCES, term_row, F32(0))
    out_ref[FREQS:] = jnp.broadcast_to(jnp.where(lane == SOURCES, error_sum, term_row), (8, 128))


def image(group, scalars, own, near, other, target, table):
    fixed = lambda i, g: (0, 0)
    whole = lambda shape: pl.BlockSpec(shape, fixed)
    return pl.pallas_call(
        image_kernel,
        grid_spec=pltpu.PrefetchScalarGridSpec(
            num_scalar_prefetch=1,
            grid=(1,),
            in_specs=[
                *[pl.BlockSpec(memory_space=pltpu.SMEM)] * GROUPS,
                whole((TILE_ROWS, 128)), whole((MARGIN, 128)), whole((MARGIN, 128)),
                pl.BlockSpec((ROWS, COLS), lambda i, g: (g[0], 0)),
                whole(IMAGE_TABLE.shape),
            ],
            out_specs=whole((FREQS + 8, 128)),
            scratch_shapes=[
                pltpu.VMEM((SOURCES * ROWS, 2 * COLS), F32),
                pltpu.VMEM((SOURCES * ROWS, 128), BF16),
                pltpu.VMEM((ROWS, COLS), F32),
                pltpu.VMEM((ROWS, COLS), F32),
                pltpu.VMEM((128, 128), F32),
                pltpu.VMEM((SOURCES, 128), F32),
                pltpu.VMEM((128, 128), F32),
                pltpu.VMEM((ROWS, STEP * 128), BF16),
                pltpu.VMEM((FRAME, 128), BF16),
            ],
        ),
        out_shape=jax.ShapeDtypeStruct((FREQS + 8, 128), F32),
        compiler_params=pltpu.CompilerParams(vmem_limit_bytes=44 * MIB),
        name="image",
    )(group, *scalars, own, near, other, target, table)


def total_kernel(chip_ref, far_ref, grad_ref, sums_ref):
    grad_ref[...] = chip_ref[:FREQS] + far_ref[:FREQS]
    row = chip_ref[FREQS:FREQS + 1] + far_ref[FREQS:FREQS + 1]
    sums_ref[...] = jnp.broadcast_to(row[None], sums_ref.shape)


def total(chip, far, peers):
    return pl.pallas_call(
        total_kernel,
        out_shape=[jax.ShapeDtypeStruct((FREQS, 128), F32), jax.ShapeDtypeStruct((peers, 1, 128), F32)],
        compiler_params=pltpu.CompilerParams(vmem_limit_bytes=1 * MIB),
        name="total",
    )(chip, far)


def split_dot(table, x):
    high = x.astype(BF16)
    low = (x - high.astype(F32)).astype(BF16)
    return dot(jnp.concatenate([table, table], 1), jnp.concatenate([high, low], 0))


def dot_split(x, table):
    high = x.astype(BF16)
    low = (x - high.astype(F32)).astype(BF16)
    return dot(jnp.concatenate([high, low], 1), jnp.concatenate([table, table], 0))


def product_gradient(spectrum_grad):
    lower = pltpu.roll(spectrum_grad, FREQS, 1) * halves_sign(FREQS, 1.0, -1.0)
    return jnp.concatenate([spectrum_grad, lower], 0)


def owned_kernel(grad_ref, logits_ref, row_ref, column_ref, out_ref, edges_ref, slope_ref):
    column_grad = split_dot(row_ref[...], product_gradient(grad_ref[...]))
    opening = jax.nn.sigmoid(logits_ref[...])
    slope = opening * (F32(1.0) - opening)
    out = dot_split(column_grad, column_ref[...]) * slope
    out_ref[...] = out
    edges_ref[:MARGIN] = out[:MARGIN]
    edges_ref[MARGIN:] = out[TILE_ROWS - MARGIN:]
    slope_ref[:MARGIN] = slope[:MARGIN]
    slope_ref[MARGIN:] = slope[TILE_ROWS - MARGIN:]


def owned_gradient(spectrum_grad, mask_logits):
    return pl.pallas_call(
        owned_kernel,
        out_shape=[jax.ShapeDtypeStruct((n, COLS), F32) for n in (TILE_ROWS, 2 * MARGIN, 2 * MARGIN)],
        compiler_params=pltpu.CompilerParams(vmem_limit_bytes=10 * MIB),
        name="owned_gradient",
    )(spectrum_grad, mask_logits,
      jnp.asarray(np.ascontiguousarray(ROW_FORWARD.T[MARGIN:MARGIN + TILE_ROWS])),
      jnp.asarray(np.ascontiguousarray(COLUMN_FORWARD.T)))


def last_kernel(group_ref, near_ref, other_ref, edges_ref, slope_ref, row_ref, column_ref, sums_ref,
                packed_ref, grad_ref, out_ref, weight_grad_ref, loss_ref,
                rows_ref, semaphores, *, pixels):
    del grad_ref
    even = group_ref[0] % 2 == 0
    before = jnp.where(even, near_ref[...], other_ref[...])
    after = jnp.where(even, other_ref[...], near_ref[...])
    column_grad = jnp.concatenate([split_dot(row_ref[:MARGIN], product_gradient(before)),
                                   split_dot(row_ref[MARGIN:], product_gradient(after))], 0)
    rows_ref[...] = edges_ref[...] + dot_split(column_grad, column_ref[...]) * slope_ref[...]
    copies = [
        pltpu.make_async_copy(rows_ref.at[pl.ds(0, MARGIN), :], out_ref.at[pl.ds(0, MARGIN), :], semaphores.at[0]),
        pltpu.make_async_copy(rows_ref.at[pl.ds(MARGIN, MARGIN), :],
                              out_ref.at[pl.ds(TILE_ROWS - MARGIN, MARGIN), :], semaphores.at[1]),
    ]
    for copy in copies:
        copy.start()
    total = jnp.sum(sums_ref[...], 0)
    row = total
    for bit, width in ((1, PER_GROUP), (2, 2 * PER_GROUP)):
        row = jnp.where(jnp.bitwise_and(group_ref[0], bit) != 0, pltpu.roll(row, 128 - width, 1), row)
    weight_grad_ref[...] = row[:, :PER_GROUP] / (F32(2.0) * packed_ref[0:1]) / F32(pixels)
    loss_ref[...] = total[:, SOURCES:SOURCES + 1] / F32(pixels)
    for copy in copies:
        copy.wait()


def last_steps(group, near, other, edges, slope, grad, sums, packed, pixels):
    rows = np.concatenate([ROW_FORWARD.T[MARGIN + TILE_ROWS:], ROW_FORWARD.T[:MARGIN]], 0)
    block = pl.BlockSpec()
    hbm = pl.BlockSpec(memory_space=pltpu.HBM)
    return pl.pallas_call(
        functools.partial(last_kernel, pixels=pixels),
        in_specs=[pl.BlockSpec(memory_space=pltpu.SMEM)] + [block] * 8 + [hbm],
        out_specs=[hbm, block, block],
        out_shape=[jax.ShapeDtypeStruct((TILE_ROWS, COLS), F32), jax.ShapeDtypeStruct((1, PER_GROUP), F32),
                   jax.ShapeDtypeStruct((1, 1), F32)],
        scratch_shapes=[pltpu.VMEM((2 * MARGIN, COLS), F32), pltpu.SemaphoreType.DMA((2,))],
        input_output_aliases={9: 0},
        compiler_params=pltpu.CompilerParams(vmem_limit_bytes=4 * MIB),
        name="last_steps",
    )(group, near, other, edges, slope, jnp.asarray(np.ascontiguousarray(rows)),
      jnp.asarray(np.ascontiguousarray(COLUMN_FORWARD.T)), sums, packed, grad)


def from_tile_beside(x):
    peers = lax.axis_size("tile")
    pairs = [(s * peers + i, s * peers + j) for s in range(GROUPS) for i in range(peers)
             for j in [i + 1 - 2 * (s % 2)] if 0 <= j < peers]
    return lax.ppermute(x, ("src", "tile"), pairs)


def from_group(x, d):
    return lax.ppermute(x, "src", [(i, i ^ d) for i in range(GROUPS)])


def from_core(x):
    return from_group(x, 1)


def from_chip(x):
    return from_group(x, 2)


def on_device(mask_logits, target, weights, shifts):
    peers = lax.axis_size("tile")
    group = lax.axis_index("src").astype(jnp.int32).reshape(1)
    edge, packed = edge_spectrum(group, mask_logits, weights, shifts)
    near = from_tile_beside(edge)
    packed_far = from_chip(packed)
    packed_core = from_core(packed)
    own, table = column_spectrum(mask_logits)
    near, packed_far, own = lax.optimization_barrier((near, packed_far, own))
    scalars = [packed, packed_core, packed_far, from_core(packed_far)]
    partial = image(group, scalars, own, near, from_core(near), target, table)
    chip = partial + from_core(partial)
    spectrum_grad, sums = total(chip, from_chip(chip), peers)
    near_grad = from_tile_beside(spectrum_grad)
    sums = lax.all_to_all(sums, "tile", 0, 0, tiled=True)
    grad, edges, slope = owned_gradient(spectrum_grad, mask_logits)
    near_grad, edges = lax.optimization_barrier((near_grad, edges))
    mask_grad, weight_grad, loss = last_steps(
        group, near_grad, from_core(near_grad), edges, slope, grad, sums, packed, TILE_ROWS * COLS * peers)
    return mask_grad, weight_grad.reshape(PER_GROUP), loss.reshape(())


def solution(mesh):
    placed = (P("tile", None), P("tile", None), P("src"), P("src", None))
    return jax.shard_map(
        on_device,
        mesh=mesh,
        in_specs=placed,
        out_specs=(P("tile", None), P("src"), P()),
        check_vma=False,
    )
```

```python
import functools

import numpy as np
import jax
import jax.numpy as jnp
from jax import lax
from jax.experimental import pallas as pl
from jax.experimental.pallas import tpu as pltpu
from jax.sharding import PartitionSpec as P

FREQS = 64
RADIUS = 20
MARGIN = 64
COLS = 512
TILE_ROWS = 512
FRAME = 640
SOURCES = 64
GROUPS = 4
PER_GROUP = SOURCES // GROUPS
ROWS = TILE_ROWS // GROUPS
MIB = 1024 * 1024
STEEPNESS = 12.0
THRESHOLD = 0.2
STEP = 16
F32 = jnp.float32
BF16 = jnp.bfloat16


def angles(length_used, offset, period):
    position = np.arange(length_used, dtype=np.int32)[:, None] + offset
    frequency = np.arange(FREQS, dtype=np.int32)[None, :] - FREQS // 2
    cycles = np.mod(position * frequency, period).astype(np.float32)
    angle_value = (cycles * np.float32(2.0 * 3.141592653589793 / period)).astype(np.float64)
    return np.cos(angle_value).astype(np.float32), np.sin(angle_value).astype(np.float32)


def make_tables():
    column_cosine, column_sine = angles(COLS, 0, COLS)
    column_forward = np.concatenate([column_cosine, -column_sine], 1)
    frame_cosine, frame_sine = angles(FRAME, 0, FRAME)
    row_forward = np.concatenate([frame_cosine.T, -frame_sine.T], 0)
    owned_cosine, owned_sine = angles(TILE_ROWS, MARGIN, FRAME)
    row_inverse = np.concatenate([owned_cosine, owned_sine], 1) / np.float32(FRAME)
    cosine_scaled = column_cosine.T / np.float32(COLS)
    sine_scaled = column_sine.T / np.float32(COLS)
    upper_block = np.concatenate([cosine_scaled, sine_scaled], 1)
    lower_block = np.concatenate([-sine_scaled, cosine_scaled], 1)
    column_inverse = np.concatenate([upper_block, lower_block], 0)
    chunked = column_inverse.reshape(2 * FREQS, 2, COLS // 128, 128).transpose(0, 2, 1, 3)
    chunked = chunked.reshape(2 * FREQS, 2 * COLS)
    rounded = lambda a: np.ascontiguousarray(a).astype(BF16)
    return [rounded(a) for a in (column_forward, row_forward, row_inverse, chunked)]


COLUMN_FORWARD, ROW_FORWARD, ROW_INVERSE, COLUMN_INVERSE = make_tables()


def stacked(table):
    return np.concatenate([table[:, c:c + 128] for c in range(0, table.shape[1], 128)], 0)


PARTS = [ROW_INVERSE, stacked(ROW_INVERSE.T), COLUMN_INVERSE.T, stacked(COLUMN_INVERSE), stacked(ROW_FORWARD)]
IMAGE_TABLE = np.ascontiguousarray(np.concatenate(PARTS, 0))
INVERSE_T_AT = 2 * TILE_ROWS
INVERSE_AT = INVERSE_T_AT + 2 * COLS
FORWARD_AT = INVERSE_AT + 8 * 128


def dot(a, b):
    return jnp.dot(a, b, preferred_element_type=F32)


def halves_sign(rows, left, right):
    lane = lax.broadcasted_iota(jnp.int32, (rows, 128), 1)
    return jnp.where(lane < FREQS, F32(left), F32(right))


def edge_kernel(group_ref, logits_ref, table_ref, weights_ref, shifts_ref, edge_out, packed_out,
                rows, table, weights, shifts, semaphores):
    start = jnp.where(group_ref[0] % 2 == 0, TILE_ROWS - MARGIN, 0)
    rows_from = logits_ref.at[pl.ds(pl.multiple_of(start, MARGIN), MARGIN), :]
    pairs = ((rows_from, rows), (table_ref, table), (weights_ref, weights), (shifts_ref, shifts))
    copies = [pltpu.make_async_copy(a, b, semaphores.at[i]) for i, (a, b) in enumerate(pairs)]
    for copy in copies:
        copy.start()
    for copy in copies:
        copy.wait()
    edge_out[...] = dot(jax.nn.sigmoid(rows[...]).astype(BF16), table[...]).astype(BF16)
    packed_out[0:1] = weights[...]
    packed_out[1:3] = shifts[...].astype(F32)


def edge_spectrum(group, mask_logits, weights, shifts):
    return pl.pallas_call(
        edge_kernel,
        in_specs=[pl.BlockSpec(memory_space=pltpu.SMEM)] + [pl.BlockSpec(memory_space=pltpu.HBM)] * 4,
        out_shape=[jax.ShapeDtypeStruct((MARGIN, 128), BF16), jax.ShapeDtypeStruct((3, PER_GROUP), F32)],
        scratch_shapes=[
            pltpu.VMEM((MARGIN, COLS), F32), pltpu.VMEM((COLS, 128), BF16),
            pltpu.VMEM((1, PER_GROUP), F32), pltpu.VMEM((2, PER_GROUP), jnp.int32),
            pltpu.SemaphoreType.DMA((4,)),
        ],
        compiler_params=pltpu.CompilerParams(vmem_limit_bytes=60 * MIB),
        name="edge_spectrum",
    )(group, mask_logits, jnp.asarray(COLUMN_FORWARD), weights.reshape(1, PER_GROUP), shifts.T)


def column_kernel(logits_ref, table_ref, image_table_ref, out_ref, image_table_out, semaphore):
    copy = pltpu.make_async_copy(image_table_ref, image_table_out, semaphore)
    copy.start()
    out_ref[...] = dot(jax.nn.sigmoid(logits_ref[...]).astype(BF16), table_ref[...]).astype(BF16)
    copy.wait()


def column_spectrum(mask_logits):
    return pl.pallas_call(
        column_kernel,
        in_specs=[pl.BlockSpec(), pl.BlockSpec(), pl.BlockSpec(memory_space=pltpu.HBM)],
        out_shape=[jax.ShapeDtypeStruct((TILE_ROWS, 128), BF16), jax.ShapeDtypeStruct(IMAGE_TABLE.shape, BF16)],
        scratch_shapes=[pltpu.SemaphoreType.DMA],
        compiler_params=pltpu.CompilerParams(vmem_limit_bytes=8 * MIB),
        name="column_spectrum",
    )(mask_logits, jnp.asarray(COLUMN_FORWARD), jnp.asarray(IMAGE_TABLE))


def pupil(scalars, step, j):
    ref, i = scalars[j % GROUPS], step * (STEP // GROUPS) + j // GROUPS
    across, along = ref[1, i], ref[2, i]
    row = lax.broadcasted_iota(jnp.int32, (FREQS, 128), 0) - FREQS // 2
    lane = jnp.bitwise_and(lax.broadcasted_iota(jnp.int32, (FREQS, 128), 1), FREQS - 1) - FREQS // 2
    row, lane = row.astype(F32) - across, lane.astype(F32) - along
    return row * row + lane * lane <= F32(RADIUS * RADIUS)


def image_kernel(group_ref, own_scalars, scalars_1, scalars_2, scalars_3, own_ref, near_ref, other_ref, target_ref, table_ref, out_ref,
                 fields_ref, row_field_ref, intensity_ref, cotangent_ref, spectra_ref, terms_ref, grad_ref, rounded_ref, frame_ref):
    scalars = [own_scalars, scalars_1, scalars_2, scalars_3]
    def beside(start, count):
        return jnp.concatenate([table_ref[start + 128 * i:start + 128 * (i + 1), :] for i in range(count)], 1)

    row_inverse = table_ref.at[pl.ds(pl.multiple_of(group_ref[0] * ROWS, ROWS), ROWS), :]
    row_inverse_t = table_ref.at[pl.ds(pl.multiple_of(TILE_ROWS + group_ref[0] * 128, 128), 128), :]
    even = group_ref[0] % 2 == 0
    frame_ref[MARGIN:MARGIN + TILE_ROWS] = own_ref[...]

    @pl.when(even)
    def _():
        frame_ref[:MARGIN] = near_ref[...]
        frame_ref[MARGIN + TILE_ROWS:] = other_ref[...]

    @pl.when(jnp.logical_not(even))
    def _():
        frame_ref[:MARGIN] = other_ref[...]
        frame_ref[MARGIN + TILE_ROWS:] = near_ref[...]

    product = dot(beside(FORWARD_AT, FRAME // 128), frame_ref[...])
    swapped = pltpu.roll(product[FREQS:], FREQS, 1)
    spectrum = (product[:FREQS] + halves_sign(FREQS, -1.0, 1.0) * swapped).astype(BF16).astype(F32)
    spectra_ref[:FREQS] = spectrum
    spectra_ref[FREQS:] = pltpu.roll(spectrum, FREQS, 1) * halves_sign(FREQS, -1.0, 1.0)
    intensity_ref[...] = jnp.zeros_like(intensity_ref)

    steps = SOURCES // STEP

    def image_rows(step):
        blocks = []
        for j in range(STEP):
            inside = pupil(scalars, step, j)
            inside = jnp.concatenate([inside, inside], 0)
            blocks.append(jnp.where(inside, spectra_ref[...], F32(0)).astype(BF16))
        row_field = dot(row_inverse[...], jnp.concatenate(blocks, 1)).astype(BF16)
        for j in range(STEP):
            start = pl.multiple_of((step * STEP + j) * ROWS, ROWS)
            row_field_ref[pl.ds(start, ROWS), :] = row_field[:, 128 * j:128 * (j + 1)]

    def weight(step, j):
        return scalars[j % GROUPS][0, step * (STEP // GROUPS) + j // GROUPS]

    image_rows(0)

    @pl.loop(0, steps)
    def _(step):
        start = pl.multiple_of(step * (STEP * ROWS), STEP * ROWS)
        row_field = row_field_ref[pl.ds(start, STEP * ROWS), :]
        for n in range(4):
            fields = dot(row_field, beside(INVERSE_AT + 256 * n, 2))
            fields_ref[pl.ds(start, STEP * ROWS), 256 * n:256 * (n + 1)] = fields
            power = fields[:, :128] * fields[:, :128] + fields[:, 128:] * fields[:, 128:]
            total = weight(step, 0) * power[:ROWS]
            for j in range(1, STEP):
                total = total + weight(step, j) * power[j * ROWS:(j + 1) * ROWS]
            intensity_ref[:, 128 * n:128 * (n + 1)] += total
        image_rows(jnp.minimum(step + 1, steps - 1))

    printed = jax.nn.sigmoid(F32(STEEPNESS) * (intensity_ref[...] - F32(THRESHOLD)))
    error_value = printed - target_ref[...].astype(F32)
    cotangent_ref[...] = F32(2.0 * STEEPNESS) * error_value * printed * (F32(1.0) - printed)
    error_rows = jnp.sum(error_value * error_value, 0, keepdims=True)
    error_lanes = (error_rows[:, :128] + error_rows[:, 128:256]) + (error_rows[:, 256:384] + error_rows[:, 384:])
    error_sum = jnp.sum(error_lanes, 1, keepdims=True)
    grad_ref[...] = jnp.zeros_like(grad_ref)

    rounded_ref[...] = jnp.zeros_like(rounded_ref)

    def add_block_grad(step):
        block_grad = dot(row_inverse_t[...], rounded_ref[...])
        total = jnp.zeros((2 * FREQS, 128), F32)
        for j in range(STEP):
            inside = pupil(scalars, step, j)
            inside = jnp.concatenate([inside, inside], 0)
            total = total + jnp.where(inside, block_grad[:, 128 * j:128 * (j + 1)], F32(0))
        grad_ref[...] += total

    @pl.loop(0, steps)
    def _(step):
        start = pl.multiple_of(step * (STEP * ROWS), STEP * ROWS)
        add_block_grad(jnp.maximum(step - 1, 0))
        row_grad = None
        for n in range(4):
            cot = cotangent_ref[:, 128 * n:128 * (n + 1)]
            parts = []
            for j in range(STEP):
                scaling = (F32(2.0) * weight(step, j)) * cot
                at = pl.multiple_of(start + j * ROWS, ROWS)
                fields = fields_ref[pl.ds(at, ROWS), 256 * n:256 * (n + 1)]
                parts.append((jnp.concatenate([scaling, scaling], 1) * fields).astype(BF16))
            part = dot(jnp.concatenate(parts, 0), table_ref[INVERSE_T_AT + 256 * n:INVERSE_T_AT + 256 * (n + 1), :])
            row_grad = part if row_grad is None else row_grad + part
        row_field = row_field_ref[pl.ds(start, STEP * ROWS), :].astype(F32)
        terms = row_grad * row_field
        rounded = row_grad.astype(BF16)
        for j in range(STEP):
            terms_ref[pl.ds(step * STEP + j, 1), :] = jnp.sum(terms[j * ROWS:(j + 1) * ROWS], 0, keepdims=True)
            rounded_ref[:, 128 * j:128 * (j + 1)] = rounded[j * ROWS:(j + 1) * ROWS]

    add_block_grad(steps - 1)
    grads = grad_ref[...]
    out_ref[:FREQS] = grads[:FREQS] + halves_sign(FREQS, 1.0, -1.0) * pltpu.roll(grads[FREQS:], FREQS, 1)
    term = jnp.sum(terms_ref[...], 1, keepdims=True)
    row = lax.broadcasted_iota(jnp.int32, (SOURCES, 128), 0)
    lane = lax.broadcasted_iota(jnp.int32, (SOURCES, 128), 1)
    wanted = (row % GROUPS) * PER_GROUP + row // GROUPS
    term_row = jnp.sum(jnp.where(wanted == lane, term, F32(0)), 0, keepdims=True)
    lane = lax.broadcasted_iota(jnp.int32, (1, 128), 1)
    own = group_ref[0]
    for bit, width in ((1, PER_GROUP), (2, 2 * PER_GROUP)):
        swapped = jnp.where((lane // width) % 2 == 0, pltpu.roll(term_row, 128 - width, 1),
                            pltpu.roll(term_row, width, 1))
        term_row = jnp.where(jnp.bitwise_and(own, bit) != 0, swapped, term_row)
    term_row = jnp.where(lane < SOURCES, term_row, F32(0))
    out_ref[FREQS:] = jnp.broadcast_to(jnp.where(lane == SOURCES, error_sum, term_row), (8, 128))


def image(group, scalars, own, near, other, target, table):
    fixed = lambda i, g: (0, 0)
    whole = lambda shape: pl.BlockSpec(shape, fixed)
    return pl.pallas_call(
        image_kernel,
        grid_spec=pltpu.PrefetchScalarGridSpec(
            num_scalar_prefetch=1,
            grid=(1,),
            in_specs=[
                *[pl.BlockSpec(memory_space=pltpu.SMEM)] * GROUPS,
                whole((TILE_ROWS, 128)), whole((MARGIN, 128)), whole((MARGIN, 128)),
                pl.BlockSpec((ROWS, COLS), lambda i, g: (g[0], 0)),
                whole(IMAGE_TABLE.shape),
            ],
            out_specs=whole((FREQS + 8, 128)),
            scratch_shapes=[
                pltpu.VMEM((SOURCES * ROWS, 2 * COLS), F32),
                pltpu.VMEM((SOURCES * ROWS, 128), BF16),
                pltpu.VMEM((ROWS, COLS), F32),
                pltpu.VMEM((ROWS, COLS), F32),
                pltpu.VMEM((128, 128), F32),
                pltpu.VMEM((SOURCES, 128), F32),
                pltpu.VMEM((128, 128), F32),
                pltpu.VMEM((ROWS, STEP * 128), BF16),
                pltpu.VMEM((FRAME, 128), BF16),
            ],
        ),
        out_shape=jax.ShapeDtypeStruct((FREQS + 8, 128), F32),
        compiler_params=pltpu.CompilerParams(vmem_limit_bytes=44 * MIB),
        name="image",
    )(group, *scalars, own, near, other, target, table)


def total_kernel(chip_ref, far_ref, grad_ref, sums_ref):
    grad_ref[...] = chip_ref[:FREQS] + far_ref[:FREQS]
    row = chip_ref[FREQS:FREQS + 1] + far_ref[FREQS:FREQS + 1]
    sums_ref[...] = jnp.broadcast_to(row[None], sums_ref.shape)


def total(chip, far, peers):
    return pl.pallas_call(
        total_kernel,
        out_shape=[jax.ShapeDtypeStruct((FREQS, 128), F32), jax.ShapeDtypeStruct((peers, 1, 128), F32)],
        compiler_params=pltpu.CompilerParams(vmem_limit_bytes=1 * MIB),
        name="total",
    )(chip, far)


def split_dot(table, x):
    high = x.astype(BF16)
    low = (x - high.astype(F32)).astype(BF16)
    return dot(jnp.concatenate([table, table], 1), jnp.concatenate([high, low], 0))


def dot_split(x, table):
    high = x.astype(BF16)
    low = (x - high.astype(F32)).astype(BF16)
    return dot(jnp.concatenate([high, low], 1), jnp.concatenate([table, table], 0))


def product_gradient(spectrum_grad):
    lower = pltpu.roll(spectrum_grad, FREQS, 1) * halves_sign(FREQS, 1.0, -1.0)
    return jnp.concatenate([spectrum_grad, lower], 0)


def owned_kernel(grad_ref, logits_ref, row_ref, column_ref, out_ref, edges_ref, slope_ref):
    column_grad = split_dot(row_ref[...], product_gradient(grad_ref[...]))
    opening = jax.nn.sigmoid(logits_ref[...])
    slope = opening * (F32(1.0) - opening)
    out = dot_split(column_grad, column_ref[...]) * slope
    out_ref[...] = out
    edges_ref[:MARGIN] = out[:MARGIN]
    edges_ref[MARGIN:] = out[TILE_ROWS - MARGIN:]
    slope_ref[:MARGIN] = slope[:MARGIN]
    slope_ref[MARGIN:] = slope[TILE_ROWS - MARGIN:]


def owned_gradient(spectrum_grad, mask_logits):
    return pl.pallas_call(
        owned_kernel,
        out_shape=[jax.ShapeDtypeStruct((n, COLS), F32) for n in (TILE_ROWS, 2 * MARGIN, 2 * MARGIN)],
        compiler_params=pltpu.CompilerParams(vmem_limit_bytes=10 * MIB),
        name="owned_gradient",
    )(spectrum_grad, mask_logits,
      jnp.asarray(np.ascontiguousarray(ROW_FORWARD.T[MARGIN:MARGIN + TILE_ROWS])),
      jnp.asarray(np.ascontiguousarray(COLUMN_FORWARD.T)))


def last_kernel(group_ref, near_ref, other_ref, edges_ref, slope_ref, row_ref, column_ref, sums_ref,
                packed_ref, grad_ref, out_ref, weight_grad_ref, loss_ref,
                rows_ref, semaphores, *, pixels):
    del grad_ref
    even = group_ref[0] % 2 == 0
    before = jnp.where(even, near_ref[...], other_ref[...])
    after = jnp.where(even, other_ref[...], near_ref[...])
    column_grad = jnp.concatenate([split_dot(row_ref[:MARGIN], product_gradient(before)),
                                   split_dot(row_ref[MARGIN:], product_gradient(after))], 0)
    rows_ref[...] = edges_ref[...] + dot_split(column_grad, column_ref[...]) * slope_ref[...]
    copies = [
        pltpu.make_async_copy(rows_ref.at[pl.ds(0, MARGIN), :], out_ref.at[pl.ds(0, MARGIN), :], semaphores.at[0]),
        pltpu.make_async_copy(rows_ref.at[pl.ds(MARGIN, MARGIN), :],
                              out_ref.at[pl.ds(TILE_ROWS - MARGIN, MARGIN), :], semaphores.at[1]),
    ]
    for copy in copies:
        copy.start()
    total = jnp.sum(sums_ref[...], 0)
    row = total
    for bit, width in ((1, PER_GROUP), (2, 2 * PER_GROUP)):
        row = jnp.where(jnp.bitwise_and(group_ref[0], bit) != 0, pltpu.roll(row, 128 - width, 1), row)
    weight_grad_ref[...] = row[:, :PER_GROUP] / (F32(2.0) * packed_ref[0:1]) / F32(pixels)
    loss_ref[...] = total[:, SOURCES:SOURCES + 1] / F32(pixels)
    for copy in copies:
        copy.wait()


def last_steps(group, near, other, edges, slope, grad, sums, packed, pixels):
    rows = np.concatenate([ROW_FORWARD.T[MARGIN + TILE_ROWS:], ROW_FORWARD.T[:MARGIN]], 0)
    block = pl.BlockSpec()
    hbm = pl.BlockSpec(memory_space=pltpu.HBM)
    return pl.pallas_call(
        functools.partial(last_kernel, pixels=pixels),
        in_specs=[pl.BlockSpec(memory_space=pltpu.SMEM)] + [block] * 8 + [hbm],
        out_specs=[hbm, block, block],
        out_shape=[jax.ShapeDtypeStruct((TILE_ROWS, COLS), F32), jax.ShapeDtypeStruct((1, PER_GROUP), F32),
                   jax.ShapeDtypeStruct((1, 1), F32)],
        scratch_shapes=[pltpu.VMEM((2 * MARGIN, COLS), F32), pltpu.SemaphoreType.DMA((2,))],
        input_output_aliases={9: 0},
        compiler_params=pltpu.CompilerParams(vmem_limit_bytes=4 * MIB),
        name="last_steps",
    )(group, near, other, edges, slope, jnp.asarray(np.ascontiguousarray(rows)),
      jnp.asarray(np.ascontiguousarray(COLUMN_FORWARD.T)), sums, packed, grad)


def from_tile_beside(x):
    peers = lax.axis_size("tile")
    plane = peers // 4
    pairs = []
    for group in range(GROUPS):
        for i in range(peers):
            j = i + 1 - 2 * (group % 2)
            if 0 <= j < peers:
                other = group if i // plane == j // plane else group ^ 2
                pairs.append((group * peers + i, other * peers + j))
    return lax.ppermute(x, ("src", "tile"), pairs)


def from_group(x, d):
    return lax.ppermute(x, "src", [(i, i ^ d) for i in range(GROUPS)])


def from_core(x):
    return from_group(x, 1)


def from_chip(x):
    return from_group(x, 2)


def on_device(mask_logits, target, weights, shifts):
    peers = lax.axis_size("tile")
    group = lax.axis_index("src").astype(jnp.int32).reshape(1)
    edge, packed = edge_spectrum(group, mask_logits, weights, shifts)
    near = from_tile_beside(edge)
    packed_far = from_chip(packed)
    packed_core = from_core(packed)
    own, table = column_spectrum(mask_logits)
    near, packed_far, own = lax.optimization_barrier((near, packed_far, own))
    scalars = [packed, packed_core, packed_far, from_core(packed_far)]
    partial = image(group, scalars, own, near, from_core(near), target, table)
    chip = partial + from_core(partial)
    spectrum_grad, sums = total(chip, from_chip(chip), peers)
    near_grad = from_tile_beside(spectrum_grad)
    sums = lax.all_to_all(sums, "tile", 0, 0, tiled=True)
    grad, edges, slope = owned_gradient(spectrum_grad, mask_logits)
    near_grad, edges = lax.optimization_barrier((near_grad, edges))
    mask_grad, weight_grad, loss = last_steps(
        group, near_grad, from_core(near_grad), edges, slope, grad, sums, packed, TILE_ROWS * COLS * peers)
    return mask_grad, weight_grad.reshape(PER_GROUP), loss.reshape(())


def solution(mesh):
    placed = (P("tile", None), P("tile", None), P("src"), P("src", None))
    return jax.shard_map(
        on_device,
        mesh=mesh,
        in_specs=placed,
        out_specs=(P("tile", None), P("src"), P()),
        check_vma=False,
    )
```

```python
import functools

import numpy as np
import jax
import jax.numpy as jnp
from jax import lax
from jax.experimental import pallas as pl
from jax.experimental.pallas import tpu as pltpu
from jax.sharding import PartitionSpec as P


FREQS = 64
RADIUS = 20
MARGIN = 64
COLS = 512
TILE_ROWS = 512
FRAME = 640
SOURCES = 64
GROUPS = 4
PER_GROUP = SOURCES // GROUPS
ROWS = TILE_ROWS // GROUPS
MIB = 1024 * 1024
STEEPNESS = 12.0
THRESHOLD = 0.2
STEP = 16
F32 = jnp.float32
BF16 = jnp.bfloat16


def angles(length_used, offset, period):
    position = np.arange(length_used, dtype=np.int32)[:, None] + offset
    frequency = np.arange(FREQS, dtype=np.int32)[None, :] - FREQS // 2
    cycles = np.mod(position * frequency, period).astype(np.float32)
    angle_value = (cycles * np.float32(2.0 * 3.141592653589793 / period)).astype(np.float64)
    return np.cos(angle_value).astype(np.float32), np.sin(angle_value).astype(np.float32)


def make_tables():
    column_cosine, column_sine = angles(COLS, 0, COLS)
    column_forward = np.concatenate([column_cosine, -column_sine], 1)
    frame_cosine, frame_sine = angles(FRAME, 0, FRAME)
    row_forward = np.concatenate([frame_cosine.T, -frame_sine.T], 0)
    owned_cosine, owned_sine = angles(TILE_ROWS, MARGIN, FRAME)
    row_inverse = np.concatenate([owned_cosine, owned_sine], 1) / np.float32(FRAME)
    cosine_scaled = column_cosine.T / np.float32(COLS)
    sine_scaled = column_sine.T / np.float32(COLS)
    upper_block = np.concatenate([cosine_scaled, sine_scaled], 1)
    lower_block = np.concatenate([-sine_scaled, cosine_scaled], 1)
    column_inverse = np.concatenate([upper_block, lower_block], 0)
    chunked = column_inverse.reshape(2 * FREQS, 2, COLS // 128, 128).transpose(0, 2, 1, 3)
    chunked = chunked.reshape(2 * FREQS, 2 * COLS)
    rounded = lambda a: np.ascontiguousarray(a).astype(BF16)
    return [rounded(a) for a in (column_forward, row_forward, row_inverse, chunked)]


COLUMN_FORWARD, ROW_FORWARD, ROW_INVERSE, COLUMN_INVERSE = make_tables()


def stacked(table):
    return np.concatenate([table[:, c:c + 128] for c in range(0, table.shape[1], 128)], 0)


PARTS = [ROW_INVERSE, stacked(ROW_INVERSE.T), COLUMN_INVERSE.T, stacked(COLUMN_INVERSE), stacked(ROW_FORWARD)]
IMAGE_TABLE = np.ascontiguousarray(np.concatenate(PARTS, 0))
INVERSE_T_AT = 2 * TILE_ROWS
INVERSE_AT = INVERSE_T_AT + 2 * COLS
FORWARD_AT = INVERSE_AT + 8 * 128


def dot(a, b):
    return jnp.dot(a, b, preferred_element_type=F32)


def halves_sign(rows, left, right):
    lane = lax.broadcasted_iota(jnp.int32, (rows, 128), 1)
    return jnp.where(lane < FREQS, F32(left), F32(right))


def edge_kernel(group_ref, logits_ref, table_ref, weights_ref, shifts_ref, edge_out, packed_out,
                rows, table, weights, shifts, semaphores):
    start = jnp.where(group_ref[0] % 2 == 0, TILE_ROWS - MARGIN, 0)
    rows_from = logits_ref.at[pl.ds(pl.multiple_of(start, MARGIN), MARGIN), :]
    pairs = ((rows_from, rows), (table_ref, table), (weights_ref, weights), (shifts_ref, shifts))
    copies = [pltpu.make_async_copy(a, b, semaphores.at[i]) for i, (a, b) in enumerate(pairs)]
    for copy in copies:
        copy.start()
    for copy in copies:
        copy.wait()
    edge_out[...] = dot(jax.nn.sigmoid(rows[...]).astype(BF16), table[...]).astype(BF16)
    packed_out[0:1] = weights[...]
    packed_out[1:3] = shifts[...].astype(F32)


def edge_spectrum(group, mask_logits, weights, shifts):
    return pl.pallas_call(
        edge_kernel,
        in_specs=[pl.BlockSpec(memory_space=pltpu.SMEM)] + [pl.BlockSpec(memory_space=pltpu.HBM)] * 4,
        out_shape=[jax.ShapeDtypeStruct((MARGIN, 128), BF16), jax.ShapeDtypeStruct((3, PER_GROUP), F32)],
        scratch_shapes=[
            pltpu.VMEM((MARGIN, COLS), F32), pltpu.VMEM((COLS, 128), BF16),
            pltpu.VMEM((1, PER_GROUP), F32), pltpu.VMEM((2, PER_GROUP), jnp.int32),
            pltpu.SemaphoreType.DMA((4,)),
        ],
        compiler_params=pltpu.CompilerParams(vmem_limit_bytes=60 * MIB),
        name="edge_spectrum",
    )(group, mask_logits, jnp.asarray(COLUMN_FORWARD), weights.reshape(1, PER_GROUP), shifts.T)


def column_kernel(logits_ref, table_ref, image_table_ref, out_ref, image_table_out, semaphore):
    copy = pltpu.make_async_copy(image_table_ref, image_table_out, semaphore)
    copy.start()
    out_ref[...] = dot(jax.nn.sigmoid(logits_ref[...]).astype(BF16), table_ref[...]).astype(BF16)
    copy.wait()


def column_spectrum(mask_logits):
    return pl.pallas_call(
        column_kernel,
        in_specs=[pl.BlockSpec(), pl.BlockSpec(), pl.BlockSpec(memory_space=pltpu.HBM)],
        out_shape=[jax.ShapeDtypeStruct((TILE_ROWS, 128), BF16), jax.ShapeDtypeStruct(IMAGE_TABLE.shape, BF16)],
        scratch_shapes=[pltpu.SemaphoreType.DMA],
        compiler_params=pltpu.CompilerParams(vmem_limit_bytes=8 * MIB),
        name="column_spectrum",
    )(mask_logits, jnp.asarray(COLUMN_FORWARD), jnp.asarray(IMAGE_TABLE))


def pupil(scalars, step, j):
    ref, i = scalars[j % GROUPS], step * (STEP // GROUPS) + j // GROUPS
    across, along = ref[1, i], ref[2, i]
    row = lax.broadcasted_iota(jnp.int32, (FREQS, 128), 0) - FREQS // 2
    lane = jnp.bitwise_and(lax.broadcasted_iota(jnp.int32, (FREQS, 128), 1), FREQS - 1) - FREQS // 2
    row, lane = row.astype(F32) - across, lane.astype(F32) - along
    return row * row + lane * lane <= F32(RADIUS * RADIUS)


def image_kernel(group_ref, own_scalars, scalars_1, scalars_2, scalars_3, own_ref, near_ref, other_ref, target_ref, table_ref, out_ref, sums_ref,
                 fields_ref, row_field_ref, intensity_ref, cotangent_ref, spectra_ref, terms_ref, grad_ref, rounded_ref, frame_ref):
    scalars = [own_scalars, scalars_1, scalars_2, scalars_3]

    def beside(start, count):
        return jnp.concatenate([table_ref[start + 128 * i:start + 128 * (i + 1), :] for i in range(count)], 1)

    row_inverse = table_ref.at[pl.ds(pl.multiple_of(group_ref[0] * ROWS, ROWS), ROWS), :]
    row_inverse_t = table_ref.at[pl.ds(pl.multiple_of(TILE_ROWS + group_ref[0] * 128, 128), 128), :]
    even = group_ref[0] % 2 == 0
    frame_ref[MARGIN:MARGIN + TILE_ROWS] = own_ref[...]

    @pl.when(even)
    def _():
        frame_ref[:MARGIN] = near_ref[...]
        frame_ref[MARGIN + TILE_ROWS:] = other_ref[...]

    @pl.when(jnp.logical_not(even))
    def _():
        frame_ref[:MARGIN] = other_ref[...]
        frame_ref[MARGIN + TILE_ROWS:] = near_ref[...]

    product = dot(beside(FORWARD_AT, FRAME // 128), frame_ref[...])
    swapped = pltpu.roll(product[FREQS:], FREQS, 1)
    spectrum = (product[:FREQS] + halves_sign(FREQS, -1.0, 1.0) * swapped).astype(BF16).astype(F32)
    spectra_ref[:FREQS] = spectrum
    spectra_ref[FREQS:] = pltpu.roll(spectrum, FREQS, 1) * halves_sign(FREQS, -1.0, 1.0)
    intensity_ref[...] = jnp.zeros_like(intensity_ref)

    steps = SOURCES // STEP

    def image_rows(step):
        blocks = []
        for j in range(STEP):
            inside = pupil(scalars, step, j)
            inside = jnp.concatenate([inside, inside], 0)
            blocks.append(jnp.where(inside, spectra_ref[...], F32(0)).astype(BF16))
        row_field = dot(row_inverse[...], jnp.concatenate(blocks, 1)).astype(BF16)
        for j in range(STEP):
            start = pl.multiple_of((step * STEP + j) * ROWS, ROWS)
            row_field_ref[pl.ds(start, ROWS), :] = row_field[:, 128 * j:128 * (j + 1)]

    def weight(step, j):
        return scalars[j % GROUPS][0, step * (STEP // GROUPS) + j // GROUPS]

    image_rows(0)

    @pl.loop(0, steps)
    def _(step):
        start = pl.multiple_of(step * (STEP * ROWS), STEP * ROWS)
        row_field = row_field_ref[pl.ds(start, STEP * ROWS), :]
        for n in range(4):
            fields = dot(row_field, beside(INVERSE_AT + 256 * n, 2))
            fields_ref[pl.ds(start, STEP * ROWS), 256 * n:256 * (n + 1)] = fields
            power = fields[:, :128] * fields[:, :128] + fields[:, 128:] * fields[:, 128:]
            total = weight(step, 0) * power[:ROWS]
            for j in range(1, STEP):
                total = total + weight(step, j) * power[j * ROWS:(j + 1) * ROWS]
            intensity_ref[:, 128 * n:128 * (n + 1)] += total
        image_rows(jnp.minimum(step + 1, steps - 1))

    printed = jax.nn.sigmoid(F32(STEEPNESS) * (intensity_ref[...] - F32(THRESHOLD)))
    error_value = printed - target_ref[...].astype(F32)
    cotangent_ref[...] = F32(2.0 * STEEPNESS) * error_value * printed * (F32(1.0) - printed)
    error_rows = jnp.sum(error_value * error_value, 0, keepdims=True)
    error_lanes = (error_rows[:, :128] + error_rows[:, 128:256]) + (error_rows[:, 256:384] + error_rows[:, 384:])
    error_sum = jnp.sum(error_lanes, 1, keepdims=True)
    grad_ref[...] = jnp.zeros_like(grad_ref)

    rounded_ref[...] = jnp.zeros_like(rounded_ref)

    def add_block_grad(step):
        block_grad = dot(row_inverse_t[...], rounded_ref[...])
        total = jnp.zeros((2 * FREQS, 128), F32)
        for j in range(STEP):
            inside = pupil(scalars, step, j)
            inside = jnp.concatenate([inside, inside], 0)
            total = total + jnp.where(inside, block_grad[:, 128 * j:128 * (j + 1)], F32(0))
        grad_ref[...] += total

    @pl.loop(0, steps)
    def _(step):
        start = pl.multiple_of(step * (STEP * ROWS), STEP * ROWS)
        add_block_grad(jnp.maximum(step - 1, 0))
        row_grad = None
        for n in range(4):
            cot = cotangent_ref[:, 128 * n:128 * (n + 1)]
            parts = []
            for j in range(STEP):
                scaling = (F32(2.0) * weight(step, j)) * cot
                at = pl.multiple_of(start + j * ROWS, ROWS)
                fields = fields_ref[pl.ds(at, ROWS), 256 * n:256 * (n + 1)]
                parts.append((jnp.concatenate([scaling, scaling], 1) * fields).astype(BF16))
            part = dot(jnp.concatenate(parts, 0), table_ref[INVERSE_T_AT + 256 * n:INVERSE_T_AT + 256 * (n + 1), :])
            row_grad = part if row_grad is None else row_grad + part
        row_field = row_field_ref[pl.ds(start, STEP * ROWS), :].astype(F32)
        terms = row_grad * row_field
        rounded = row_grad.astype(BF16)
        for j in range(STEP):
            terms_ref[pl.ds(step * STEP + j, 1), :] = jnp.sum(terms[j * ROWS:(j + 1) * ROWS], 0, keepdims=True)
            rounded_ref[:, 128 * j:128 * (j + 1)] = rounded[j * ROWS:(j + 1) * ROWS]

    add_block_grad(steps - 1)
    grads = grad_ref[...]
    out_ref[...] = grads[:FREQS] + halves_sign(FREQS, 1.0, -1.0) * pltpu.roll(grads[FREQS:], FREQS, 1)
    term = jnp.sum(terms_ref[...], 1, keepdims=True)
    row = lax.broadcasted_iota(jnp.int32, (SOURCES, 128), 0)
    lane = lax.broadcasted_iota(jnp.int32, (SOURCES, 128), 1)
    wanted = (row % GROUPS) * PER_GROUP + row // GROUPS
    term_row = jnp.sum(jnp.where(wanted == lane, term, F32(0)), 0, keepdims=True)
    lane = lax.broadcasted_iota(jnp.int32, (1, 128), 1)
    own = group_ref[0]
    for bit, width in ((1, PER_GROUP), (2, 2 * PER_GROUP)):
        swapped = jnp.where((lane // width) % 2 == 0, pltpu.roll(term_row, 128 - width, 1),
                            pltpu.roll(term_row, width, 1))
        term_row = jnp.where(jnp.bitwise_and(own, bit) != 0, swapped, term_row)
    term_row = jnp.where(lane < SOURCES, term_row, F32(0))
    sums_ref[...] = jnp.broadcast_to(jnp.where(lane == SOURCES, error_sum, term_row)[None], sums_ref.shape)


def image(group, scalars, own, near, other, target, table, peers):
    fixed = lambda i, g: (0, 0)
    whole = lambda shape: pl.BlockSpec(shape, fixed)
    return pl.pallas_call(
        image_kernel,
        grid_spec=pltpu.PrefetchScalarGridSpec(
            num_scalar_prefetch=1,
            grid=(1,),
            in_specs=[
                *[pl.BlockSpec(memory_space=pltpu.SMEM)] * GROUPS,
                whole((TILE_ROWS, 128)), whole((MARGIN, 128)), whole((MARGIN, 128)),
                pl.BlockSpec((ROWS, COLS), lambda i, g: (g[0], 0)),
                whole(IMAGE_TABLE.shape),
            ],
            out_specs=[whole((FREQS, 128)), pl.BlockSpec((peers, 1, 128), lambda i, g: (0, 0, 0))],
            scratch_shapes=[
                pltpu.VMEM((SOURCES * ROWS, 2 * COLS), F32),
                pltpu.VMEM((SOURCES * ROWS, 128), BF16),
                pltpu.VMEM((ROWS, COLS), F32),
                pltpu.VMEM((ROWS, COLS), F32),
                pltpu.VMEM((128, 128), F32),
                pltpu.VMEM((SOURCES, 128), F32),
                pltpu.VMEM((128, 128), F32),
                pltpu.VMEM((ROWS, STEP * 128), BF16),
                pltpu.VMEM((FRAME, 128), BF16),
            ],
        ),
        out_shape=[jax.ShapeDtypeStruct((FREQS, 128), F32), jax.ShapeDtypeStruct((peers, 1, 128), F32)],
        compiler_params=pltpu.CompilerParams(vmem_limit_bytes=44 * MIB),
        name="image",
    )(group, *scalars, own, near, other, target, table)


def split_dot(table, x):
    high = x.astype(BF16)
    low = (x - high.astype(F32)).astype(BF16)
    return dot(jnp.concatenate([table, table], 1), jnp.concatenate([high, low], 0))


def dot_split(x, table):
    high = x.astype(BF16)
    low = (x - high.astype(F32)).astype(BF16)
    return dot(jnp.concatenate([high, low], 1), jnp.concatenate([table, table], 0))


def product_gradient(spectrum_grad):
    lower = pltpu.roll(spectrum_grad, FREQS, 1) * halves_sign(FREQS, 1.0, -1.0)
    return jnp.concatenate([spectrum_grad, lower], 0)


def owned_kernel(grad_ref, logits_ref, row_ref, column_ref, out_ref, edges_ref, slope_ref):
    column_grad = split_dot(row_ref[...], product_gradient(grad_ref[...]))
    opening = jax.nn.sigmoid(logits_ref[...])
    slope = opening * (F32(1.0) - opening)
    out = dot_split(column_grad, column_ref[...]) * slope
    out_ref[...] = out
    edges_ref[:MARGIN] = out[:MARGIN]
    edges_ref[MARGIN:] = out[TILE_ROWS - MARGIN:]
    slope_ref[:MARGIN] = slope[:MARGIN]
    slope_ref[MARGIN:] = slope[TILE_ROWS - MARGIN:]


def owned_gradient(spectrum_grad, mask_logits):
    return pl.pallas_call(
        owned_kernel,
        out_shape=[jax.ShapeDtypeStruct((n, COLS), F32) for n in (TILE_ROWS, 2 * MARGIN, 2 * MARGIN)],
        compiler_params=pltpu.CompilerParams(vmem_limit_bytes=10 * MIB),
        name="owned_gradient",
    )(spectrum_grad, mask_logits,
      jnp.asarray(np.ascontiguousarray(ROW_FORWARD.T[MARGIN:MARGIN + TILE_ROWS])),
      jnp.asarray(np.ascontiguousarray(COLUMN_FORWARD.T)))


def last_kernel(group_ref, near_ref, other_ref, edges_ref, slope_ref, row_ref, column_ref, own_ref, beside_ref,
                far_ref, across_ref, packed_ref, grad_ref, out_ref, weight_grad_ref, loss_ref,
                rows_ref, semaphores, *, pixels):
    del grad_ref
    even = group_ref[0] % 2 == 0
    before = jnp.where(even, near_ref[...], other_ref[...])
    after = jnp.where(even, other_ref[...], near_ref[...])
    column_grad = jnp.concatenate([split_dot(row_ref[:MARGIN], product_gradient(before)),
                                   split_dot(row_ref[MARGIN:], product_gradient(after))], 0)
    rows_ref[...] = edges_ref[...] + dot_split(column_grad, column_ref[...]) * slope_ref[...]
    copies = [
        pltpu.make_async_copy(rows_ref.at[pl.ds(0, MARGIN), :], out_ref.at[pl.ds(0, MARGIN), :], semaphores.at[0]),
        pltpu.make_async_copy(rows_ref.at[pl.ds(MARGIN, MARGIN), :],
                              out_ref.at[pl.ds(TILE_ROWS - MARGIN, MARGIN), :], semaphores.at[1]),
    ]
    for copy in copies:
        copy.start()
    total = (own_ref[...] + beside_ref[...]) + (far_ref[...] + across_ref[...])
    row = total
    for bit, width in ((1, PER_GROUP), (2, 2 * PER_GROUP)):
        row = jnp.where(jnp.bitwise_and(group_ref[0], bit) != 0, pltpu.roll(row, 128 - width, 1), row)
    weight_grad_ref[...] = row[:, :PER_GROUP] / (F32(2.0) * packed_ref[0:1]) / F32(pixels)
    loss_ref[...] = total[:, SOURCES:SOURCES + 1] / F32(pixels)
    for copy in copies:
        copy.wait()


def last_steps(group, near, other, edges, slope, grad, sums, packed, pixels):
    rows = np.concatenate([ROW_FORWARD.T[MARGIN + TILE_ROWS:], ROW_FORWARD.T[:MARGIN]], 0)
    block = pl.BlockSpec()
    hbm = pl.BlockSpec(memory_space=pltpu.HBM)
    return pl.pallas_call(
        functools.partial(last_kernel, pixels=pixels),
        in_specs=[pl.BlockSpec(memory_space=pltpu.SMEM)] + [block] * 11 + [hbm],
        out_specs=[hbm, block, block],
        out_shape=[jax.ShapeDtypeStruct((TILE_ROWS, COLS), F32), jax.ShapeDtypeStruct((1, PER_GROUP), F32),
                   jax.ShapeDtypeStruct((1, 1), F32)],
        scratch_shapes=[pltpu.VMEM((2 * MARGIN, COLS), F32), pltpu.SemaphoreType.DMA((2,))],
        input_output_aliases={12: 0},
        compiler_params=pltpu.CompilerParams(vmem_limit_bytes=4 * MIB),
        name="last_steps",
    )(group, near, other, edges, slope, jnp.asarray(np.ascontiguousarray(rows)),
      jnp.asarray(np.ascontiguousarray(COLUMN_FORWARD.T)), *sums, packed, grad)


def from_tile_beside(x):
    peers = lax.axis_size("tile")
    pairs = [(s * peers + i, s * peers + j) for s in range(GROUPS) for i in range(peers)
             for j in [i + 1 - 2 * (s % 2)] if 0 <= j < peers]
    return lax.ppermute(x, ("src", "tile"), pairs)


def from_group(x, d):
    return lax.ppermute(x, "src", [(i, i ^ d) for i in range(GROUPS)])


def from_core(x):
    return from_group(x, 1)


def from_chip(x):
    return from_group(x, 2)


def on_device(mask_logits, target, weights, shifts):
    peers = lax.axis_size("tile")
    group = lax.axis_index("src").astype(jnp.int32).reshape(1)
    edge, packed = edge_spectrum(group, mask_logits, weights, shifts)
    near = from_tile_beside(edge)
    packed_far = from_chip(packed)
    packed_core = from_core(packed)
    own, table = column_spectrum(mask_logits)
    near, packed_far, own = lax.optimization_barrier((near, packed_far, own))
    scalars = [packed, packed_core, packed_far, from_core(packed_far)]
    partial, sums = image(group, scalars, own, near, from_core(near), target, table, peers)
    sums = lax.all_to_all(sums, "tile", 0, 0, tiled=True)
    beside = from_core(partial)
    chip = partial + beside
    spectrum_grad = chip + from_chip(chip)
    near_grad = from_tile_beside(spectrum_grad)
    sums = jnp.sum(sums, 0)
    sums_far = from_chip(sums)
    grad, edges, slope = owned_gradient(spectrum_grad, mask_logits)
    near_grad, sums_far, edges = lax.optimization_barrier((near_grad, sums_far, edges))
    sums = [sums, from_core(sums), sums_far, from_core(sums_far)]
    mask_grad, weight_grad, loss = last_steps(
        group, near_grad, from_core(near_grad), edges, slope, grad, sums, packed, TILE_ROWS * COLS * peers)
    return mask_grad, weight_grad.reshape(PER_GROUP), loss.reshape(())


def solution(mesh):
    placed = (P("tile", None), P("tile", None), P("src"), P("src", None))
    return jax.shard_map(
        on_device,
        mesh=mesh,
        in_specs=placed,
        out_specs=(P("tile", None), P("src"), P()),
        check_vma=False,
    )
```

```python
import functools

import numpy as np
import jax
import jax.numpy as jnp
from jax import lax
from jax.experimental import pallas as pl
from jax.experimental.pallas import tpu as pltpu
from jax.sharding import Mesh, PartitionSpec as P


FREQS = 64
RADIUS = 20
MARGIN = 64
COLS = 512
TILE_ROWS = 512
FRAME = 640
SOURCES = 64
GROUPS = 4
PLANES = 4
PLANE = 16
PER_GROUP = SOURCES // GROUPS
ROWS = TILE_ROWS // GROUPS
MIB = 1024 * 1024
STEEPNESS = 12.0
THRESHOLD = 0.2
STEP = 16
F32 = jnp.float32
BF16 = jnp.bfloat16


def angles(length_used, offset, period):
    position = np.arange(length_used, dtype=np.int32)[:, None] + offset
    frequency = np.arange(FREQS, dtype=np.int32)[None, :] - FREQS // 2
    cycles = np.mod(position * frequency, period).astype(np.float32)
    angle_value = (cycles * np.float32(2.0 * 3.141592653589793 / period)).astype(np.float64)
    return np.cos(angle_value).astype(np.float32), np.sin(angle_value).astype(np.float32)


def make_tables():
    column_cosine, column_sine = angles(COLS, 0, COLS)
    column_forward = np.concatenate([column_cosine, -column_sine], 1)
    frame_cosine, frame_sine = angles(FRAME, 0, FRAME)
    row_forward = np.concatenate([frame_cosine.T, -frame_sine.T], 0)
    owned_cosine, owned_sine = angles(TILE_ROWS, MARGIN, FRAME)
    row_inverse = np.concatenate([owned_cosine, owned_sine], 1) / np.float32(FRAME)
    cosine_scaled = column_cosine.T / np.float32(COLS)
    sine_scaled = column_sine.T / np.float32(COLS)
    upper_block = np.concatenate([cosine_scaled, sine_scaled], 1)
    lower_block = np.concatenate([-sine_scaled, cosine_scaled], 1)
    column_inverse = np.concatenate([upper_block, lower_block], 0)
    chunked = column_inverse.reshape(2 * FREQS, 2, COLS // 128, 128).transpose(0, 2, 1, 3)
    chunked = chunked.reshape(2 * FREQS, 2 * COLS)
    rounded = lambda a: np.ascontiguousarray(a).astype(BF16)
    return [rounded(a) for a in (column_forward, row_forward, row_inverse, chunked)]


COLUMN_FORWARD, ROW_FORWARD, ROW_INVERSE, COLUMN_INVERSE = make_tables()


def stacked(table):
    return np.concatenate([table[:, c:c + 128] for c in range(0, table.shape[1], 128)], 0)


PARTS = [ROW_INVERSE, stacked(ROW_INVERSE.T), COLUMN_INVERSE.T, stacked(COLUMN_INVERSE), stacked(ROW_FORWARD)]
IMAGE_TABLE = np.ascontiguousarray(np.concatenate(PARTS, 0))
INVERSE_T_AT = 2 * TILE_ROWS
INVERSE_AT = INVERSE_T_AT + 2 * COLS
FORWARD_AT = INVERSE_AT + 8 * 128


def dot(a, b):
    return jnp.dot(a, b, preferred_element_type=F32)


def halves_sign(rows, left, right):
    lane = lax.broadcasted_iota(jnp.int32, (rows, 128), 1)
    return jnp.where(lane < FREQS, F32(left), F32(right))


def edge_kernel(group_ref, logits_ref, table_ref, weights_ref, shifts_ref, edge_out, packed_out,
                rows, table, weights, shifts, semaphores):
    start = jnp.where(group_ref[0] % 2 == 0, TILE_ROWS - MARGIN, 0)
    rows_from = logits_ref.at[pl.ds(pl.multiple_of(start, MARGIN), MARGIN), :]
    pairs = ((rows_from, rows), (table_ref, table), (weights_ref, weights), (shifts_ref, shifts))
    copies = [pltpu.make_async_copy(a, b, semaphores.at[i]) for i, (a, b) in enumerate(pairs)]
    for copy in copies:
        copy.start()
    for copy in copies:
        copy.wait()
    edge_out[...] = dot(jax.nn.sigmoid(rows[...]).astype(BF16), table[...]).astype(BF16)
    packed_out[0:1] = weights[...]
    packed_out[1:3] = shifts[...].astype(F32)


def edge_spectrum(group, mask_logits, weights, shifts):
    return pl.pallas_call(
        edge_kernel,
        in_specs=[pl.BlockSpec(memory_space=pltpu.SMEM)] + [pl.BlockSpec(memory_space=pltpu.HBM)] * 4,
        out_shape=[jax.ShapeDtypeStruct((MARGIN, 128), BF16), jax.ShapeDtypeStruct((3, PER_GROUP), F32)],
        scratch_shapes=[
            pltpu.VMEM((MARGIN, COLS), F32), pltpu.VMEM((COLS, 128), BF16),
            pltpu.VMEM((1, PER_GROUP), F32), pltpu.VMEM((2, PER_GROUP), jnp.int32),
            pltpu.SemaphoreType.DMA((4,)),
        ],
        compiler_params=pltpu.CompilerParams(vmem_limit_bytes=60 * MIB),
        name="edge_spectrum",
    )(group, mask_logits, jnp.asarray(COLUMN_FORWARD), weights.reshape(1, PER_GROUP), shifts.T)


def column_kernel(logits_ref, table_ref, image_table_ref, out_ref, image_table_out, semaphore):
    copy = pltpu.make_async_copy(image_table_ref, image_table_out, semaphore)
    copy.start()
    out_ref[...] = dot(jax.nn.sigmoid(logits_ref[...]).astype(BF16), table_ref[...]).astype(BF16)
    copy.wait()


def column_spectrum(mask_logits):
    return pl.pallas_call(
        column_kernel,
        in_specs=[pl.BlockSpec(), pl.BlockSpec(), pl.BlockSpec(memory_space=pltpu.HBM)],
        out_shape=[jax.ShapeDtypeStruct((TILE_ROWS, 128), BF16), jax.ShapeDtypeStruct(IMAGE_TABLE.shape, BF16)],
        scratch_shapes=[pltpu.SemaphoreType.DMA],
        compiler_params=pltpu.CompilerParams(vmem_limit_bytes=8 * MIB),
        name="column_spectrum",
    )(mask_logits, jnp.asarray(COLUMN_FORWARD), jnp.asarray(IMAGE_TABLE))


def pupil(scalars, step, j):
    ref, i = scalars[j % GROUPS], step * (STEP // GROUPS) + j // GROUPS
    across, along = ref[1, i], ref[2, i]
    row = lax.broadcasted_iota(jnp.int32, (FREQS, 128), 0) - FREQS // 2
    lane = jnp.bitwise_and(lax.broadcasted_iota(jnp.int32, (FREQS, 128), 1), FREQS - 1) - FREQS // 2
    row, lane = row.astype(F32) - across, lane.astype(F32) - along
    return row * row + lane * lane <= F32(RADIUS * RADIUS)


def image_kernel(group_ref, own_scalars, scalars_1, scalars_2, scalars_3, own_ref, near_ref, other_ref, target_ref, table_ref, out_ref, sums_ref,
                 fields_ref, row_field_ref, intensity_ref, cotangent_ref, spectra_ref, terms_ref, grad_ref, rounded_ref, frame_ref):
    scalars = [own_scalars, scalars_1, scalars_2, scalars_3]

    def beside(start, count):
        return jnp.concatenate([table_ref[start + 128 * i:start + 128 * (i + 1), :] for i in range(count)], 1)

    row_inverse = table_ref.at[pl.ds(pl.multiple_of(group_ref[0] * ROWS, ROWS), ROWS), :]
    row_inverse_t = table_ref.at[pl.ds(pl.multiple_of(TILE_ROWS + group_ref[0] * 128, 128), 128), :]
    even = group_ref[0] % 2 == 0
    frame_ref[MARGIN:MARGIN + TILE_ROWS] = own_ref[...]

    @pl.when(even)
    def _():
        frame_ref[:MARGIN] = near_ref[...]
        frame_ref[MARGIN + TILE_ROWS:] = other_ref[...]

    @pl.when(jnp.logical_not(even))
    def _():
        frame_ref[:MARGIN] = other_ref[...]
        frame_ref[MARGIN + TILE_ROWS:] = near_ref[...]

    product = dot(beside(FORWARD_AT, FRAME // 128), frame_ref[...])
    swapped = pltpu.roll(product[FREQS:], FREQS, 1)
    spectrum = (product[:FREQS] + halves_sign(FREQS, -1.0, 1.0) * swapped).astype(BF16).astype(F32)
    spectra_ref[:FREQS] = spectrum
    spectra_ref[FREQS:] = pltpu.roll(spectrum, FREQS, 1) * halves_sign(FREQS, -1.0, 1.0)
    intensity_ref[...] = jnp.zeros_like(intensity_ref)

    steps = SOURCES // STEP

    def image_rows(step):
        blocks = []
        for j in range(STEP):
            inside = pupil(scalars, step, j)
            inside = jnp.concatenate([inside, inside], 0)
            blocks.append(jnp.where(inside, spectra_ref[...], F32(0)).astype(BF16))
        row_field = dot(row_inverse[...], jnp.concatenate(blocks, 1)).astype(BF16)
        for j in range(STEP):
            start = pl.multiple_of((step * STEP + j) * ROWS, ROWS)
            row_field_ref[pl.ds(start, ROWS), :] = row_field[:, 128 * j:128 * (j + 1)]

    def weight(step, j):
        return scalars[j % GROUPS][0, step * (STEP // GROUPS) + j // GROUPS]

    image_rows(0)

    @pl.loop(0, steps)
    def _(step):
        start = pl.multiple_of(step * (STEP * ROWS), STEP * ROWS)
        row_field = row_field_ref[pl.ds(start, STEP * ROWS), :]
        for n in range(4):
            fields = dot(row_field, beside(INVERSE_AT + 256 * n, 2))
            fields_ref[pl.ds(start, STEP * ROWS), 256 * n:256 * (n + 1)] = fields
            power = fields[:, :128] * fields[:, :128] + fields[:, 128:] * fields[:, 128:]
            total = weight(step, 0) * power[:ROWS]
            for j in range(1, STEP):
                total = total + weight(step, j) * power[j * ROWS:(j + 1) * ROWS]
            intensity_ref[:, 128 * n:128 * (n + 1)] += total
        image_rows(jnp.minimum(step + 1, steps - 1))

    printed = jax.nn.sigmoid(F32(STEEPNESS) * (intensity_ref[...] - F32(THRESHOLD)))
    error_value = printed - target_ref[...].astype(F32)
    cotangent_ref[...] = F32(2.0 * STEEPNESS) * error_value * printed * (F32(1.0) - printed)
    error_rows = jnp.sum(error_value * error_value, 0, keepdims=True)
    error_lanes = (error_rows[:, :128] + error_rows[:, 128:256]) + (error_rows[:, 256:384] + error_rows[:, 384:])
    error_sum = jnp.sum(error_lanes, 1, keepdims=True)
    grad_ref[...] = jnp.zeros_like(grad_ref)

    rounded_ref[...] = jnp.zeros_like(rounded_ref)

    def add_block_grad(step):
        block_grad = dot(row_inverse_t[...], rounded_ref[...])
        total = jnp.zeros((2 * FREQS, 128), F32)
        for j in range(STEP):
            inside = pupil(scalars, step, j)
            inside = jnp.concatenate([inside, inside], 0)
            total = total + jnp.where(inside, block_grad[:, 128 * j:128 * (j + 1)], F32(0))
        grad_ref[...] += total

    @pl.loop(0, steps)
    def _(step):
        start = pl.multiple_of(step * (STEP * ROWS), STEP * ROWS)
        add_block_grad(jnp.maximum(step - 1, 0))
        row_grad = None
        for n in range(4):
            cot = cotangent_ref[:, 128 * n:128 * (n + 1)]
            parts = []
            for j in range(STEP):
                scaling = (F32(2.0) * weight(step, j)) * cot
                at = pl.multiple_of(start + j * ROWS, ROWS)
                fields = fields_ref[pl.ds(at, ROWS), 256 * n:256 * (n + 1)]
                parts.append((jnp.concatenate([scaling, scaling], 1) * fields).astype(BF16))
            part = dot(jnp.concatenate(parts, 0), table_ref[INVERSE_T_AT + 256 * n:INVERSE_T_AT + 256 * (n + 1), :])
            row_grad = part if row_grad is None else row_grad + part
        row_field = row_field_ref[pl.ds(start, STEP * ROWS), :].astype(F32)
        terms = row_grad * row_field
        rounded = row_grad.astype(BF16)
        for j in range(STEP):
            terms_ref[pl.ds(step * STEP + j, 1), :] = jnp.sum(terms[j * ROWS:(j + 1) * ROWS], 0, keepdims=True)
            rounded_ref[:, 128 * j:128 * (j + 1)] = rounded[j * ROWS:(j + 1) * ROWS]

    add_block_grad(steps - 1)
    grads = grad_ref[...]
    out_ref[...] = grads[:FREQS] + halves_sign(FREQS, 1.0, -1.0) * pltpu.roll(grads[FREQS:], FREQS, 1)
    term = jnp.sum(terms_ref[...], 1, keepdims=True)
    row = lax.broadcasted_iota(jnp.int32, (SOURCES, 128), 0)
    lane = lax.broadcasted_iota(jnp.int32, (SOURCES, 128), 1)
    wanted = (row % GROUPS) * PER_GROUP + row // GROUPS
    term_row = jnp.sum(jnp.where(wanted == lane, term, F32(0)), 0, keepdims=True)
    lane = lax.broadcasted_iota(jnp.int32, (1, 128), 1)
    own = group_ref[0]
    for bit, width in ((1, PER_GROUP), (2, 2 * PER_GROUP)):
        swapped = jnp.where((lane // width) % 2 == 0, pltpu.roll(term_row, 128 - width, 1),
                            pltpu.roll(term_row, width, 1))
        term_row = jnp.where(jnp.bitwise_and(own, bit) != 0, swapped, term_row)
    term_row = jnp.where(lane < SOURCES, term_row, F32(0))
    sums_ref[...] = jnp.broadcast_to(jnp.where(lane == SOURCES, error_sum, term_row)[None], sums_ref.shape)


def image(group, scalars, own, near, other, target, table):
    fixed = lambda i, g: (0, 0)
    whole = lambda shape: pl.BlockSpec(shape, fixed)
    return pl.pallas_call(
        image_kernel,
        grid_spec=pltpu.PrefetchScalarGridSpec(
            num_scalar_prefetch=1,
            grid=(1,),
            in_specs=[
                *[pl.BlockSpec(memory_space=pltpu.SMEM)] * GROUPS,
                whole((TILE_ROWS, 128)), whole((MARGIN, 128)), whole((MARGIN, 128)),
                pl.BlockSpec((ROWS, COLS), lambda i, g: (g[0], 0)),
                whole(IMAGE_TABLE.shape),
            ],
            out_specs=[whole((FREQS, 128)), pl.BlockSpec((PLANE, 1, 128), lambda i, g: (0, 0, 0))],
            scratch_shapes=[
                pltpu.VMEM((SOURCES * ROWS, 2 * COLS), F32),
                pltpu.VMEM((SOURCES * ROWS, 128), BF16),
                pltpu.VMEM((ROWS, COLS), F32),
                pltpu.VMEM((ROWS, COLS), F32),
                pltpu.VMEM((128, 128), F32),
                pltpu.VMEM((SOURCES, 128), F32),
                pltpu.VMEM((128, 128), F32),
                pltpu.VMEM((ROWS, STEP * 128), BF16),
                pltpu.VMEM((FRAME, 128), BF16),
            ],
        ),
        out_shape=[jax.ShapeDtypeStruct((FREQS, 128), F32), jax.ShapeDtypeStruct((PLANE, 1, 128), F32)],
        compiler_params=pltpu.CompilerParams(vmem_limit_bytes=44 * MIB),
        name="image",
    )(group, *scalars, own, near, other, target, table)


def regroup_kernel(rows_ref, out_ref):
    out_ref[...] = jnp.broadcast_to(jnp.sum(rows_ref[...], 0)[None], out_ref.shape)


def regroup(rows):
    return pl.pallas_call(
        regroup_kernel,
        out_shape=jax.ShapeDtypeStruct((GROUPS * PLANES, 1, 128), F32),
        compiler_params=pltpu.CompilerParams(vmem_limit_bytes=1 * MIB),
        name="regroup",
    )(rows)


def split_dot(table, x):
    high = x.astype(BF16)
    low = (x - high.astype(F32)).astype(BF16)
    return dot(jnp.concatenate([table, table], 1), jnp.concatenate([high, low], 0))


def dot_split(x, table):
    high = x.astype(BF16)
    low = (x - high.astype(F32)).astype(BF16)
    return dot(jnp.concatenate([high, low], 1), jnp.concatenate([table, table], 0))


def product_gradient(spectrum_grad):
    lower = pltpu.roll(spectrum_grad, FREQS, 1) * halves_sign(FREQS, 1.0, -1.0)
    return jnp.concatenate([spectrum_grad, lower], 0)


def owned_kernel(grad_ref, logits_ref, row_ref, column_ref, out_ref, edges_ref, slope_ref):
    column_grad = split_dot(row_ref[...], product_gradient(grad_ref[...]))
    opening = jax.nn.sigmoid(logits_ref[...])
    slope = opening * (F32(1.0) - opening)
    out = dot_split(column_grad, column_ref[...]) * slope
    out_ref[...] = out
    edges_ref[:MARGIN] = out[:MARGIN]
    edges_ref[MARGIN:] = out[TILE_ROWS - MARGIN:]
    slope_ref[:MARGIN] = slope[:MARGIN]
    slope_ref[MARGIN:] = slope[TILE_ROWS - MARGIN:]


def owned_gradient(spectrum_grad, mask_logits):
    return pl.pallas_call(
        owned_kernel,
        out_shape=[jax.ShapeDtypeStruct((n, COLS), F32) for n in (TILE_ROWS, 2 * MARGIN, 2 * MARGIN)],
        compiler_params=pltpu.CompilerParams(vmem_limit_bytes=10 * MIB),
        name="owned_gradient",
    )(spectrum_grad, mask_logits,
      jnp.asarray(np.ascontiguousarray(ROW_FORWARD.T[MARGIN:MARGIN + TILE_ROWS])),
      jnp.asarray(np.ascontiguousarray(COLUMN_FORWARD.T)))


def last_kernel(group_ref, near_ref, other_ref, edges_ref, slope_ref, row_ref, column_ref, sums_ref,
                packed_ref, grad_ref, out_ref, weight_grad_ref, loss_ref,
                rows_ref, semaphores, *, pixels):
    del grad_ref
    even = group_ref[0] % 2 == 0
    before = jnp.where(even, near_ref[...], other_ref[...])
    after = jnp.where(even, other_ref[...], near_ref[...])
    column_grad = jnp.concatenate([split_dot(row_ref[:MARGIN], product_gradient(before)),
                                   split_dot(row_ref[MARGIN:], product_gradient(after))], 0)
    rows_ref[...] = edges_ref[...] + dot_split(column_grad, column_ref[...]) * slope_ref[...]
    copies = [
        pltpu.make_async_copy(rows_ref.at[pl.ds(0, MARGIN), :], out_ref.at[pl.ds(0, MARGIN), :], semaphores.at[0]),
        pltpu.make_async_copy(rows_ref.at[pl.ds(MARGIN, MARGIN), :],
                              out_ref.at[pl.ds(TILE_ROWS - MARGIN, MARGIN), :], semaphores.at[1]),
    ]
    for copy in copies:
        copy.start()
    total = jnp.sum(sums_ref[...], 0)
    row = total
    for bit, width in ((1, PER_GROUP), (2, 2 * PER_GROUP)):
        row = jnp.where(jnp.bitwise_and(group_ref[0], bit) != 0, pltpu.roll(row, 128 - width, 1), row)
    weight_grad_ref[...] = row[:, :PER_GROUP] / (F32(2.0) * packed_ref[0:1]) / F32(pixels)
    loss_ref[...] = total[:, SOURCES:SOURCES + 1] / F32(pixels)
    for copy in copies:
        copy.wait()


def last_steps(group, near, other, edges, slope, grad, sums, packed, pixels):
    rows = np.concatenate([ROW_FORWARD.T[MARGIN + TILE_ROWS:], ROW_FORWARD.T[:MARGIN]], 0)
    block = pl.BlockSpec()
    hbm = pl.BlockSpec(memory_space=pltpu.HBM)
    return pl.pallas_call(
        functools.partial(last_kernel, pixels=pixels),
        in_specs=[pl.BlockSpec(memory_space=pltpu.SMEM)] + [block] * 8 + [hbm],
        out_specs=[hbm, block, block],
        out_shape=[jax.ShapeDtypeStruct((TILE_ROWS, COLS), F32), jax.ShapeDtypeStruct((1, PER_GROUP), F32),
                   jax.ShapeDtypeStruct((1, 1), F32)],
        scratch_shapes=[pltpu.VMEM((2 * MARGIN, COLS), F32), pltpu.SemaphoreType.DMA((2,))],
        input_output_aliases={9: 0},
        compiler_params=pltpu.CompilerParams(vmem_limit_bytes=4 * MIB),
        name="last_steps",
    )(group, near, other, edges, slope, jnp.asarray(np.ascontiguousarray(rows)),
      jnp.asarray(np.ascontiguousarray(COLUMN_FORWARD.T)), sums, packed, grad)


def from_tile_beside(x):
    peers = PLANES * PLANE
    pairs = [(s * peers + i, s * peers + j) for s in range(GROUPS) for i in range(peers)
             for j in [i + 1 - 2 * (s % 2)] if 0 <= j < peers]
    return lax.ppermute(x, ("src", "plane", "spot"), pairs)


def from_group(x, d):
    return lax.ppermute(x, "src", [(i, i ^ d) for i in range(GROUPS)])


def from_core(x):
    return from_group(x, 1)


def from_chip(x):
    return from_group(x, 2)


def on_device(mask_logits, target, weights, shifts):
    group = lax.axis_index("src").astype(jnp.int32).reshape(1)
    edge, packed = edge_spectrum(group, mask_logits, weights, shifts)
    near = from_tile_beside(edge)
    packed_far = from_chip(packed)
    packed_core = from_core(packed)
    own, table = column_spectrum(mask_logits)
    near, packed_far, own = lax.optimization_barrier((near, packed_far, own))
    scalars = [packed, packed_core, packed_far, from_core(packed_far)]
    partial, sums = image(group, scalars, own, near, from_core(near), target, table)
    sums = lax.all_to_all(sums, "spot", 0, 0, tiled=True)
    beside = from_core(partial)
    chip = partial + beside
    far = from_chip(chip)
    sums = regroup(sums)
    sums = lax.all_to_all(sums, ("src", "plane"), 0, 0, tiled=True)
    spectrum_grad = chip + far
    near_grad = from_tile_beside(spectrum_grad)
    grad, edges, slope = owned_gradient(spectrum_grad, mask_logits)
    near_grad, edges = lax.optimization_barrier((near_grad, edges))
    mask_grad, weight_grad, loss = last_steps(
        group, near_grad, from_core(near_grad), edges, slope, grad, sums, packed,
        TILE_ROWS * COLS * PLANES * PLANE)
    return mask_grad, weight_grad.reshape(PER_GROUP), loss.reshape(())


def solution(mesh):
    split = Mesh(mesh.devices.reshape(GROUPS, PLANES, PLANE), ("src", "plane", "spot"))
    tile = ("plane", "spot")
    return jax.shard_map(
        on_device,
        mesh=split,
        in_specs=(P(tile, None), P(tile, None), P("src"), P("src", None)),
        out_specs=(P(tile, None), P("src"), P()),
        check_vma=False,
    )
```

```python
import functools

import numpy as np
import jax
import jax.numpy as jnp
from jax import lax
from jax.experimental import pallas as pl
from jax.experimental.pallas import tpu as pltpu
from jax.sharding import PartitionSpec as P


FREQS = 64
RADIUS = 20
MARGIN = 64
COLS = 512
TILE_ROWS = 512
FRAME = 640
SOURCES = 64
GROUPS = 4
PER_GROUP = SOURCES // GROUPS
ROWS = TILE_ROWS // GROUPS
MIB = 1024 * 1024
STEEPNESS = 12.0
THRESHOLD = 0.2
STEP = 32
F32 = jnp.float32
BF16 = jnp.bfloat16


def angles(length_used, offset, period):
    position = np.arange(length_used, dtype=np.int32)[:, None] + offset
    frequency = np.arange(FREQS, dtype=np.int32)[None, :] - FREQS // 2
    cycles = np.mod(position * frequency, period).astype(np.float32)
    angle_value = (cycles * np.float32(2.0 * 3.141592653589793 / period)).astype(np.float64)
    return np.cos(angle_value).astype(np.float32), np.sin(angle_value).astype(np.float32)


def make_tables():
    column_cosine, column_sine = angles(COLS, 0, COLS)
    column_forward = np.concatenate([column_cosine, -column_sine], 1)
    frame_cosine, frame_sine = angles(FRAME, 0, FRAME)
    row_forward = np.concatenate([frame_cosine.T, -frame_sine.T], 0)
    owned_cosine, owned_sine = angles(TILE_ROWS, MARGIN, FRAME)
    row_inverse = np.concatenate([owned_cosine, owned_sine], 1) / np.float32(FRAME)
    cosine_scaled = column_cosine.T / np.float32(COLS)
    sine_scaled = column_sine.T / np.float32(COLS)
    upper_block = np.concatenate([cosine_scaled, sine_scaled], 1)
    lower_block = np.concatenate([-sine_scaled, cosine_scaled], 1)
    column_inverse = np.concatenate([upper_block, lower_block], 0)
    chunked = column_inverse.reshape(2 * FREQS, 2, COLS // 128, 128).transpose(0, 2, 1, 3)
    chunked = chunked.reshape(2 * FREQS, 2 * COLS)
    rounded = lambda a: np.ascontiguousarray(a).astype(BF16)
    return [rounded(a) for a in (column_forward, row_forward, row_inverse, chunked)]


COLUMN_FORWARD, ROW_FORWARD, ROW_INVERSE, COLUMN_INVERSE = make_tables()


def stacked(table):
    return np.concatenate([table[:, c:c + 128] for c in range(0, table.shape[1], 128)], 0)


PARTS = [ROW_INVERSE, stacked(ROW_INVERSE.T), COLUMN_INVERSE.T, stacked(COLUMN_INVERSE), stacked(ROW_FORWARD)]
IMAGE_TABLE = np.ascontiguousarray(np.concatenate(PARTS, 0))
INVERSE_T_AT = 2 * TILE_ROWS
INVERSE_AT = INVERSE_T_AT + 2 * COLS
FORWARD_AT = INVERSE_AT + 8 * 128


def dot(a, b):
    return jnp.dot(a, b, preferred_element_type=F32)


def halves_sign(rows, left, right):
    lane = lax.broadcasted_iota(jnp.int32, (rows, 128), 1)
    return jnp.where(lane < FREQS, F32(left), F32(right))


def edge_kernel(group_ref, logits_ref, table_ref, weights_ref, shifts_ref, edge_out, packed_out,
                rows, table, weights, shifts, semaphores):
    start = jnp.where(group_ref[0] % 2 == 0, TILE_ROWS - MARGIN, 0)
    rows_from = logits_ref.at[pl.ds(pl.multiple_of(start, MARGIN), MARGIN), :]
    pairs = ((rows_from, rows), (table_ref, table), (weights_ref, weights), (shifts_ref, shifts))
    copies = [pltpu.make_async_copy(a, b, semaphores.at[i]) for i, (a, b) in enumerate(pairs)]
    for copy in copies:
        copy.start()
    for copy in copies:
        copy.wait()
    edge_out[...] = dot(jax.nn.sigmoid(rows[...]).astype(BF16), table[...]).astype(BF16)
    packed_out[0:1] = weights[...]
    packed_out[1:3] = shifts[...].astype(F32)


def edge_spectrum(group, mask_logits, weights, shifts):
    return pl.pallas_call(
        edge_kernel,
        in_specs=[pl.BlockSpec(memory_space=pltpu.SMEM)] + [pl.BlockSpec(memory_space=pltpu.HBM)] * 4,
        out_shape=[jax.ShapeDtypeStruct((MARGIN, 128), BF16), jax.ShapeDtypeStruct((3, PER_GROUP), F32)],
        scratch_shapes=[
            pltpu.VMEM((MARGIN, COLS), F32), pltpu.VMEM((COLS, 128), BF16),
            pltpu.VMEM((1, PER_GROUP), F32), pltpu.VMEM((2, PER_GROUP), jnp.int32),
            pltpu.SemaphoreType.DMA((4,)),
        ],
        compiler_params=pltpu.CompilerParams(vmem_limit_bytes=60 * MIB),
        name="edge_spectrum",
    )(group, mask_logits, jnp.asarray(COLUMN_FORWARD), weights.reshape(1, PER_GROUP), shifts.T)


def column_kernel(logits_ref, table_ref, image_table_ref, out_ref, image_table_out, semaphore):
    copy = pltpu.make_async_copy(image_table_ref, image_table_out, semaphore)
    copy.start()
    out_ref[...] = dot(jax.nn.sigmoid(logits_ref[...]).astype(BF16), table_ref[...]).astype(BF16)
    copy.wait()


def column_spectrum(mask_logits):
    return pl.pallas_call(
        column_kernel,
        in_specs=[pl.BlockSpec(), pl.BlockSpec(), pl.BlockSpec(memory_space=pltpu.HBM)],
        out_shape=[jax.ShapeDtypeStruct((TILE_ROWS, 128), BF16), jax.ShapeDtypeStruct(IMAGE_TABLE.shape, BF16)],
        scratch_shapes=[pltpu.SemaphoreType.DMA],
        compiler_params=pltpu.CompilerParams(vmem_limit_bytes=8 * MIB),
        name="column_spectrum",
    )(mask_logits, jnp.asarray(COLUMN_FORWARD), jnp.asarray(IMAGE_TABLE))


def pupil(scalars, step, j):
    ref, i = scalars[j % GROUPS], step * (STEP // GROUPS) + j // GROUPS
    across, along = ref[1, i], ref[2, i]
    row = lax.broadcasted_iota(jnp.int32, (FREQS, 128), 0) - FREQS // 2
    lane = jnp.bitwise_and(lax.broadcasted_iota(jnp.int32, (FREQS, 128), 1), FREQS - 1) - FREQS // 2
    row, lane = row.astype(F32) - across, lane.astype(F32) - along
    return row * row + lane * lane <= F32(RADIUS * RADIUS)


def image_kernel(group_ref, own_scalars, scalars_1, scalars_2, scalars_3, own_ref, near_ref, other_ref, target_ref, table_ref, out_ref,
                 fields_ref, row_field_ref, intensity_ref, cotangent_ref, spectra_ref, terms_ref, grad_ref, rounded_ref, frame_ref):
    scalars = [own_scalars, scalars_1, scalars_2, scalars_3]

    def beside(start, count):
        return jnp.concatenate([table_ref[start + 128 * i:start + 128 * (i + 1), :] for i in range(count)], 1)

    row_inverse = table_ref.at[pl.ds(pl.multiple_of(group_ref[0] * ROWS, ROWS), ROWS), :]
    row_inverse_t = table_ref.at[pl.ds(pl.multiple_of(TILE_ROWS + group_ref[0] * 128, 128), 128), :]
    even = group_ref[0] % 2 == 0
    frame_ref[MARGIN:MARGIN + TILE_ROWS] = own_ref[...]

    @pl.when(even)
    def _():
        frame_ref[:MARGIN] = near_ref[...]
        frame_ref[MARGIN + TILE_ROWS:] = other_ref[...]

    @pl.when(jnp.logical_not(even))
    def _():
        frame_ref[:MARGIN] = other_ref[...]
        frame_ref[MARGIN + TILE_ROWS:] = near_ref[...]

    product = dot(beside(FORWARD_AT, FRAME // 128), frame_ref[...])
    swapped = pltpu.roll(product[FREQS:], FREQS, 1)
    spectrum = (product[:FREQS] + halves_sign(FREQS, -1.0, 1.0) * swapped).astype(BF16).astype(F32)
    spectra_ref[:FREQS] = spectrum
    spectra_ref[FREQS:] = pltpu.roll(spectrum, FREQS, 1) * halves_sign(FREQS, -1.0, 1.0)
    intensity_ref[...] = jnp.zeros_like(intensity_ref)

    steps = SOURCES // STEP

    def image_rows(step):
        blocks = []
        for j in range(STEP):
            inside = pupil(scalars, step, j)
            inside = jnp.concatenate([inside, inside], 0)
            blocks.append(jnp.where(inside, spectra_ref[...], F32(0)).astype(BF16))
        row_field = dot(row_inverse[...], jnp.concatenate(blocks, 1)).astype(BF16)
        for j in range(STEP):
            start = pl.multiple_of((step * STEP + j) * ROWS, ROWS)
            row_field_ref[pl.ds(start, ROWS), :] = row_field[:, 128 * j:128 * (j + 1)]

    def weight(step, j):
        return scalars[j % GROUPS][0, step * (STEP // GROUPS) + j // GROUPS]

    image_rows(0)

    @pl.loop(0, steps)
    def _(step):
        start = pl.multiple_of(step * (STEP * ROWS), STEP * ROWS)
        row_field = row_field_ref[pl.ds(start, STEP * ROWS), :]
        for n in range(4):
            fields = dot(row_field, beside(INVERSE_AT + 256 * n, 2))
            fields_ref[pl.ds(start, STEP * ROWS), 256 * n:256 * (n + 1)] = fields
            power = fields[:, :128] * fields[:, :128] + fields[:, 128:] * fields[:, 128:]
            total = weight(step, 0) * power[:ROWS]
            for j in range(1, STEP):
                total = total + weight(step, j) * power[j * ROWS:(j + 1) * ROWS]
            intensity_ref[:, 128 * n:128 * (n + 1)] += total
        image_rows(jnp.minimum(step + 1, steps - 1))

    printed = jax.nn.sigmoid(F32(STEEPNESS) * (intensity_ref[...] - F32(THRESHOLD)))
    error_value = printed - target_ref[...].astype(F32)
    cotangent_ref[...] = F32(2.0 * STEEPNESS) * error_value * printed * (F32(1.0) - printed)
    error_rows = jnp.sum(error_value * error_value, 0, keepdims=True)
    error_lanes = (error_rows[:, :128] + error_rows[:, 128:256]) + (error_rows[:, 256:384] + error_rows[:, 384:])
    error_sum = jnp.sum(error_lanes, 1, keepdims=True)
    grad_ref[...] = jnp.zeros_like(grad_ref)

    rounded_ref[...] = jnp.zeros_like(rounded_ref)

    def add_block_grad(step):
        block_grad = dot(row_inverse_t[...], rounded_ref[...])
        total = jnp.zeros((2 * FREQS, 128), F32)
        for j in range(STEP):
            inside = pupil(scalars, step, j)
            inside = jnp.concatenate([inside, inside], 0)
            total = total + jnp.where(inside, block_grad[:, 128 * j:128 * (j + 1)], F32(0))
        grad_ref[...] += total

    @pl.loop(0, steps)
    def _(step):
        start = pl.multiple_of(step * (STEP * ROWS), STEP * ROWS)
        add_block_grad(jnp.maximum(step - 1, 0))
        row_grad = None
        for n in range(4):
            cot = cotangent_ref[:, 128 * n:128 * (n + 1)]
            parts = []
            for j in range(STEP):
                scaling = (F32(2.0) * weight(step, j)) * cot
                at = pl.multiple_of(start + j * ROWS, ROWS)
                fields = fields_ref[pl.ds(at, ROWS), 256 * n:256 * (n + 1)]
                parts.append((jnp.concatenate([scaling, scaling], 1) * fields).astype(BF16))
            part = dot(jnp.concatenate(parts, 0), table_ref[INVERSE_T_AT + 256 * n:INVERSE_T_AT + 256 * (n + 1), :])
            row_grad = part if row_grad is None else row_grad + part
        row_field = row_field_ref[pl.ds(start, STEP * ROWS), :].astype(F32)
        terms = row_grad * row_field
        rounded = row_grad.astype(BF16)
        for j in range(STEP):
            terms_ref[pl.ds(step * STEP + j, 1), :] = jnp.sum(terms[j * ROWS:(j + 1) * ROWS], 0, keepdims=True)
            rounded_ref[:, 128 * j:128 * (j + 1)] = rounded[j * ROWS:(j + 1) * ROWS]

    add_block_grad(steps - 1)
    grads = grad_ref[...]
    out_ref[:FREQS] = grads[:FREQS] + halves_sign(FREQS, 1.0, -1.0) * pltpu.roll(grads[FREQS:], FREQS, 1)
    term = jnp.sum(terms_ref[...], 1, keepdims=True)
    row = lax.broadcasted_iota(jnp.int32, (SOURCES, 128), 0)
    lane = lax.broadcasted_iota(jnp.int32, (SOURCES, 128), 1)
    wanted = (row % GROUPS) * PER_GROUP + row // GROUPS
    term_row = jnp.sum(jnp.where(wanted == lane, term, F32(0)), 0, keepdims=True)
    lane = lax.broadcasted_iota(jnp.int32, (1, 128), 1)
    own = group_ref[0]
    for bit, width in ((1, PER_GROUP), (2, 2 * PER_GROUP)):
        swapped = jnp.where((lane // width) % 2 == 0, pltpu.roll(term_row, 128 - width, 1),
                            pltpu.roll(term_row, width, 1))
        term_row = jnp.where(jnp.bitwise_and(own, bit) != 0, swapped, term_row)
    term_row = jnp.where(lane < SOURCES, term_row, F32(0))
    out_ref[FREQS:] = jnp.broadcast_to(jnp.where(lane == SOURCES, error_sum, term_row), (8, 128))


def image(group, scalars, own, near, other, target, table):
    fixed = lambda i, g: (0, 0)
    whole = lambda shape: pl.BlockSpec(shape, fixed)
    return pl.pallas_call(
        image_kernel,
        grid_spec=pltpu.PrefetchScalarGridSpec(
            num_scalar_prefetch=1,
            grid=(1,),
            in_specs=[
                *[pl.BlockSpec(memory_space=pltpu.SMEM)] * GROUPS,
                whole((TILE_ROWS, 128)), whole((MARGIN, 128)), whole((MARGIN, 128)),
                pl.BlockSpec((ROWS, COLS), lambda i, g: (g[0], 0)),
                whole(IMAGE_TABLE.shape),
            ],
            out_specs=whole((FREQS + 8, 128)),
            scratch_shapes=[
                pltpu.VMEM((SOURCES * ROWS, 2 * COLS), F32),
                pltpu.VMEM((SOURCES * ROWS, 128), BF16),
                pltpu.VMEM((ROWS, COLS), F32),
                pltpu.VMEM((ROWS, COLS), F32),
                pltpu.VMEM((128, 128), F32),
                pltpu.VMEM((SOURCES, 128), F32),
                pltpu.VMEM((128, 128), F32),
                pltpu.VMEM((ROWS, STEP * 128), BF16),
                pltpu.VMEM((FRAME, 128), BF16),
            ],
        ),
        out_shape=jax.ShapeDtypeStruct((FREQS + 8, 128), F32),
        compiler_params=pltpu.CompilerParams(vmem_limit_bytes=44 * MIB),
        name="image",
    )(group, *scalars, own, near, other, target, table)


def total_kernel(chip_ref, far_ref, grad_ref, sums_ref):
    grad_ref[...] = chip_ref[:FREQS] + far_ref[:FREQS]
    row = chip_ref[FREQS:FREQS + 1] + far_ref[FREQS:FREQS + 1]
    sums_ref[...] = jnp.broadcast_to(row[None], sums_ref.shape)


def total(chip, far, peers):
    return pl.pallas_call(
        total_kernel,
        out_shape=[jax.ShapeDtypeStruct((FREQS, 128), F32), jax.ShapeDtypeStruct((peers, 1, 128), F32)],
        compiler_params=pltpu.CompilerParams(vmem_limit_bytes=1 * MIB),
        name="total",
    )(chip, far)


def split_dot(table, x):
    high = x.astype(BF16)
    low = (x - high.astype(F32)).astype(BF16)
    return dot(jnp.concatenate([table, table], 1), jnp.concatenate([high, low], 0))


def dot_split(x, table):
    high = x.astype(BF16)
    low = (x - high.astype(F32)).astype(BF16)
    return dot(jnp.concatenate([high, low], 1), jnp.concatenate([table, table], 0))


def product_gradient(spectrum_grad):
    lower = pltpu.roll(spectrum_grad, FREQS, 1) * halves_sign(FREQS, 1.0, -1.0)
    return jnp.concatenate([spectrum_grad, lower], 0)


def owned_kernel(grad_ref, logits_ref, row_ref, column_ref, out_ref, edges_ref, slope_ref):
    column_grad = split_dot(row_ref[...], product_gradient(grad_ref[...]))
    opening = jax.nn.sigmoid(logits_ref[...])
    slope = opening * (F32(1.0) - opening)
    out = dot_split(column_grad, column_ref[...]) * slope
    out_ref[...] = out
    edges_ref[:MARGIN] = out[:MARGIN]
    edges_ref[MARGIN:] = out[TILE_ROWS - MARGIN:]
    slope_ref[:MARGIN] = slope[:MARGIN]
    slope_ref[MARGIN:] = slope[TILE_ROWS - MARGIN:]


def owned_gradient(spectrum_grad, mask_logits):
    return pl.pallas_call(
        owned_kernel,
        out_shape=[jax.ShapeDtypeStruct((n, COLS), F32) for n in (TILE_ROWS, 2 * MARGIN, 2 * MARGIN)],
        compiler_params=pltpu.CompilerParams(vmem_limit_bytes=10 * MIB),
        name="owned_gradient",
    )(spectrum_grad, mask_logits,
      jnp.asarray(np.ascontiguousarray(ROW_FORWARD.T[MARGIN:MARGIN + TILE_ROWS])),
      jnp.asarray(np.ascontiguousarray(COLUMN_FORWARD.T)))


def last_kernel(group_ref, near_ref, other_ref, edges_ref, slope_ref, row_ref, column_ref, sums_ref,
                packed_ref, grad_ref, out_ref, weight_grad_ref, loss_ref,
                rows_ref, semaphores, *, pixels):
    del grad_ref
    even = group_ref[0] % 2 == 0
    before = jnp.where(even, near_ref[...], other_ref[...])
    after = jnp.where(even, other_ref[...], near_ref[...])
    column_grad = jnp.concatenate([split_dot(row_ref[:MARGIN], product_gradient(before)),
                                   split_dot(row_ref[MARGIN:], product_gradient(after))], 0)
    rows_ref[...] = edges_ref[...] + dot_split(column_grad, column_ref[...]) * slope_ref[...]
    copies = [
        pltpu.make_async_copy(rows_ref.at[pl.ds(0, MARGIN), :], out_ref.at[pl.ds(0, MARGIN), :], semaphores.at[0]),
        pltpu.make_async_copy(rows_ref.at[pl.ds(MARGIN, MARGIN), :],
                              out_ref.at[pl.ds(TILE_ROWS - MARGIN, MARGIN), :], semaphores.at[1]),
    ]
    for copy in copies:
        copy.start()
    total = jnp.sum(sums_ref[...], 0)
    row = total
    for bit, width in ((1, PER_GROUP), (2, 2 * PER_GROUP)):
        row = jnp.where(jnp.bitwise_and(group_ref[0], bit) != 0, pltpu.roll(row, 128 - width, 1), row)
    weight_grad_ref[...] = row[:, :PER_GROUP] / (F32(2.0) * packed_ref[0:1]) / F32(pixels)
    loss_ref[...] = total[:, SOURCES:SOURCES + 1] / F32(pixels)
    for copy in copies:
        copy.wait()


def last_steps(group, near, other, edges, slope, grad, sums, packed, pixels):
    rows = np.concatenate([ROW_FORWARD.T[MARGIN + TILE_ROWS:], ROW_FORWARD.T[:MARGIN]], 0)
    block = pl.BlockSpec()
    hbm = pl.BlockSpec(memory_space=pltpu.HBM)
    return pl.pallas_call(
        functools.partial(last_kernel, pixels=pixels),
        in_specs=[pl.BlockSpec(memory_space=pltpu.SMEM)] + [block] * 8 + [hbm],
        out_specs=[hbm, block, block],
        out_shape=[jax.ShapeDtypeStruct((TILE_ROWS, COLS), F32), jax.ShapeDtypeStruct((1, PER_GROUP), F32),
                   jax.ShapeDtypeStruct((1, 1), F32)],
        scratch_shapes=[pltpu.VMEM((2 * MARGIN, COLS), F32), pltpu.SemaphoreType.DMA((2,))],
        input_output_aliases={9: 0},
        compiler_params=pltpu.CompilerParams(vmem_limit_bytes=4 * MIB),
        name="last_steps",
    )(group, near, other, edges, slope, jnp.asarray(np.ascontiguousarray(rows)),
      jnp.asarray(np.ascontiguousarray(COLUMN_FORWARD.T)), sums, packed, grad)


def from_tile_beside(x):
    peers = lax.axis_size("tile")
    plane = peers // 4
    pairs = []
    for group in range(GROUPS):
        for i in range(peers):
            j = i + 1 - 2 * (group % 2)
            if 0 <= j < peers:
                other = group if i // plane == j // plane else group ^ 2
                pairs.append((group * peers + i, other * peers + j))
    return lax.ppermute(x, ("src", "tile"), pairs)


def from_group(x, d):
    return lax.ppermute(x, "src", [(i, i ^ d) for i in range(GROUPS)])


def from_core(x):
    return from_group(x, 1)


def from_chip(x):
    return from_group(x, 2)


def from_group_nearby(x):
    peers = lax.axis_size("tile")
    pairs = [(s * peers + i, (s ^ 2) * peers + (i ^ 8)) for s in range(GROUPS) for i in range(peers)]
    return lax.ppermute(x, ("src", "tile"), pairs)


def on_device(mask_logits, target, weights, shifts):
    peers = lax.axis_size("tile")
    group = lax.axis_index("src").astype(jnp.int32).reshape(1)
    edge, packed = edge_spectrum(group, mask_logits, weights, shifts)
    packed_far = from_group_nearby(packed)
    near = from_tile_beside(edge)
    packed_core = from_core(packed)
    own, table = column_spectrum(mask_logits)
    near, packed_far, own = lax.optimization_barrier((near, packed_far, own))
    scalars = [packed, packed_core, packed_far, from_core(packed_far)]
    partial = image(group, scalars, own, near, from_core(near), target, table)
    chip = partial + from_core(partial)
    spectrum_grad, sums = total(chip, from_chip(chip), peers)
    sums = lax.all_to_all(sums, "tile", 0, 0, tiled=True)
    near_grad = from_tile_beside(spectrum_grad)
    grad, edges, slope = owned_gradient(spectrum_grad, mask_logits)
    near_grad, edges = lax.optimization_barrier((near_grad, edges))
    mask_grad, weight_grad, loss = last_steps(
        group, near_grad, from_core(near_grad), edges, slope, grad, sums, packed, TILE_ROWS * COLS * peers)
    return mask_grad, weight_grad.reshape(PER_GROUP), loss.reshape(())


def solution(mesh):
    placed = (P("tile", None), P("tile", None), P("src"), P("src", None))
    return jax.shard_map(
        on_device,
        mesh=mesh,
        in_specs=placed,
        out_specs=(P("tile", None), P("src"), P()),
        check_vma=False,
    )
```

```python
import functools

import numpy as np
import jax
import jax.numpy as jnp
from jax import lax
from jax.experimental import pallas as pl
from jax.experimental.pallas import tpu as pltpu
from jax.sharding import PartitionSpec as P


FREQS = 64
RADIUS = 20
MARGIN = 64
COLS = 512
TILE_ROWS = 512
FRAME = 640
SOURCES = 64
GROUPS = 4
PER_GROUP = SOURCES // GROUPS
ROWS = TILE_ROWS // GROUPS
MIB = 1024 * 1024
STEEPNESS = 12.0
THRESHOLD = 0.2
STEP = 32
F32 = jnp.float32
BF16 = jnp.bfloat16


def angles(length_used, offset, period):
    position = np.arange(length_used, dtype=np.int32)[:, None] + offset
    frequency = np.arange(FREQS, dtype=np.int32)[None, :] - FREQS // 2
    cycles = np.mod(position * frequency, period).astype(np.float32)
    angle_value = (cycles * np.float32(2.0 * 3.141592653589793 / period)).astype(np.float64)
    return np.cos(angle_value).astype(np.float32), np.sin(angle_value).astype(np.float32)


def make_tables():
    column_cosine, column_sine = angles(COLS, 0, COLS)
    column_forward = np.concatenate([column_cosine, -column_sine], 1)
    frame_cosine, frame_sine = angles(FRAME, 0, FRAME)
    row_forward = np.concatenate([frame_cosine.T, -frame_sine.T], 0)
    owned_cosine, owned_sine = angles(TILE_ROWS, MARGIN, FRAME)
    row_inverse = np.concatenate([owned_cosine, owned_sine], 1) / np.float32(FRAME)
    cosine_scaled = column_cosine.T / np.float32(COLS)
    sine_scaled = column_sine.T / np.float32(COLS)
    upper_block = np.concatenate([cosine_scaled, sine_scaled], 1)
    lower_block = np.concatenate([-sine_scaled, cosine_scaled], 1)
    column_inverse = np.concatenate([upper_block, lower_block], 0)
    chunked = column_inverse.reshape(2 * FREQS, 2, COLS // 128, 128).transpose(0, 2, 1, 3)
    chunked = chunked.reshape(2 * FREQS, 2 * COLS)
    rounded = lambda a: np.ascontiguousarray(a).astype(BF16)
    return [rounded(a) for a in (column_forward, row_forward, row_inverse, chunked)]


COLUMN_FORWARD, ROW_FORWARD, ROW_INVERSE, COLUMN_INVERSE = make_tables()


def stacked(table):
    return np.concatenate([table[:, c:c + 128] for c in range(0, table.shape[1], 128)], 0)


PARTS = [ROW_INVERSE, stacked(ROW_INVERSE.T), COLUMN_INVERSE.T, stacked(COLUMN_INVERSE), stacked(ROW_FORWARD)]
IMAGE_TABLE = np.ascontiguousarray(np.concatenate(PARTS, 0))
INVERSE_T_AT = 2 * TILE_ROWS
INVERSE_AT = INVERSE_T_AT + 2 * COLS
FORWARD_AT = INVERSE_AT + 8 * 128


def dot(a, b):
    return jnp.dot(a, b, preferred_element_type=F32)


def halves_sign(rows, left, right):
    lane = lax.broadcasted_iota(jnp.int32, (rows, 128), 1)
    return jnp.where(lane < FREQS, F32(left), F32(right))


def edge_kernel(group_ref, logits_ref, table_ref, weights_ref, shifts_ref, edge_out, packed_out,
                rows, table, weights, shifts, semaphores):
    start = jnp.where(group_ref[0] % 2 == 0, TILE_ROWS - MARGIN, 0)
    rows_from = logits_ref.at[pl.ds(pl.multiple_of(start, MARGIN), MARGIN), :]
    pairs = ((rows_from, rows), (table_ref, table), (weights_ref, weights), (shifts_ref, shifts))
    copies = [pltpu.make_async_copy(a, b, semaphores.at[i]) for i, (a, b) in enumerate(pairs)]
    for copy in copies:
        copy.start()
    for copy in copies:
        copy.wait()
    edge_out[...] = dot(jax.nn.sigmoid(rows[...]).astype(BF16), table[...]).astype(BF16)
    packed_out[0:1] = weights[...]
    packed_out[1:3] = shifts[...].astype(F32)


def edge_spectrum(group, mask_logits, weights, shifts):
    return pl.pallas_call(
        edge_kernel,
        in_specs=[pl.BlockSpec(memory_space=pltpu.SMEM)] + [pl.BlockSpec(memory_space=pltpu.HBM)] * 4,
        out_shape=[jax.ShapeDtypeStruct((MARGIN, 128), BF16), jax.ShapeDtypeStruct((3, PER_GROUP), F32)],
        scratch_shapes=[
            pltpu.VMEM((MARGIN, COLS), F32), pltpu.VMEM((COLS, 128), BF16),
            pltpu.VMEM((1, PER_GROUP), F32), pltpu.VMEM((2, PER_GROUP), jnp.int32),
            pltpu.SemaphoreType.DMA((4,)),
        ],
        compiler_params=pltpu.CompilerParams(vmem_limit_bytes=60 * MIB),
        name="edge_spectrum",
    )(group, mask_logits, jnp.asarray(COLUMN_FORWARD), weights.reshape(1, PER_GROUP), shifts.T)


def column_kernel(logits_ref, table_ref, image_table_ref, out_ref, image_table_out, semaphore):
    copy = pltpu.make_async_copy(image_table_ref, image_table_out, semaphore)
    copy.start()
    out_ref[...] = dot(jax.nn.sigmoid(logits_ref[...]).astype(BF16), table_ref[...]).astype(BF16)
    copy.wait()


def column_spectrum(mask_logits):
    return pl.pallas_call(
        column_kernel,
        in_specs=[pl.BlockSpec(), pl.BlockSpec(), pl.BlockSpec(memory_space=pltpu.HBM)],
        out_shape=[jax.ShapeDtypeStruct((TILE_ROWS, 128), BF16), jax.ShapeDtypeStruct(IMAGE_TABLE.shape, BF16)],
        scratch_shapes=[pltpu.SemaphoreType.DMA],
        compiler_params=pltpu.CompilerParams(vmem_limit_bytes=8 * MIB),
        name="column_spectrum",
    )(mask_logits, jnp.asarray(COLUMN_FORWARD), jnp.asarray(IMAGE_TABLE))


def pupil(scalars, step, j):
    ref, i = scalars[j % GROUPS], step * (STEP // GROUPS) + j // GROUPS
    across, along = ref[1, i], ref[2, i]
    row = lax.broadcasted_iota(jnp.int32, (FREQS, 128), 0) - FREQS // 2
    lane = jnp.bitwise_and(lax.broadcasted_iota(jnp.int32, (FREQS, 128), 1), FREQS - 1) - FREQS // 2
    row, lane = row.astype(F32) - across, lane.astype(F32) - along
    return row * row + lane * lane <= F32(RADIUS * RADIUS)


def image_kernel(group_ref, own_scalars, scalars_1, scalars_2, scalars_3, own_ref, near_ref, other_ref, target_ref, table_ref, out_ref, sums_ref,
                 fields_ref, row_field_ref, intensity_ref, cotangent_ref, spectra_ref, terms_ref, grad_ref, rounded_ref, frame_ref):
    scalars = [own_scalars, scalars_1, scalars_2, scalars_3]

    def beside(start, count):
        return jnp.concatenate([table_ref[start + 128 * i:start + 128 * (i + 1), :] for i in range(count)], 1)

    row_inverse = table_ref.at[pl.ds(pl.multiple_of(group_ref[0] * ROWS, ROWS), ROWS), :]
    row_inverse_t = table_ref.at[pl.ds(pl.multiple_of(TILE_ROWS + group_ref[0] * 128, 128), 128), :]
    even = group_ref[0] % 2 == 0
    frame_ref[MARGIN:MARGIN + TILE_ROWS] = own_ref[...]

    @pl.when(even)
    def _():
        frame_ref[:MARGIN] = near_ref[...]
        frame_ref[MARGIN + TILE_ROWS:] = other_ref[...]

    @pl.when(jnp.logical_not(even))
    def _():
        frame_ref[:MARGIN] = other_ref[...]
        frame_ref[MARGIN + TILE_ROWS:] = near_ref[...]

    product = dot(beside(FORWARD_AT, FRAME // 128), frame_ref[...])
    swapped = pltpu.roll(product[FREQS:], FREQS, 1)
    spectrum = (product[:FREQS] + halves_sign(FREQS, -1.0, 1.0) * swapped).astype(BF16).astype(F32)
    spectra_ref[:FREQS] = spectrum
    spectra_ref[FREQS:] = pltpu.roll(spectrum, FREQS, 1) * halves_sign(FREQS, -1.0, 1.0)
    intensity_ref[...] = jnp.zeros_like(intensity_ref)

    steps = SOURCES // STEP

    def image_rows(step):
        blocks = []
        for j in range(STEP):
            inside = pupil(scalars, step, j)
            inside = jnp.concatenate([inside, inside], 0)
            blocks.append(jnp.where(inside, spectra_ref[...], F32(0)).astype(BF16))
        row_field = dot(row_inverse[...], jnp.concatenate(blocks, 1)).astype(BF16)
        for j in range(STEP):
            start = pl.multiple_of((step * STEP + j) * ROWS, ROWS)
            row_field_ref[pl.ds(start, ROWS), :] = row_field[:, 128 * j:128 * (j + 1)]

    def weight(step, j):
        return scalars[j % GROUPS][0, step * (STEP // GROUPS) + j // GROUPS]

    image_rows(0)

    @pl.loop(0, steps)
    def _(step):
        start = pl.multiple_of(step * (STEP * ROWS), STEP * ROWS)
        row_field = row_field_ref[pl.ds(start, STEP * ROWS), :]
        for n in range(4):
            fields = dot(row_field, beside(INVERSE_AT + 256 * n, 2))
            fields_ref[pl.ds(start, STEP * ROWS), 256 * n:256 * (n + 1)] = fields
            power = fields[:, :128] * fields[:, :128] + fields[:, 128:] * fields[:, 128:]
            total = weight(step, 0) * power[:ROWS]
            for j in range(1, STEP):
                total = total + weight(step, j) * power[j * ROWS:(j + 1) * ROWS]
            intensity_ref[:, 128 * n:128 * (n + 1)] += total
        image_rows(jnp.minimum(step + 1, steps - 1))

    printed = jax.nn.sigmoid(F32(STEEPNESS) * (intensity_ref[...] - F32(THRESHOLD)))
    error_value = printed - target_ref[...].astype(F32)
    cotangent_ref[...] = F32(2.0 * STEEPNESS) * error_value * printed * (F32(1.0) - printed)
    error_rows = jnp.sum(error_value * error_value, 0, keepdims=True)
    error_lanes = (error_rows[:, :128] + error_rows[:, 128:256]) + (error_rows[:, 256:384] + error_rows[:, 384:])
    error_sum = jnp.sum(error_lanes, 1, keepdims=True)
    grad_ref[...] = jnp.zeros_like(grad_ref)

    rounded_ref[...] = jnp.zeros_like(rounded_ref)

    def add_block_grad(step):
        block_grad = dot(row_inverse_t[...], rounded_ref[...])
        total = jnp.zeros((2 * FREQS, 128), F32)
        for j in range(STEP):
            inside = pupil(scalars, step, j)
            inside = jnp.concatenate([inside, inside], 0)
            total = total + jnp.where(inside, block_grad[:, 128 * j:128 * (j + 1)], F32(0))
        grad_ref[...] += total

    @pl.loop(0, steps)
    def _(step):
        start = pl.multiple_of(step * (STEP * ROWS), STEP * ROWS)
        add_block_grad(jnp.maximum(step - 1, 0))
        row_grad = None
        for n in range(4):
            cot = cotangent_ref[:, 128 * n:128 * (n + 1)]
            parts = []
            for j in range(STEP):
                scaling = (F32(2.0) * weight(step, j)) * cot
                at = pl.multiple_of(start + j * ROWS, ROWS)
                fields = fields_ref[pl.ds(at, ROWS), 256 * n:256 * (n + 1)]
                parts.append((jnp.concatenate([scaling, scaling], 1) * fields).astype(BF16))
            part = dot(jnp.concatenate(parts, 0), table_ref[INVERSE_T_AT + 256 * n:INVERSE_T_AT + 256 * (n + 1), :])
            row_grad = part if row_grad is None else row_grad + part
        row_field = row_field_ref[pl.ds(start, STEP * ROWS), :].astype(F32)
        terms = row_grad * row_field
        rounded = row_grad.astype(BF16)
        for j in range(STEP):
            terms_ref[pl.ds(step * STEP + j, 1), :] = jnp.sum(terms[j * ROWS:(j + 1) * ROWS], 0, keepdims=True)
            rounded_ref[:, 128 * j:128 * (j + 1)] = rounded[j * ROWS:(j + 1) * ROWS]

    add_block_grad(steps - 1)
    grads = grad_ref[...]
    out_ref[...] = grads[:FREQS] + halves_sign(FREQS, 1.0, -1.0) * pltpu.roll(grads[FREQS:], FREQS, 1)
    term = jnp.sum(terms_ref[...], 1, keepdims=True)
    row = lax.broadcasted_iota(jnp.int32, (SOURCES, 128), 0)
    lane = lax.broadcasted_iota(jnp.int32, (SOURCES, 128), 1)
    wanted = (row % GROUPS) * PER_GROUP + row // GROUPS
    term_row = jnp.sum(jnp.where(wanted == lane, term, F32(0)), 0, keepdims=True)
    lane = lax.broadcasted_iota(jnp.int32, (1, 128), 1)
    own = group_ref[0]
    for bit, width in ((1, PER_GROUP), (2, 2 * PER_GROUP)):
        swapped = jnp.where((lane // width) % 2 == 0, pltpu.roll(term_row, 128 - width, 1),
                            pltpu.roll(term_row, width, 1))
        term_row = jnp.where(jnp.bitwise_and(own, bit) != 0, swapped, term_row)
    term_row = jnp.where(lane < SOURCES, term_row, F32(0))
    sums_ref[...] = jnp.where(lane == SOURCES, error_sum, term_row)


def image(group, scalars, own, near, other, target, table):
    fixed = lambda i, g: (0, 0)
    whole = lambda shape: pl.BlockSpec(shape, fixed)
    return pl.pallas_call(
        image_kernel,
        grid_spec=pltpu.PrefetchScalarGridSpec(
            num_scalar_prefetch=1,
            grid=(1,),
            in_specs=[
                *[pl.BlockSpec(memory_space=pltpu.SMEM)] * GROUPS,
                whole((TILE_ROWS, 128)), whole((MARGIN, 128)), whole((MARGIN, 128)),
                pl.BlockSpec((ROWS, COLS), lambda i, g: (g[0], 0)),
                whole(IMAGE_TABLE.shape),
            ],
            out_specs=[whole((FREQS, 128)), whole((1, 128))],
            scratch_shapes=[
                pltpu.VMEM((SOURCES * ROWS, 2 * COLS), F32),
                pltpu.VMEM((SOURCES * ROWS, 128), BF16),
                pltpu.VMEM((ROWS, COLS), F32),
                pltpu.VMEM((ROWS, COLS), F32),
                pltpu.VMEM((128, 128), F32),
                pltpu.VMEM((SOURCES, 128), F32),
                pltpu.VMEM((128, 128), F32),
                pltpu.VMEM((ROWS, STEP * 128), BF16),
                pltpu.VMEM((FRAME, 128), BF16),
            ],
        ),
        out_shape=[jax.ShapeDtypeStruct((FREQS, 128), F32), jax.ShapeDtypeStruct((1, 128), F32)],
        compiler_params=pltpu.CompilerParams(vmem_limit_bytes=44 * MIB),
        name="image",
    )(group, *scalars, own, near, other, target, table)


def spread_kernel(chip_ref, near_ref, out_ref):
    out_ref[...] = jnp.broadcast_to((chip_ref[...] + near_ref[...])[None], out_ref.shape)


def spread(chip, near, peers):
    return pl.pallas_call(
        spread_kernel,
        out_shape=jax.ShapeDtypeStruct((peers, 1, 128), F32),
        compiler_params=pltpu.CompilerParams(vmem_limit_bytes=1 * MIB),
        name="spread",
    )(chip, near)


def split_dot(table, x):
    high = x.astype(BF16)
    low = (x - high.astype(F32)).astype(BF16)
    return dot(jnp.concatenate([table, table], 1), jnp.concatenate([high, low], 0))


def dot_split(x, table):
    high = x.astype(BF16)
    low = (x - high.astype(F32)).astype(BF16)
    return dot(jnp.concatenate([high, low], 1), jnp.concatenate([table, table], 0))


def product_gradient(spectrum_grad):
    lower = pltpu.roll(spectrum_grad, FREQS, 1) * halves_sign(FREQS, 1.0, -1.0)
    return jnp.concatenate([spectrum_grad, lower], 0)


def owned_kernel(grad_ref, logits_ref, row_ref, column_ref, out_ref, edges_ref, slope_ref):
    column_grad = split_dot(row_ref[...], product_gradient(grad_ref[...]))
    opening = jax.nn.sigmoid(logits_ref[...])
    slope = opening * (F32(1.0) - opening)
    out = dot_split(column_grad, column_ref[...]) * slope
    out_ref[...] = out
    edges_ref[:MARGIN] = out[:MARGIN]
    edges_ref[MARGIN:] = out[TILE_ROWS - MARGIN:]
    slope_ref[:MARGIN] = slope[:MARGIN]
    slope_ref[MARGIN:] = slope[TILE_ROWS - MARGIN:]


def owned_gradient(spectrum_grad, mask_logits):
    return pl.pallas_call(
        owned_kernel,
        out_shape=[jax.ShapeDtypeStruct((n, COLS), F32) for n in (TILE_ROWS, 2 * MARGIN, 2 * MARGIN)],
        compiler_params=pltpu.CompilerParams(vmem_limit_bytes=10 * MIB),
        name="owned_gradient",
    )(spectrum_grad, mask_logits,
      jnp.asarray(np.ascontiguousarray(ROW_FORWARD.T[MARGIN:MARGIN + TILE_ROWS])),
      jnp.asarray(np.ascontiguousarray(COLUMN_FORWARD.T)))


def last_kernel(group_ref, near_ref, other_ref, edges_ref, slope_ref, row_ref, column_ref, sums_ref,
                packed_ref, grad_ref, out_ref, weight_grad_ref, loss_ref,
                rows_ref, semaphores, *, pixels):
    del grad_ref
    even = group_ref[0] % 2 == 0
    before = jnp.where(even, near_ref[...], other_ref[...])
    after = jnp.where(even, other_ref[...], near_ref[...])
    column_grad = jnp.concatenate([split_dot(row_ref[:MARGIN], product_gradient(before)),
                                   split_dot(row_ref[MARGIN:], product_gradient(after))], 0)
    rows_ref[...] = edges_ref[...] + dot_split(column_grad, column_ref[...]) * slope_ref[...]
    copies = [
        pltpu.make_async_copy(rows_ref.at[pl.ds(0, MARGIN), :], out_ref.at[pl.ds(0, MARGIN), :], semaphores.at[0]),
        pltpu.make_async_copy(rows_ref.at[pl.ds(MARGIN, MARGIN), :],
                              out_ref.at[pl.ds(TILE_ROWS - MARGIN, MARGIN), :], semaphores.at[1]),
    ]
    for copy in copies:
        copy.start()
    pairs = sums_ref[...].reshape(4, 2, 8, 1, 128)
    total = jnp.sum((pairs[:, 0] + pairs[:, 1]).reshape(32, 1, 128), 0)
    row = total
    for bit, width in ((1, PER_GROUP), (2, 2 * PER_GROUP)):
        row = jnp.where(jnp.bitwise_and(group_ref[0], bit) != 0, pltpu.roll(row, 128 - width, 1), row)
    weight_grad_ref[...] = row[:, :PER_GROUP] / (F32(2.0) * packed_ref[0:1]) / F32(pixels)
    loss_ref[...] = total[:, SOURCES:SOURCES + 1] / F32(pixels)
    for copy in copies:
        copy.wait()


def last_steps(group, near, other, edges, slope, grad, sums, packed, pixels):
    rows = np.concatenate([ROW_FORWARD.T[MARGIN + TILE_ROWS:], ROW_FORWARD.T[:MARGIN]], 0)
    block = pl.BlockSpec()
    hbm = pl.BlockSpec(memory_space=pltpu.HBM)
    return pl.pallas_call(
        functools.partial(last_kernel, pixels=pixels),
        in_specs=[pl.BlockSpec(memory_space=pltpu.SMEM)] + [block] * 8 + [hbm],
        out_specs=[hbm, block, block],
        out_shape=[jax.ShapeDtypeStruct((TILE_ROWS, COLS), F32), jax.ShapeDtypeStruct((1, PER_GROUP), F32),
                   jax.ShapeDtypeStruct((1, 1), F32)],
        scratch_shapes=[pltpu.VMEM((2 * MARGIN, COLS), F32), pltpu.SemaphoreType.DMA((2,))],
        input_output_aliases={9: 0},
        compiler_params=pltpu.CompilerParams(vmem_limit_bytes=4 * MIB),
        name="last_steps",
    )(group, near, other, edges, slope, jnp.asarray(np.ascontiguousarray(rows)),
      jnp.asarray(np.ascontiguousarray(COLUMN_FORWARD.T)), sums, packed, grad)


def from_tile_beside(x):
    peers = lax.axis_size("tile")
    plane = peers // 4
    pairs = []
    for group in range(GROUPS):
        for i in range(peers):
            j = i + 1 - 2 * (group % 2)
            if 0 <= j < peers:
                other = group if i // plane == j // plane else group ^ 2
                pairs.append((group * peers + i, other * peers + j))
    return lax.ppermute(x, ("src", "tile"), pairs)


def from_group(x, d):
    return lax.ppermute(x, "src", [(i, i ^ d) for i in range(GROUPS)])


def from_core(x):
    return from_group(x, 1)


def from_chip(x):
    return from_group(x, 2)


def from_group_nearby(x):
    peers = lax.axis_size("tile")
    pairs = [(s * peers + i, (s ^ 2) * peers + (i ^ 8)) for s in range(GROUPS) for i in range(peers)]
    return lax.ppermute(x, ("src", "tile"), pairs)


def on_device(mask_logits, target, weights, shifts):
    peers = lax.axis_size("tile")
    group = lax.axis_index("src").astype(jnp.int32).reshape(1)
    edge, packed = edge_spectrum(group, mask_logits, weights, shifts)
    packed_far = from_group_nearby(packed)
    near = from_tile_beside(edge)
    packed_core = from_core(packed)
    own, table = column_spectrum(mask_logits)
    near, packed_far, packed_core, own = lax.optimization_barrier((near, packed_far, packed_core, own))
    scalars = [packed, packed_core, packed_far, from_core(packed_far)]
    partial, sums = image(group, scalars, own, near, from_core(near), target, table)
    sums = sums + from_core(sums)
    chip = partial + from_core(partial)
    sums_near = from_group_nearby(sums)
    far = from_chip(chip)
    sums = spread(sums, sums_near, peers)
    sums = lax.all_to_all(sums, "tile", 0, 0, tiled=True)
    spectrum_grad = chip + far
    near_grad = from_tile_beside(spectrum_grad)
    grad, edges, slope = owned_gradient(spectrum_grad, mask_logits)
    near_grad, edges = lax.optimization_barrier((near_grad, edges))
    mask_grad, weight_grad, loss = last_steps(
        group, near_grad, from_core(near_grad), edges, slope, grad, sums, packed, TILE_ROWS * COLS * peers)
    return mask_grad, weight_grad.reshape(PER_GROUP), loss.reshape(())


def solution(mesh):
    placed = (P("tile", None), P("tile", None), P("src"), P("src", None))
    return jax.shard_map(
        on_device,
        mesh=mesh,
        in_specs=placed,
        out_specs=(P("tile", None), P("src"), P()),
        check_vma=False,
    )
```
